32 devices in a mesh: areal: 8 (over z, y), layer: 4 (over x, core).
Axes of the slice: x: 2, y: 2, z: 4, core: 2. Of those that a mesh axis runs over, the one named last changes fastest.
Arguments:
- right_side: float32 [3, 16, 64, 256], P(None, 'layer', 'areal'), may hold values from -6 to 6
- diag_blocks: bfloat16 [3, 3, 16, 64, 256], P(None, None, 'layer', 'areal'), may hold values from -3 to 9
- couplings: bfloat16 [6, 3, 3, 16, 64, 256], P(None, None, None, 'layer', 'areal'), may hold values from -1 to 1
- pivot_inverse: bfloat16 [3, 3, 16, 64, 256], P(None, None, 'layer', 'areal'), may hold values from -0.2 to 0.2
- lower_blocks: bfloat16 [3, 3, 16, 64, 256], P(None, None, 'layer', 'areal'), may hold values from -0.1 to 1
- upper_blocks: bfloat16 [3, 3, 16, 64, 256], P(None, None, 'layer', 'areal'), may hold values from -0.1 to 1
- active_cells: int32 [16, 64, 256], P('layer', 'areal'), may hold values 0 or 1
- link_from: int32 [4, 32768], P('layer', 'areal'), may hold values from 0 to 8191
- link_owner: int32 [4, 32768, 1], P('layer', 'areal'), may hold values from 0 to 7; in each aligned block of 4096 rows (0 to 4095, 4096 to 8191, ..., all dimensions but the last counted through in order) at most 1024 rows name the same one
- link_target: int32 [4, 32768], P('layer', 'areal'), may hold values from 0 to 8191
- link_blocks: bfloat16 [3, 3, 4, 32768], P(None, None, 'layer', 'areal'), may hold values from -1.5 to 1.5
Outputs:
- update: float32 [3, 16, 64, 256], P(None, 'layer', 'areal')
- hessenberg: float32 [5, 4], replicated
The draws below stay inside these ranges and needn't reach their ends.
Inputs may be any that keep to these rules, and one draw needn't show every extreme that they name: `link_owner`: among the 4096 connections listed on one device, at most 1024 name the same owner, and in every draw that number is reached.
All inputs are finite; a program needn't handle non-finite values. No bound on the sum of `active_cells` on one device may be relied on, other than what follows from the above.
Results may differ from the reference program's by a relative error of at most 0.0003.
Values sent between devices are 32-bit elements; how exact they have to be, the bound alone decides.
No kernel may reach another device: no remote copies, remote signals or barrier semaphores. Data moves between devices by JAX's collectives and lax.ppermute only.
A program may use at most 64 MiB of HBM per device.

```python
import math
import jax
import jax.numpy as jnp
import numpy as np
from jax import lax

LZ = 4
SXD = 8
SY = 256
NNC_DEV = 4096
ITERS = 4
NZ = 16
NXA = 64
SECTIONS = 4
NNC_ALL = 32768
CAP = 1024
N_AREAL = 8


def eye_mask():
    return jnp.eye(3, dtype=jnp.float32)[:, :, None, None, None]


def draw_diag_blocks(key, part):
    dimensions = (3, 3, NZ, NXA, SY)
    lead_key, rest_key = jax.random.split(key)
    leading = jax.random.uniform(lead_key, dimensions, jnp.float32, 6.0, 9.0)
    others = jnp.clip(0.6 * jax.random.normal(rest_key, dimensions, jnp.float32), -3.0, 3.0)
    return (eye_mask() * leading + (1.0 - eye_mask()) * others).astype(jnp.bfloat16)


def draw_pivot_inverse(key, part):
    dimensions = (3, 3, NZ, NXA, SY)
    lead_key, rest_key = jax.random.split(key)
    leading = jax.random.uniform(lead_key, dimensions, jnp.float32, 0.11, 0.17)
    others = jnp.clip(0.03 * jax.random.normal(rest_key, dimensions, jnp.float32), -0.2, 0.2)
    return (eye_mask() * leading + (1.0 - eye_mask()) * others).astype(jnp.bfloat16)


def draw_lower_blocks(key, part):
    dimensions = (3, 3, NZ, NXA, SY)
    rate_key, side_key = jax.random.split(key)
    low_rate = math.log(1.0 / (3.0 * NZ))
    high_rate = math.log(0.2)
    rates = jnp.exp(jax.random.uniform(rate_key, dimensions, jnp.float32, low_rate, high_rate))
    keeping = jnp.exp(-rates)
    sideways = jax.random.uniform(side_key, dimensions, jnp.float32, -0.5, 0.5) * (1.0 - keeping)
    return (eye_mask() * keeping + (1.0 - eye_mask()) * sideways).astype(jnp.bfloat16)


def draw_upper_blocks(key, part):
    dimensions = (3, 3, NZ, NXA, SY)
    rate_key, side_key = jax.random.split(jax.random.fold_in(key, 7))
    low_rate = math.log(1.0 / (3.0 * NZ))
    high_rate = math.log(0.2)
    rates = jnp.exp(jax.random.uniform(rate_key, dimensions, jnp.float32, low_rate, high_rate))
    keeping = jnp.exp(-rates)
    sideways = jax.random.uniform(side_key, dimensions, jnp.float32, -0.5, 0.5) * (1.0 - keeping)
    return (eye_mask() * keeping + (1.0 - eye_mask()) * sideways).astype(jnp.bfloat16)


def with_ends(array, rng, least, high):
    spot = [jax.random.randint(jax.random.fold_in(rng, axis), (), 0, length) for axis, length in enumerate(array.shape)]
    widest = array.shape.index(max(array.shape))
    next_to = spot[:widest] + [(spot[widest] + 1) % array.shape[widest]] + spot[widest + 1:]
    return array.at[tuple(spot)].set(least).at[tuple(next_to)].set(high)


def shard_levels(key, extent, pieces, least, top_value):
    def one(dim, parts):
        steps = jax.random.uniform(jax.random.fold_in(jax.random.fold_in(key, 6), dim), (parts,), jnp.float32, least / len(pieces), top_value / len(pieces))
        return jnp.repeat(jnp.exp(steps), extent[dim] // parts).reshape((-1,) + (1,) * (len(extent) - dim - 1))

    loudness = one(*pieces[0])
    for cut in pieces[1:]:
        loudness = loudness * one(*cut)
    return loudness


def routed_block(rng, own, number, rows, number_of, top, bound, skew):
    sequence = jax.random.permutation(rng, number_of)
    heavy_load, usual = portions_of(number_of, rows * top, bound, skew, True), portions_of(number_of, rows * top, bound, skew, False)
    places = jnp.arange(number_of)

    def named(tallies, turn):
        used = int((tallies > 0).sum())
        fixed = max(1, used // 4)
        passed = fixed + (places - fixed + turn * (used - fixed)) % max(1, number_of - fixed)
        return jnp.zeros((number_of,), jnp.int32).at[sequence[jnp.where(places < fixed, places, passed)]].set(jnp.asarray(tallies, jnp.int32))

    tallies = jnp.where(number % 4 == 0, named(heavy_load, number // 4), named(usual, number - number // 4 - 1))
    mixed = jax.random.permutation(jax.random.fold_in(own, 3), number_of)
    source_of, receiver = mixed[0:number_of // 2 * 2:2], mixed[1:number_of // 2 * 2:2]
    slack = jnp.minimum(tallies[source_of] - 1, bound - tallies[receiver]) // 2
    slack = jnp.where((source_of == sequence[0]) | (receiver == sequence[0]) | (tallies[receiver] == 0), 0, jnp.maximum(slack, 0))
    passed = jax.random.randint(jax.random.fold_in(own, 4), (number_of // 2,), 0, 1 << 20) % (slack + 1)
    tallies = tallies.at[source_of].add(-passed).at[receiver].add(passed)
    labels = jnp.searchsorted(jnp.cumsum(tallies), jnp.arange(rows * top), side="right").astype(jnp.int32)
    listing = labels.reshape(top, rows).T
    listing = listing[jax.random.permutation(jax.random.fold_in(own, 1), rows)]
    turn = jax.random.randint(jax.random.fold_in(own, 2), (rows, 1), 0, top)
    return jnp.take_along_axis(listing, (jnp.arange(top)[None, :] + turn) % top, axis=1)


def portions_of(number_of, total, limit, skew, full):
    portions = [(1 << 20) // math.isqrt(grade ** skew) + 1 for grade in range(1, number_of + 1)]
    largest = limit if full else min(limit, max(-(-total // number_of), total * portions[0] // sum(portions)))
    least = 1 if total - largest >= number_of - 1 else 0
    holding, spare = [largest] + [least] * (number_of - 1), total - largest - least * (number_of - 1)
    while spare > 0:
        candidates = [i for i in range(1, number_of) if holding[i] < largest] or [i for i in range(1, number_of) if holding[i] < limit]
        mass, left = sum([portions[i] for i in candidates]), spare
        for i in candidates:
            addition = min(limit - holding[i], max(1, left * portions[i] // mass), spare)
            holding[i] = holding[i] + addition
            spare = spare - addition
    return np.array(holding)


def normal_values(rng, shape, deviation, most, pieces=(), kind=jnp.bfloat16):
    level = shard_levels(rng, shape, pieces, -0.22, 0.18) if pieces else 1.0
    drawn = jax.random.normal(rng, shape, jnp.float32) * deviation * level
    return jnp.minimum(jnp.maximum(drawn, -most), most).astype(kind)


def setup_inputs(seed: int = 0) -> dict:
    splits = jax.random.split(jax.random.key(seed), 12)
    right_side = normal_values(splits[0], (3, NZ, NXA, SY), 1.0, 6.0, ((1, 4), (2, 8)), jnp.float32)
    diag_blocks = draw_diag_blocks(jax.random.fold_in(splits[11], 71), 0)
    couplings = normal_values(splits[2], (6, 3, 3, NZ, NXA, SY), 0.25, 1.0, ((3, 4), (4, 8)))
    pivot_inverse = draw_pivot_inverse(jax.random.fold_in(splits[11], 71), 0)
    lower_blocks = draw_lower_blocks(jax.random.fold_in(splits[11], 71), 0)
    upper_blocks = draw_upper_blocks(jax.random.fold_in(splits[11], 71), 0)
    active_cells = with_ends((jax.random.randint(splits[6], (NZ, NXA, SY), 0, 10) < 9).astype(jnp.int32), jax.random.fold_in(splits[6], 1), 0, 1)
    link_from = with_ends(jax.random.randint(splits[7], (SECTIONS, NNC_ALL), 0, LZ * SXD * SY), jax.random.fold_in(splits[7], 1), 0, (LZ * SXD * SY) - 1).astype(jnp.int32)
    link_owner_keys = jax.random.split(jax.random.fold_in(splits[8], 1), SECTIONS * NNC_ALL // NNC_DEV)
    link_owner_turns = jax.random.permutation(jax.random.fold_in(splits[8], 3), SECTIONS * NNC_ALL // NNC_DEV)
    link_owner = jax.vmap(lambda own, number: routed_block(jax.random.fold_in(splits[8], 2), own, number, NNC_DEV, N_AREAL, 1, CAP, 2))(link_owner_keys, link_owner_turns).reshape((SECTIONS, NNC_ALL, 1))
    link_target = with_ends(jax.random.randint(splits[9], (SECTIONS, NNC_ALL), 0, LZ * SXD * SY), jax.random.fold_in(splits[9], 1), 0, (LZ * SXD * SY) - 1).astype(jnp.int32)
    link_blocks = normal_values(splits[10], (3, 3, SECTIONS, NNC_ALL), 0.3, 1.5, ((2, 4), (3, 8)))
    return {"right_side": right_side, "diag_blocks": diag_blocks, "couplings": couplings, "pivot_inverse": pivot_inverse, "lower_blocks": lower_blocks, "upper_blocks": upper_blocks, "active_cells": active_cells, "link_from": link_from, "link_owner": link_owner, "link_target": link_target, "link_blocks": link_blocks}


tiny_square = 1e-06

def apply_block(matrix_blocks, vector):
    return lax.optimization_barrier(jnp.sum(matrix_blocks.astype(jnp.float32) * vector[None], axis=1))

def operate(vector, active, diag_blocks, couplings, link_matrix, source_flat, target_flat):
    held_cells = vector * active[None]
    padded = jnp.pad(held_cells, ((0, 0), (1, 1), (1, 1), (1, 1)))
    beside = [padded[:, :-2, 1:-1, 1:-1], padded[:, 2:, 1:-1, 1:-1], padded[:, 1:-1, :-2, 1:-1], padded[:, 1:-1, 2:, 1:-1], padded[:, 1:-1, 1:-1, :-2], padded[:, 1:-1, 1:-1, 2:]]
    result = apply_block(diag_blocks, held_cells)
    for direction in range(6):
        result = result + apply_block(couplings[direction], beside[direction])
    flattened = held_cells.reshape(3, -1)
    sending = apply_block(link_matrix, flattened[:, source_flat])
    result = result.reshape(3, -1).at[:, target_flat].add(sending).reshape(vector.shape)
    return active[None] * result + (1.0 - active[None]) * vector

def substitution_step(previous, inputs):
    current = inputs[0] - apply_block(inputs[1], previous)
    return (current, current)

def precondition(vector, pivot_inverse, lower_blocks, upper_blocks):
    scaled = apply_block(pivot_inverse, vector)
    moved = jnp.moveaxis(scaled, 1, 0)
    start = jnp.zeros(moved.shape[1:], jnp.float32)
    final_state, forward = lax.scan(substitution_step, start, (moved, jnp.moveaxis(lower_blocks, 2, 0)))
    final_state, backward = lax.scan(substitution_step, start, (forward, jnp.moveaxis(upper_blocks, 2, 0)), reverse=True)
    return jnp.moveaxis(backward, 0, 1)

def least_squares(hessenberg, initial):
    columns = hessenberg.shape[1]
    upper_form = hessenberg
    target_vector = jnp.zeros((columns + 1,), jnp.float32).at[0].set(initial)
    cosines = []
    sine_values = []
    for column in range(columns):
        entries = upper_form[:, column]
        for previous in range(column):
            upper_entry = entries[previous]
            lower_entry = entries[previous + 1]
            entries = entries.at[previous].set(cosines[previous] * upper_entry + sine_values[previous] * lower_entry)
            entries = entries.at[previous + 1].set(-sine_values[previous] * upper_entry + cosines[previous] * lower_entry)
        upper_entry = entries[column]
        lower_entry = entries[column + 1]
        radius = jnp.sqrt(upper_entry * upper_entry + lower_entry * lower_entry)
        cosines.append(upper_entry / radius)
        sine_values.append(lower_entry / radius)
        entries = entries.at[column].set(radius).at[column + 1].set(0.0)
        upper_form = upper_form.at[:, column].set(entries)
        leading = target_vector[column]
        target_vector = target_vector.at[column].set(cosines[column] * leading).at[column + 1].set(-sine_values[column] * leading)
    solution = [None] * columns
    for row_at in range(columns - 1, -1, -1):
        partial_sum = target_vector[row_at]
        for later_row in range(row_at + 1, columns):
            partial_sum = partial_sum - upper_form[row_at, later_row] * solution[later_row]
        solution[row_at] = partial_sum / upper_form[row_at, row_at]
    return solution

def reference(right_side, diag_blocks, couplings, pivot_inverse, lower_blocks, upper_blocks, active_cells, link_from, link_owner, link_target, link_blocks):
    active = active_cells.astype(jnp.float32)
    section = jnp.arange(SECTIONS, dtype=jnp.int32)[:, None]
    sender = (jnp.arange(NNC_ALL, dtype=jnp.int32) // NNC_DEV)[None, :]
    plane_cells = SXD * SY

    def global_flat(local_cell, areal_at):
        layer_at = section * LZ + local_cell // plane_cells
        row_at = areal_at * SXD + local_cell % plane_cells // SY
        return ((layer_at * NXA + row_at) * SY + local_cell % SY).reshape(-1).astype(jnp.int32)
    source_flat = global_flat(link_from, sender)
    target_flat = global_flat(link_target, link_owner[:, :, 0])
    link_matrix = link_blocks.reshape(3, 3, -1)

    def norm_of(vector):
        return jnp.sqrt(jnp.sum(vector * vector) + tiny_square)
    initial = norm_of(right_side)
    basis_list = [right_side / initial]
    directions = []
    hessenberg = jnp.zeros((ITERS + 1, ITERS), jnp.float32)
    for column in range(ITERS):
        direction = precondition(basis_list[column], pivot_inverse, lower_blocks, upper_blocks)
        directions.append(direction)
        result = operate(direction, active, diag_blocks, couplings, link_matrix, source_flat, target_flat)
        weights = jnp.stack([jnp.sum(earlier * result) for earlier in basis_list])
        for position in range(column + 1):
            result = result - weights[position] * basis_list[position]
        length = norm_of(result)
        hessenberg = hessenberg.at[:column + 1, column].set(weights).at[column + 1, column].set(length)
        basis_list.append(result / length)
    coefficients = least_squares(hessenberg, initial)
    update = coefficients[0] * directions[0]
    for position in range(1, ITERS):
        update = update + coefficients[position] * directions[position]
    return (update, hessenberg)
```

```python
import functools

import jax
import jax.numpy as jnp
from jax import lax
from jax.experimental import pallas as pl
from jax.experimental.pallas import tpu as pltpu
from jax.sharding import PartitionSpec as P

ITERS = 4
PARTS = 3
TINY = 1e-06

F32 = jnp.float32
BF16 = jnp.bfloat16
VMEM = pl.BlockSpec(memory_space=pltpu.VMEM)


def call(kernel, outs, scratch=(), name=None, flops=1 << 22, moved=1 << 20):
    many = isinstance(outs, (list, tuple))
    return pl.pallas_call(
        kernel,
        out_shape=outs,
        out_specs=[VMEM] * len(outs) if many else VMEM,
        scratch_shapes=list(scratch),
        compiler_params=pltpu.CompilerParams(vmem_limit_bytes=40 << 20),
        cost_estimate=pl.CostEstimate(flops=flops, bytes_accessed=moved, transcendentals=0),
        name=name,
    )


def wide(value):
    return value.astype(F32)


def times(blocks, vector):
    result = []
    for row in blocks:
        total = row[0] * vector[0]
        for entry, element in zip(row[1:], vector[1:]):
            total = total + entry * element
        result.append(total)
    return result


def block_at(ref, layer):
    return [[wide(ref[c, d, layer]) for d in range(3)] for c in range(3)]


def minus(left, right):
    return [a - b for a, b in zip(left, right)]


def plus(left, right):
    return [a + b for a, b in zip(left, right)]


def local_sweeps(planes, pivot, lower, upper, layers):
    forward = []
    previous = None
    for k in range(layers):
        current = times(block_at(pivot, k), planes[k])
        if previous is not None:
            current = minus(current, times(block_at(lower, k), previous))
        forward.append(current)
        previous = current
    backward = [None] * layers
    previous = None
    for k in range(layers - 1, -1, -1):
        current = forward[k]
        if previous is not None:
            current = minus(current, times(block_at(upper, k), previous))
        backward[k] = current
        previous = current
    return forward[layers - 1], backward


def section_kernel(
    right_ref, pivot_ref, lower_ref, upper_ref, active_ref,
    edge_ref, alone_ref, from_above_ref, from_below_ref, matrix_ref,
):
    layers, rows = right_ref.shape[1], right_ref.shape[2]
    planes = [[right_ref[c, k] for c in range(3)] for k in range(layers)]
    lowest, solved = local_sweeps(planes, pivot_ref, lower_ref, upper_ref, layers)
    edge_ref[...] = jnp.zeros(edge_ref.shape, F32)
    for c in range(3):
        edge_ref[c * rows : (c + 1) * rows] = lowest[c]
        edge_ref[(3 + c) * rows : (4 + c) * rows] = solved[0][c]
        for k in range(layers):
            alone_ref[c, k] = solved[k][c]
    for d in range(3):
        carried = []
        previous = None
        for k in range(layers):
            blocks = block_at(lower_ref, k)
            if previous is None:
                previous = [-blocks[c][d] for c in range(3)]
            else:
                previous = [-value for value in times(blocks, previous)]
            carried.append(previous)
        for c in range(3):
            matrix_ref[(c * 3 + d) * rows : (c * 3 + d + 1) * rows] = carried[-1][c]
        response = carried[-1]
        for k in range(layers - 1, -1, -1):
            if k < layers - 1:
                response = minus(carried[k], times(block_at(upper_ref, k), response))
            for c in range(3):
                from_above_ref[c, d, k] = response[c]
        for c in range(3):
            matrix_ref[(9 + c * 3 + d) * rows : (10 + c * 3 + d) * rows] = response[c]
        response = None
        for k in range(layers - 1, -1, -1):
            blocks = block_at(upper_ref, k)
            if response is None:
                for c in range(3):
                    matrix_ref[(27 + c * 3 + d) * rows : (28 + c * 3 + d) * rows] = blocks[c][d]
                response = [-blocks[c][d] for c in range(3)]
            else:
                response = [-value for value in times(blocks, response)]
            for c in range(3):
                from_below_ref[c, d, k] = response[c]
        for c in range(3):
            matrix_ref[(18 + c * 3 + d) * rows : (19 + c * 3 + d) * rows] = response[c]
    matrix_ref[36 * rows : 37 * rows] = wide(active_ref[0])
    matrix_ref[37 * rows : 38 * rows] = wide(active_ref[layers - 1])


def routing_kernel(
    peers, from_ref, owner_ref, target_ref, block_ref,
    slot_block_ref, slot_source_ref, slot_target_ref, stacked, products,
):
    rows, width = from_ref.shape
    slots = slot_source_ref.shape[0]
    per_peer = slots // peers
    owner = owner_ref[...]
    for o in range(peers):
        stacked[o * rows : (o + 1) * rows] = jnp.where(owner == o, 1.0, 0.0).astype(BF16)
    chosen = stacked[...]
    ones_before = jnp.where(
        lax.broadcasted_iota(jnp.int32, (width, width), 0)
        < lax.broadcasted_iota(jnp.int32, (width, width), 1),
        1.0,
        0.0,
    ).astype(BF16)
    within = jnp.dot(chosen, ones_before, preferred_element_type=F32)
    totals = jnp.dot(chosen, jnp.ones((width, width), BF16), preferred_element_type=F32)
    row_before = jnp.where(
        lax.broadcasted_iota(jnp.int32, (rows, rows), 1)
        < lax.broadcasted_iota(jnp.int32, (rows, rows), 0),
        1.0,
        0.0,
    ).astype(BF16)
    rank = jnp.zeros((rows, width), F32)
    for o in range(peers):
        part = slice(o * rows, (o + 1) * rows)
        before = jnp.dot(row_before, totals[part].astype(BF16), preferred_element_type=F32)
        rank = rank + jnp.where(owner == o, within[part] + before, 0.0)
    rank = rank.astype(jnp.int32)
    slot_row = owner * per_peer + rank // width
    slot_column = rank % width
    source = from_ref[...]
    target = target_ref[...]
    payloads = [
        wide(source // width),
        wide(source % width),
        wide(target // width),
        wide(target % width),
    ] + [wide(block_ref[c, d]) for c in range(3) for d in range(3)]
    row_number = lax.broadcasted_iota(jnp.int32, (slots, width), 0)
    column_number = lax.broadcasted_iota(jnp.int32, (width, width), 0)
    total = jnp.zeros((len(payloads) * slots, width), F32)
    for r in range(rows):
        in_row = row_number == slot_row[r : r + 1]
        left = jnp.concatenate(
            [jnp.where(in_row, payload[r : r + 1], 0.0).astype(BF16) for payload in payloads], axis=0
        )
        right = jnp.where(column_number == slot_column[r : r + 1], 1.0, 0.0).astype(BF16)
        total = total + lax.dot_general(
            left, right, (((1,), (1,)), ((), ())), preferred_element_type=F32
        )
    products[...] = total
    slot_source_ref[...] = (products[0:slots] * width + products[slots : 2 * slots]).astype(jnp.int32)
    slot_target_ref[...] = products[2 * slots : 3 * slots] * width + products[3 * slots : 4 * slots]
    for c in range(3):
        for d in range(3):
            at = 4 + c * 3 + d
            slot_block_ref[c, d] = products[at * slots : (at + 1) * slots]


def couple_kernel(
    first, sections, edge_ref, matrix_ref, alone_ref, above_ref, below_ref, active_ref,
    slot_block_ref, slot_source_ref, slot_target_ref,
    solved_ref, layer_ref, sent_ref, arriving, tops, borders, table,
):
    layers, rows = alone_ref.shape[1], alone_ref.shape[2]
    width = alone_ref.shape[3]
    peers = sent_ref.shape[0]
    slots = slot_source_ref.shape[0]
    per_peer = slots // peers
    s = lax.axis_index("layer")
    a = lax.axis_index("areal")

    def matrix(section, which):
        return [
            [
                matrix_ref[section, (which * 9 + c * 3 + d) * rows : (which * 9 + c * 3 + d + 1) * rows]
                for d in range(3)
            ]
            for c in range(3)
        ]

    def edge(section, which):
        return [
            edge_ref[section, (which * 3 + c) * rows : (which * 3 + c + 1) * rows] for c in range(3)
        ]

    zero = jnp.zeros((rows, width), F32)
    coming = [[zero] * 3]
    for section in range(1, sections):
        value = edge(section - 1, 0)
        if section > 1:
            value = plus(value, times(matrix(section - 1, 0), coming[section - 1]))
        coming.append(value)
    rising = [None] * sections + [[zero] * 3]
    for section in range(sections - 1, 0, -1):
        value = plus(edge(section, 1), times(matrix(section, 1), coming[section]))
        if section < sections - 1:
            value = plus(value, times(matrix(section, 2), rising[section + 1]))
        rising[section] = value
    rising[0] = [zero] * 3
    for section in range(sections):
        for c in range(3):
            arriving[section, c] = coming[section][c]
            tops[section, c] = rising[section + 1][c]
    above = [arriving[s, c] for c in range(3)]
    below = [tops[s, c] for c in range(3)]
    active = [wide(active_ref[k]) for k in range(layers)]
    for k in range(layers):
        for c in range(3):
            value = alone_ref[c, k]
            for d in range(3):
                value = value + above_ref[c, d, k] * above[d] + below_ref[c, d, k] * below[d]
            solved_ref[c, k] = value
            held = value * active[k]
            table[c, k * rows : (k + 1) * rows] = held
            borders[0, c * layers + k : c * layers + k + 1] = held[0:1]
            borders[1, c * layers + k : c * layers + k + 1] = held[rows - 1 : rows]
    before = jnp.maximum(s - 1, 0)
    after = jnp.minimum(s + 1, sections - 1)
    bottom = [
        [
            matrix_ref[before, (27 + c * 3 + d) * rows : (28 + c * 3 + d) * rows]
            for d in range(3)
        ]
        for c in range(3)
    ]
    own_top = [solved_ref[c, 0] for c in range(3)]
    upstairs = minus(above, times(bottom, own_top))
    upper_active = jnp.where(s > 0, matrix_ref[before, 37 * rows : 38 * rows], 0.0)
    lower_active = jnp.where(s < sections - 1, matrix_ref[after, 36 * rows : 37 * rows], 0.0)
    for c in range(3):
        layer_ref[0, c] = upstairs[c] * upper_active
        layer_ref[1, c] = below[c] * lower_active
    half = 128
    groups = [(g, h) for g in range(slots // 8) for h in range(width // half)]
    for g in range(slots // 8):
        for h in range(width // half):
            source = slot_source_ref[g * 8 : (g + 1) * 8, h * half : (h + 1) * half]
            line = source // half
            lane = source % half
            found = [jnp.zeros((8, half), F32)] * 3
            for r in range(layers * rows):
                for q in range(width // half):
                    here = line == r * (width // half) + q
                    for c in range(3):
                        row = jnp.broadcast_to(
                            table[c, r : r + 1, q * half : (q + 1) * half], (8, half)
                        )
                        picked = jnp.take_along_axis(row, lane, axis=1)
                        found[c] = jnp.where(here, picked, found[c])
            for c in range(3):
                value = slot_block_ref[c, 0, g * 8 : (g + 1) * 8, h * half : (h + 1) * half] * found[0]
                for d in range(1, 3):
                    value = value + (
                        slot_block_ref[c, d, g * 8 : (g + 1) * 8, h * half : (h + 1) * half] * found[d]
                    )
                for i in range(8):
                    slot = g * 8 + i
                    peer, at = slot // per_peer, slot % per_peer
                    sent_ref[
                        peer, c * per_peer + at : c * per_peer + at + 1, h * half : (h + 1) * half
                    ] = value[i : i + 1]
    base = 3 * per_peer
    many = 3 * layers
    sums = edge_ref[0, 6 * rows : 6 * rows + 1]
    for section in range(1, sections):
        sums = sums + edge_ref[section, 6 * rows : 6 * rows + 1]
    for peer in range(peers):
        side = jnp.where(peer > a, 1, 0)
        sent_ref[peer, base : base + many] = borders[side, 0:many]
        sent_ref[peer, base + many : base + many + 1] = sums
        if first:
            sent_ref[peer, base + many + 1 : base + many + 1 + per_peer] = slot_target_ref[
                peer * per_peer : (peer + 1) * per_peer
            ]


def weights_of(sums, upto):
    value = lambda step, at: sums[step : step + 1, at : at + 1]
    squared = value(0, 0)
    beta = jnp.sqrt(squared + TINY)
    unscale = 1.0 / beta
    gram = [[squared * unscale * unscale]]
    columns = []
    lengths = []
    for step in range(upto):
        if step == 0:
            weights = [value(0, 1) * unscale * unscale]
            own = value(0, 2) * unscale * unscale
        else:
            weights = [value(step, i) for i in range(step + 1)]
            own = value(step, step + 1)
        size = step + 1
        shadow = []
        for i in range(size):
            total = weights[0] * gram[i][0]
            for k in range(1, size):
                total = total + weights[k] * gram[i][k]
            shadow.append(total)
        left = own
        for i in range(size):
            left = left - weights[i] * (2.0 * weights[i] - shadow[i])
        left = jnp.maximum(left, 0.0)
        length = jnp.sqrt(left + TINY)
        inverse = 1.0 / length
        column = [(weights[i] - shadow[i]) * inverse for i in range(size)]
        for i in range(size):
            gram[i].append(column[i])
        gram.append(column + [left * inverse * inverse])
        columns.append(weights)
        lengths.append(length)
    return beta, unscale, columns, lengths


def operate_kernel(step, *refs):
    last = step == ITERS - 1
    (got_ref, target_ref, solved_ref, layer_ref, diag_ref, coupling_ref, active_ref) = refs[:7]
    at = 7
    if not last:
        pivot_ref, lower_ref, upper_ref = refs[at : at + 3]
        at += 3
    right_ref = refs[at]
    at += 1
    if step > 0:
        sums_ref = refs[at]
        at += 1
        earlier = []
        for i in range(step):
            earlier.append(refs[at : at + (2 if i == 0 else 3)])
            at += len(earlier[-1])
    outs = refs[at:]
    layers, rows, width = solved_ref.shape[1:]
    peers = got_ref.shape[0]
    per_peer = layers * rows // peers
    base = 3 * per_peer
    many = 3 * layers
    cells = layers * rows
    a = lax.axis_index("areal")
    total_ref = outs[-1]
    products_ref = outs[-2]
    outs = outs[:-2]

    row_number = lax.broadcasted_iota(jnp.int32, (cells, width), 0)
    column_number = lax.broadcasted_iota(jnp.int32, (width, width), 0)
    total_ref[...] = jnp.zeros(total_ref.shape, F32)

    def from_peer(peer, carry):
        lefts, rights = [], []
        for i in range(per_peer):
            where = target_ref[peer, base + many + 1 + i : base + many + 2 + i].astype(jnp.int32)
            in_row = row_number == where // width
            rights.append(jnp.where(column_number == where % width, 1.0, 0.0).astype(BF16))
            pieces = []
            for c in range(3):
                rest = got_ref[peer, c * per_peer + i : c * per_peer + i + 1]
                for part in range(PARTS):
                    piece = rest.astype(BF16).astype(F32)
                    rest = rest - piece
                    pieces.append(jnp.where(in_row, piece, 0.0).astype(BF16))
            lefts.append(jnp.concatenate(pieces, axis=0))
        left = jnp.concatenate(lefts, axis=1)
        right = jnp.concatenate(rights, axis=1)
        total_ref[...] += lax.dot_general(
            left, right, (((1,), (1,)), ((), ())), preferred_element_type=F32
        )
        return carry

    lax.fori_loop(0, peers, from_peer, 0)

    active = [wide(active_ref[k]) for k in range(layers)]
    held = [[solved_ref[c, k] * active[k] for c in range(3)] for k in range(layers)]
    row_at = lax.broadcasted_iota(jnp.int32, (rows, width), 0)
    column_at = lax.broadcasted_iota(jnp.int32, (rows, width), 1)
    before, after = jnp.maximum(a - 1, 0), jnp.minimum(a + 1, peers - 1)
    has_before = jnp.where(a > 0, 1.0, 0.0)
    has_after = jnp.where(a < peers - 1, 1.0, 0.0)
    applied = []
    for k in range(layers):
        beside = []
        beside.append(held[k - 1] if k > 0 else [layer_ref[0, c] for c in range(3)])
        beside.append(held[k + 1] if k < layers - 1 else [layer_ref[1, c] for c in range(3)])
        sides = [[], [], [], []]
        for c in range(3):
            border = base + c * layers + k
            low = got_ref[before, border : border + 1] * has_before
            high = got_ref[after, border : border + 1] * has_after
            value = held[k][c]
            sides[0].append(jnp.where(row_at == 0, low, pltpu.roll(value, 1, 0)))
            sides[1].append(jnp.where(row_at == rows - 1, high, pltpu.roll(value, rows - 1, 0)))
            sides[2].append(jnp.where(column_at == 0, 0.0, pltpu.roll(value, 1, 1)))
            sides[3].append(jnp.where(column_at == width - 1, 0.0, pltpu.roll(value, width - 1, 1)))
        result = times(block_at(diag_ref, k), held[k])
        for d, neighbour in enumerate(beside + sides):
            blocks = [[wide(coupling_ref[d, i, j, k]) for j in range(3)] for i in range(3)]
            result = plus(result, times(blocks, neighbour))
        for c in range(3):
            for part in range(PARTS):
                start = (c * PARTS + part) * cells + k * rows
                result[c] = result[c] + total_ref[start : start + rows]
        applied.append(
            [
                active[k] * result[c] + (1.0 - active[k]) * solved_ref[c, k]
                for c in range(3)
            ]
        )

    pairs = []
    if step == 0:
        (applied_ref, edge_ref, alone_ref) = outs
        for k in range(layers):
            for c in range(3):
                applied_ref[c, k] = applied[k][c]
        new = applied
        r = [[right_ref[c, k] for c in range(3)] for k in range(layers)]
        pairs = [(r, r), (r, applied), (applied, applied)]
    else:
        if last:
            (v_ref, z_ref, edge_ref, history_ref) = outs
        else:
            (v_ref, z_ref, w_ref, edge_ref, alone_ref, history_ref) = outs
        fresh = got_ref[0, base + many : base + many + 1]
        for peer in range(1, peers):
            fresh = fresh + got_ref[peer, base + many : base + many + 1]
        history_row = lax.broadcasted_iota(jnp.int32, history_ref.shape, 0)
        sums = jnp.where(history_row == step - 1, fresh, sums_ref[...])
        history_ref[...] = sums
        beta, unscale, columns, lengths = weights_of(sums, step)
        weights = columns[-1]
        inverse = 1.0 / lengths[-1]
        spread = lambda value: jnp.broadcast_to(value, (rows, width))
        lead = spread(inverse * unscale if step == 1 else inverse)
        factors = [spread(weights[i] * inverse * (unscale if i == 0 else 1.0)) for i in range(step)]
        new = []
        members = []
        v_all = [[] for _ in range(step)]
        for k in range(layers):
            new.append([])
            members.append([])
            for c in range(3):
                old_v = [right_ref[c, k]] + [earlier[i][0][c, k] for i in range(1, step)]
                old_z = [earlier[0][0][c, k]] + [earlier[i][1][c, k] for i in range(1, step)]
                old_w = [earlier[0][1][c, k]] + [earlier[i][2][c, k] for i in range(1, step)]
                v = old_w[-1] * lead
                z = solved_ref[c, k] * lead
                w = applied[k][c] * lead
                for i in range(step):
                    v = v - factors[i] * old_v[i]
                    z = z - factors[i] * old_z[i]
                    w = w - factors[i] * old_w[i]
                v_ref[c, k] = v
                z_ref[c, k] = z
                if not last:
                    w_ref[c, k] = w
                new[k].append(w)
                members[k].append(v)
        first = spread(unscale)
        basis = [[[right_ref[c, k] * first for c in range(3)] for k in range(layers)]]
        for i in range(1, step):
            basis.append([[earlier[i][0][c, k] for c in range(3)] for k in range(layers)])
        basis.append(members)
        pairs = [(member, new) for member in basis] + [(new, new)]

    edge_ref[...] = jnp.zeros(edge_ref.shape, F32)
    lane = lax.broadcasted_iota(jnp.int32, (1, width), 1)
    line = jnp.zeros((1, width), F32)
    for number, (left, right) in enumerate(pairs):
        total = jnp.zeros((rows, width), F32)
        for k in range(layers):
            for c in range(3):
                total = total + left[k][c] * right[k][c]
        total = jnp.sum(jnp.sum(total, axis=0, keepdims=True), axis=1, keepdims=True)
        line = jnp.where(lane == number, total, line)
    if last:
        for peer in range(edge_ref.shape[0]):
            edge_ref[peer] = line
    else:
        edge_ref[6 * rows : 6 * rows + 1] = line
        lowest, alone = local_sweeps(new, pivot_ref, lower_ref, upper_ref, layers)
        for c in range(3):
            edge_ref[c * rows : (c + 1) * rows] = lowest[c]
            edge_ref[(3 + c) * rows : (4 + c) * rows] = alone[0][c]
            for k in range(layers):
                alone_ref[c, k] = alone[k][c]


def finish_kernel(dots_ref, sums_ref, z0_ref, z1_ref, z2_ref, z3_ref, update_ref, hessenberg_ref):
    z_refs = (z0_ref, z1_ref, z2_ref, z3_ref)
    rows, width = z0_ref.shape[2:]
    fresh = dots_ref[0]
    for peer in range(1, dots_ref.shape[0]):
        fresh = fresh + dots_ref[peer]
    history_row = lax.broadcasted_iota(jnp.int32, sums_ref.shape, 0)
    sums = jnp.where(history_row == ITERS - 1, fresh, sums_ref[...])
    beta, unscale, columns, lengths = weights_of(sums, ITERS)
    shape = hessenberg_ref.shape
    row_at = lax.broadcasted_iota(jnp.int32, shape, 0)
    column_at = lax.broadcasted_iota(jnp.int32, shape, 1)
    table = jnp.zeros(shape, F32)
    for j in range(ITERS):
        for i, weight in enumerate(columns[j] + [lengths[j]]):
            table = jnp.where((row_at == i) & (column_at == j), weight, table)
    hessenberg_ref[...] = table
    goal = [beta]
    triangle = []
    rotations = []
    for j in range(ITERS):
        entries = list(columns[j])
        for i, (cosine, sine) in enumerate(rotations):
            upper, lower = entries[i], entries[i + 1]
            entries[i] = cosine * upper + sine * lower
            entries[i + 1] = cosine * lower - sine * upper
        radius = jnp.sqrt(entries[j] * entries[j] + lengths[j] * lengths[j])
        cosine, sine = entries[j] / radius, lengths[j] / radius
        rotations.append((cosine, sine))
        entries[j] = radius
        triangle.append(entries)
        leading = goal[j]
        goal[j] = cosine * leading
        goal.append(-sine * leading)
    answer = [None] * ITERS
    for i in range(ITERS - 1, -1, -1):
        partial = goal[i]
        for j in range(i + 1, ITERS):
            partial = partial - triangle[j][i] * answer[j]
        answer[i] = partial / triangle[i][i]
    factors = [
        jnp.broadcast_to(answer[j] * unscale if j == 0 else answer[j], (rows, width))
        for j in range(ITERS)
    ]
    for c in range(3):
        for k in range(z0_ref.shape[1]):
            value = factors[0] * z_refs[0][c, k]
            for j in range(1, ITERS):
                value = value + factors[j] * z_refs[j][c, k]
            update_ref[c, k] = value


def shape_of(*dims, kind=F32):
    return jax.ShapeDtypeStruct(dims, kind)


def local(
    right_side,
    diag_blocks,
    couplings,
    pivot_inverse,
    lower_blocks,
    upper_blocks,
    active_cells,
    link_from,
    link_owner,
    link_target,
    link_blocks,
):
    _, layers, rows, width = right_side.shape
    peers = lax.axis_size("areal")
    sections = lax.axis_size("layer")
    links = link_from.shape[1]
    capacity = 2 * links // peers
    slots = capacity * peers // width
    per_peer = slots // peers
    link_rows = links // width
    field = shape_of(3, layers, rows, width)
    edge_rows = 7 * rows
    sent_rows = -(-(4 * per_peer + 3 * layers + 1) // 8) * 8
    edge_shape = shape_of(edge_rows, width)

    edge, alone, from_above, from_below, matrices = call(
        section_kernel,
        [
            edge_shape,
            field,
            shape_of(3, 3, layers, rows, width),
            shape_of(3, 3, layers, rows, width),
            shape_of(38 * rows, width),
        ],
        name="sections",
    )(right_side, pivot_inverse, lower_blocks, upper_blocks, active_cells)
    all_matrices = lax.all_gather(matrices, "layer", axis=0, tiled=False)
    slot_block, slot_source, slot_target = call(
        functools.partial(routing_kernel, peers),
        [
            shape_of(3, 3, slots, width),
            shape_of(slots, width, kind=jnp.int32),
            shape_of(slots, width),
        ],
        [
            pltpu.VMEM((peers * link_rows, width), BF16),
            pltpu.VMEM((13 * slots, width), F32),
        ],
        name="routing",
    )(
        link_from.reshape(link_rows, width),
        link_owner.reshape(link_rows, width),
        link_target.reshape(link_rows, width),
        link_blocks.reshape(3, 3, link_rows, width),
    )

    target = None
    sums = jnp.zeros((8, width), F32)
    earlier = []
    zs = []
    for step in range(ITERS):
        last = step == ITERS - 1
        edges = lax.all_gather(edge, "layer", axis=0, tiled=False)
        solved, layer_sides, sent = call(
            functools.partial(couple_kernel, step == 0, sections),
            [field, shape_of(2, 3, rows, width), shape_of(peers, sent_rows, width)],
            [
                pltpu.VMEM((sections, 3, rows, width), F32),
                pltpu.VMEM((sections, 3, rows, width), F32),
                pltpu.VMEM((2, 16, width), F32),
                pltpu.VMEM((3, layers * rows, width), F32),
            ],
            name="couple",
        )(
            edges, all_matrices, alone, from_above, from_below, active_cells,
            slot_block, slot_source, slot_target,
        )
        got = lax.all_to_all(sent, "areal", split_axis=0, concat_axis=0, tiled=True)
        if step == 0:
            target = got
        operands = [got, target, solved, layer_sides, diag_blocks, couplings, active_cells]
        if not last:
            operands += [pivot_inverse, lower_blocks, upper_blocks]
        operands.append(right_side)
        if step > 0:
            operands.append(sums)
            for group in earlier:
                operands += list(group)
        history = shape_of(8, width)
        if step == 0:
            outs = [field, edge_shape, field]
        elif last:
            outs = [field, field, shape_of(peers * sections, 1, width), history]
        else:
            outs = [field, field, field, edge_shape, field, history]
        results = call(
            functools.partial(operate_kernel, step),
            outs,
            [
                pltpu.VMEM((8, 128), F32),
                pltpu.VMEM((3 * PARTS * layers * rows, width), F32),
            ],
            name="operate",
        )(*operands)
        if step == 0:
            applied, edge, alone = results
            earlier.append((solved, applied))
            zs.append(solved)
        elif last:
            _, z, dots, sums = results
            zs.append(z)
        else:
            v, z, w, edge, alone, sums = results
            earlier.append((v, z, w))
            zs.append(z)
    dots = lax.all_to_all(dots, ("areal", "layer"), split_axis=0, concat_axis=0, tiled=True)
    update, hessenberg = call(
        finish_kernel, [field, shape_of(ITERS + 1, ITERS)], name="finish"
    )(dots, sums, *zs)
    return update, hessenberg


def solution(mesh):
    placed = (
        P(None, "layer", "areal", None),
        P(None, None, "layer", "areal", None),
        P(None, None, None, "layer", "areal", None),
        P(None, None, "layer", "areal", None),
        P(None, None, "layer", "areal", None),
        P(None, None, "layer", "areal", None),
        P("layer", "areal", None),
        P("layer", "areal"),
        P("layer", "areal", None),
        P("layer", "areal"),
        P(None, None, "layer", "areal"),
    )
    return jax.shard_map(
        local,
        mesh=mesh,
        in_specs=placed,
        out_specs=(P(None, "layer", "areal", None), P()),
        check_vma=False,
    )
```

```python
import functools

import jax
import jax.numpy as jnp
from jax import lax
from jax.experimental import pallas as pl
from jax.experimental.pallas import tpu as pltpu
from jax.sharding import PartitionSpec as P

ITERS = 4
PARTS = 3
TINY = 1e-06

F32 = jnp.float32
BF16 = jnp.bfloat16
VMEM = pl.BlockSpec(memory_space=pltpu.VMEM)


def call(kernel, outs, scratch=(), name=None, inputs=None, flops=1 << 22, moved=1 << 20):
    many = isinstance(outs, (list, tuple))
    where = {} if inputs is None else {"in_specs": inputs}
    return pl.pallas_call(
        kernel,
        out_shape=outs,
        **where,
        out_specs=[VMEM] * len(outs) if many else VMEM,
        scratch_shapes=list(scratch),
        compiler_params=pltpu.CompilerParams(vmem_limit_bytes=40 << 20),
        cost_estimate=pl.CostEstimate(flops=flops, bytes_accessed=moved, transcendentals=0),
        name=name,
    )


def wide(value):
    return value.astype(F32)


def times(blocks, vector):
    result = []
    for row in blocks:
        total = row[0] * vector[0]
        for entry, element in zip(row[1:], vector[1:]):
            total = total + entry * element
        result.append(total)
    return result


def block_at(ref, layer):
    return [[wide(ref[c, d, layer]) for d in range(3)] for c in range(3)]


def minus(left, right):
    return [a - b for a, b in zip(left, right)]


def plus(left, right):
    return [a + b for a, b in zip(left, right)]


def local_sweeps(planes, pivot, lower, upper, layers):
    forward = []
    previous = None
    for k in range(layers):
        current = times(block_at(pivot, k), planes[k])
        if previous is not None:
            current = minus(current, times(block_at(lower, k), previous))
        forward.append(current)
        previous = current
    backward = [None] * layers
    previous = None
    for k in range(layers - 1, -1, -1):
        current = forward[k]
        if previous is not None:
            current = minus(current, times(block_at(upper, k), previous))
        backward[k] = current
        previous = current
    return forward[layers - 1], backward


def section_part(
    right_ref, pivot_ref, lower_ref, upper_ref, active_ref,
    edge_ref, next_ref, alone_ref, from_above_ref, from_below_ref, matrix_ref,
):
    layers, rows = right_ref.shape[1], right_ref.shape[2]
    planes = [[right_ref[c, k] for c in range(3)] for k in range(layers)]
    lowest, solved = local_sweeps(planes, pivot_ref, lower_ref, upper_ref, layers)
    for c in range(3):
        for ref in (edge_ref, next_ref):
            ref[c * rows : (c + 1) * rows] = lowest[c]
            ref[(3 + c) * rows : (4 + c) * rows] = solved[0][c]
        for k in range(layers):
            alone_ref[c, k] = solved[k][c]
    for d in range(3):
        carried = []
        previous = None
        for k in range(layers):
            blocks = block_at(lower_ref, k)
            if previous is None:
                previous = [-blocks[c][d] for c in range(3)]
            else:
                previous = [-value for value in times(blocks, previous)]
            carried.append(previous)
        for c in range(3):
            matrix_ref[(c * 3 + d) * rows : (c * 3 + d + 1) * rows] = carried[-1][c]
        response = carried[-1]
        for k in range(layers - 1, -1, -1):
            if k < layers - 1:
                response = minus(carried[k], times(block_at(upper_ref, k), response))
            for c in range(3):
                from_above_ref[c, d, k] = response[c]
        for c in range(3):
            matrix_ref[(9 + c * 3 + d) * rows : (10 + c * 3 + d) * rows] = response[c]
        response = None
        for k in range(layers - 1, -1, -1):
            blocks = block_at(upper_ref, k)
            if response is None:
                for c in range(3):
                    next_ref[(6 + c * 3 + d) * rows : (7 + c * 3 + d) * rows] = blocks[c][d]
                response = [-blocks[c][d] for c in range(3)]
            else:
                response = [-value for value in times(blocks, response)]
            for c in range(3):
                from_below_ref[c, d, k] = response[c]
        for c in range(3):
            matrix_ref[(18 + c * 3 + d) * rows : (19 + c * 3 + d) * rows] = response[c]
    edge_ref[6 * rows : 7 * rows] = wide(active_ref[0])
    next_ref[15 * rows : 16 * rows] = wide(active_ref[layers - 1])


def routing_part(
    peers, folded, block_ref, slot_block_ref, slot_source_ref, slot_target_ref, stacked, products
):
    rows, width = folded.shape[1:]
    slots = slot_source_ref.shape[0]
    per_peer = slots // peers
    owner = folded[1]
    for o in range(peers):
        stacked[o * rows : (o + 1) * rows] = jnp.where(owner == o, 1.0, 0.0).astype(BF16)
    chosen = stacked[...]
    ones_before = jnp.where(
        lax.broadcasted_iota(jnp.int32, (width, width), 0)
        < lax.broadcasted_iota(jnp.int32, (width, width), 1),
        1.0,
        0.0,
    ).astype(BF16)
    within = jnp.dot(chosen, ones_before, preferred_element_type=F32)
    totals = jnp.dot(chosen, jnp.ones((width, width), BF16), preferred_element_type=F32)
    row_before = jnp.where(
        lax.broadcasted_iota(jnp.int32, (rows, rows), 1)
        < lax.broadcasted_iota(jnp.int32, (rows, rows), 0),
        1.0,
        0.0,
    ).astype(BF16)
    rank = jnp.zeros((rows, width), F32)
    for o in range(peers):
        part = slice(o * rows, (o + 1) * rows)
        before = jnp.dot(row_before, totals[part].astype(BF16), preferred_element_type=F32)
        rank = rank + jnp.where(owner == o, within[part] + before, 0.0)
    rank = rank.astype(jnp.int32)
    slot_row = owner * per_peer + rank // width
    slot_column = rank % width
    source = folded[0]
    target = folded[2]
    payloads = [
        wide(source // width),
        wide(source % width),
        wide(target // width),
        wide(target % width),
    ]
    row_number = lax.broadcasted_iota(jnp.int32, (slots, width), 0)
    column_number = lax.broadcasted_iota(jnp.int32, (width, width), 0)
    total = jnp.zeros(products.shape, F32)
    for r in range(rows):
        in_row = row_number == slot_row[r : r + 1]
        left = jnp.concatenate(
            [
                jnp.where(in_row, payload, 0.0).astype(BF16)
                for payload in [payload[r : r + 1] for payload in payloads]
                + [
                    wide(block_ref[c, d : d + 1, r * width : (r + 1) * width])
                    for c in range(3)
                    for d in range(3)
                ]
            ],
            axis=0,
        )
        right = jnp.where(column_number == slot_column[r : r + 1], 1.0, 0.0).astype(BF16)
        total = total + lax.dot_general(
            left, right, (((1,), (1,)), ((), ())), preferred_element_type=F32
        )
    products[...] = total
    slot_source_ref[...] = (products[0:slots] * width + products[slots : 2 * slots]).astype(jnp.int32)
    slot_target_ref[...] = products[2 * slots : 3 * slots] * width + products[3 * slots : 4 * slots]
    for c in range(3):
        for d in range(3):
            at = 4 + c * 3 + d
            slot_block_ref[c, d] = products[at * slots : (at + 1) * slots]


def setup_kernel(
    peers,
    right_hbm, pivot_hbm, lower_hbm, upper_hbm, active_hbm,
    from_hbm, owner_hbm, target_hbm, block_hbm,
    edge_ref, next_ref, alone_ref, from_above_ref, from_below_ref, matrix_ref,
    slot_block_ref, slot_source_ref, slot_target_ref,
    right_ref, pivot_ref, lower_ref, upper_ref, active_ref,
    from_ref, owner_ref, target_ref, block_ref,
    stacked, products, folded, semaphores,
):
    copies = [
        pltpu.make_async_copy(source, landing, semaphores.at[number])
        for number, (source, landing) in enumerate(
            [
                (lower_hbm, lower_ref),
                (upper_hbm, upper_ref),
                (active_hbm, active_ref),
                (pivot_hbm, pivot_ref),
                (right_hbm, right_ref),
                (owner_hbm, owner_ref),
                (from_hbm, from_ref),
                (target_hbm, target_ref),
                (block_hbm, block_ref),
            ]
        )
    ]
    for copy in copies:
        copy.start()
    for copy in copies:
        copy.wait()
    section_part(
        right_ref, pivot_ref, lower_ref, upper_ref, active_ref,
        edge_ref, next_ref, alone_ref, from_above_ref, from_below_ref, matrix_ref,
    )
    rows, width = folded.shape[1:]
    for r in range(rows):
        for number, ref in enumerate((from_ref, owner_ref, target_ref)):
            folded[number, r : r + 1] = ref[0:1, r * width : (r + 1) * width]
    routing_part(
        peers, folded, block_ref, slot_block_ref, slot_source_ref, slot_target_ref, stacked, products
    )


def couple_kernel(
    first, sections, *refs,
):
    turned, refs = refs[: sections - 1], refs[sections - 1 :]
    if first:
        own_ref, refs = refs[0], refs[1:]
        edge_ref = refs[-1]
        refs = refs[:-1]
    else:
        edge_ref, refs = refs[0], refs[1:]
    (
        matrix_ref, alone_ref, above_ref, below_ref, active_ref,
        slot_block_ref, slot_source_ref, slot_target_ref,
        solved_ref, layer_ref, sent_ref, arriving, tops, borders, table,
    ) = refs
    layers, rows = alone_ref.shape[1], alone_ref.shape[2]
    width = alone_ref.shape[3]
    peers = sent_ref.shape[0]
    slots = slot_source_ref.shape[0]
    per_peer = slots // peers
    s = lax.axis_index("layer")
    a = lax.axis_index("areal")
    if first:
        edge_ref[s] = own_ref[0 : 6 * rows]
        for turn in range(1, sections):
            edge_ref[lax.rem(s - turn + sections, sections)] = turned[turn - 1][0 : 6 * rows]

    def matrix(section, which):
        return [
            [
                matrix_ref[section, (which * 9 + c * 3 + d) * rows : (which * 9 + c * 3 + d + 1) * rows]
                for d in range(3)
            ]
            for c in range(3)
        ]

    def edge(section, which):
        return [
            edge_ref[section, (which * 3 + c) * rows : (which * 3 + c + 1) * rows] for c in range(3)
        ]

    zero = jnp.zeros((rows, width), F32)
    coming = [[zero] * 3]
    for section in range(1, sections):
        value = edge(section - 1, 0)
        if section > 1:
            value = plus(value, times(matrix(section - 1, 0), coming[section - 1]))
        coming.append(value)
    rising = [None] * sections + [[zero] * 3]
    for section in range(sections - 1, 0, -1):
        value = plus(edge(section, 1), times(matrix(section, 1), coming[section]))
        if section < sections - 1:
            value = plus(value, times(matrix(section, 2), rising[section + 1]))
        rising[section] = value
    rising[0] = [zero] * 3
    for section in range(sections):
        for c in range(3):
            arriving[section, c] = coming[section][c]
            tops[section, c] = rising[section + 1][c]
    above = [arriving[s, c] for c in range(3)]
    below = [tops[s, c] for c in range(3)]
    active = [wide(active_ref[k]) for k in range(layers)]
    for k in range(layers):
        for c in range(3):
            value = alone_ref[c, k]
            for d in range(3):
                value = value + above_ref[c, d, k] * above[d] + below_ref[c, d, k] * below[d]
            solved_ref[c, k] = value
            held = value * active[k]
            table[c, k * rows : (k + 1) * rows] = held
            borders[0, c * layers + k : c * layers + k + 1] = held[0:1]
            borders[1, c * layers + k : c * layers + k + 1] = held[rows - 1 : rows]
    previous, following = turned[0], turned[-1]
    bottom = [
        [previous[(6 + c * 3 + d) * rows : (7 + c * 3 + d) * rows] for d in range(3)]
        for c in range(3)
    ]
    own_top = [solved_ref[c, 0] for c in range(3)]
    upstairs = minus(above, times(bottom, own_top))
    upper_active = jnp.where(s > 0, previous[15 * rows : 16 * rows], 0.0)
    lower_active = jnp.where(s < sections - 1, following[6 * rows : 7 * rows], 0.0)
    for c in range(3):
        layer_ref[0, c] = upstairs[c] * upper_active
        layer_ref[1, c] = below[c] * lower_active
    half = 128
    groups = [(g, h) for g in range(slots // 8) for h in range(width // half)]
    for g in range(slots // 8):
        for h in range(width // half):
            source = slot_source_ref[g * 8 : (g + 1) * 8, h * half : (h + 1) * half]
            line = source // half
            lane = source % half
            found = [jnp.zeros((8, half), F32)] * 3
            for r in range(layers * rows):
                for q in range(width // half):
                    here = line == r * (width // half) + q
                    for c in range(3):
                        row = jnp.broadcast_to(
                            table[c, r : r + 1, q * half : (q + 1) * half], (8, half)
                        )
                        picked = jnp.take_along_axis(row, lane, axis=1)
                        found[c] = jnp.where(here, picked, found[c])
            for c in range(3):
                value = slot_block_ref[c, 0, g * 8 : (g + 1) * 8, h * half : (h + 1) * half] * found[0]
                for d in range(1, 3):
                    value = value + (
                        slot_block_ref[c, d, g * 8 : (g + 1) * 8, h * half : (h + 1) * half] * found[d]
                    )
                for i in range(8):
                    slot = g * 8 + i
                    peer, at = slot // per_peer, slot % per_peer
                    start = (c * per_peer + at) * width + h * half
                    sent_ref[peer, 0:1, start : start + half] = value[i : i + 1]
    base = 3 * per_peer * width
    many = 3 * layers
    if not first:
        sums = edge_ref[0, 6 * rows : 6 * rows + 1, 0:half]
        for section in range(1, sections):
            sums = sums + edge_ref[section, 6 * rows : 6 * rows + 1, 0:half]
    for peer in range(peers):
        side = jnp.where(peer > a, 1, 0)
        for i in range(many):
            start = base + i * width
            sent_ref[peer, 0:1, start : start + width] = borders[side, i : i + 1]
        start = base + many * width
        if not first:
            sent_ref[peer, 0:1, start : start + half] = sums
        else:
            for i in range(per_peer):
                at = peer * per_peer + i
                sent_ref[peer, 0:1, start + i * width : start + (i + 1) * width] = slot_target_ref[
                    at : at + 1
                ]


def weights_of(sums, upto):
    value = lambda step, at: sums[step : step + 1, at : at + 1]
    squared = value(0, 0)
    beta = jnp.sqrt(squared + TINY)
    unscale = 1.0 / beta
    gram = [[squared * unscale * unscale]]
    columns = []
    lengths = []
    for step in range(upto):
        if step == 0:
            weights = [value(0, 1) * unscale * unscale]
            own = value(0, 2) * unscale * unscale
        else:
            weights = [value(step, i) for i in range(step + 1)]
            own = value(step, step + 1)
        size = step + 1
        shadow = []
        for i in range(size):
            total = weights[0] * gram[i][0]
            for k in range(1, size):
                total = total + weights[k] * gram[i][k]
            shadow.append(total)
        left = own
        for i in range(size):
            left = left - weights[i] * (2.0 * weights[i] - shadow[i])
        left = jnp.maximum(left, 0.0)
        length = jnp.sqrt(left + TINY)
        inverse = 1.0 / length
        column = [(weights[i] - shadow[i]) * inverse for i in range(size)]
        for i in range(size):
            gram[i].append(column[i])
        gram.append(column + [left * inverse * inverse])
        columns.append(weights)
        lengths.append(length)
    return beta, unscale, columns, lengths


def operate_kernel(step, *refs):
    last = step == ITERS - 1
    (got_ref, target_ref, solved_ref, layer_ref, diag_ref, coupling_ref, active_ref) = refs[:7]
    at = 7
    if not last:
        pivot_ref, lower_ref, upper_ref = refs[at : at + 3]
        at += 3
    right_ref = refs[at]
    at += 1
    if step > 0:
        sums_ref = refs[at]
        at += 1
        earlier = []
        for i in range(step):
            earlier.append(refs[at : at + (2 if i == 0 else 3)])
            at += len(earlier[-1])
    outs = refs[at:]
    layers, rows, width = solved_ref.shape[1:]
    peers = got_ref.shape[0]
    per_peer = layers * rows // peers
    base = 3 * per_peer * width
    many = 3 * layers
    ending = base + many * width
    cells = layers * rows
    a = lax.axis_index("areal")
    total_ref = outs[-1]
    outs = outs[:-1]

    row_number = lax.broadcasted_iota(jnp.int32, (cells, width), 0)
    column_number = lax.broadcasted_iota(jnp.int32, (width, width), 0)
    total_ref[...] = jnp.zeros(total_ref.shape, F32)

    def from_peer(peer, carry):
        lefts, rights = [], []
        for i in range(per_peer):
            where = target_ref[
                peer, 0:1, ending + i * width : ending + (i + 1) * width
            ].astype(jnp.int32)
            in_row = row_number == where // width
            rights.append(jnp.where(column_number == where % width, 1.0, 0.0).astype(BF16))
            pieces = []
            for c in range(3):
                start = (c * per_peer + i) * width
                rest = got_ref[peer, 0:1, start : start + width]
                for part in range(PARTS):
                    piece = rest.astype(BF16).astype(F32)
                    rest = rest - piece
                    pieces.append(jnp.where(in_row, piece, 0.0).astype(BF16))
            lefts.append(jnp.concatenate(pieces, axis=0))
        left = jnp.concatenate(lefts, axis=1)
        right = jnp.concatenate(rights, axis=1)
        total_ref[...] += lax.dot_general(
            left, right, (((1,), (1,)), ((), ())), preferred_element_type=F32
        )
        return carry

    lax.fori_loop(0, peers, from_peer, 0)

    active = [wide(active_ref[k]) for k in range(layers)]
    held = [[solved_ref[c, k] * active[k] for c in range(3)] for k in range(layers)]
    row_at = lax.broadcasted_iota(jnp.int32, (rows, width), 0)
    column_at = lax.broadcasted_iota(jnp.int32, (rows, width), 1)
    before, after = jnp.maximum(a - 1, 0), jnp.minimum(a + 1, peers - 1)
    has_before = jnp.where(a > 0, 1.0, 0.0)
    has_after = jnp.where(a < peers - 1, 1.0, 0.0)
    applied = []
    for k in range(layers):
        beside = []
        beside.append(held[k - 1] if k > 0 else [layer_ref[0, c] for c in range(3)])
        beside.append(held[k + 1] if k < layers - 1 else [layer_ref[1, c] for c in range(3)])
        sides = [[], [], [], []]
        for c in range(3):
            border = base + (c * layers + k) * width
            low = got_ref[before, 0:1, border : border + width] * has_before
            high = got_ref[after, 0:1, border : border + width] * has_after
            value = held[k][c]
            sides[0].append(jnp.where(row_at == 0, low, pltpu.roll(value, 1, 0)))
            sides[1].append(jnp.where(row_at == rows - 1, high, pltpu.roll(value, rows - 1, 0)))
            sides[2].append(jnp.where(column_at == 0, 0.0, pltpu.roll(value, 1, 1)))
            sides[3].append(jnp.where(column_at == width - 1, 0.0, pltpu.roll(value, width - 1, 1)))
        result = times(block_at(diag_ref, k), held[k])
        for d, neighbour in enumerate(beside + sides):
            blocks = [[wide(coupling_ref[d, i, j, k]) for j in range(3)] for i in range(3)]
            result = plus(result, times(blocks, neighbour))
        for c in range(3):
            for part in range(PARTS):
                start = (c * PARTS + part) * cells + k * rows
                result[c] = result[c] + total_ref[start : start + rows]
        applied.append(
            [
                active[k] * result[c] + (1.0 - active[k]) * solved_ref[c, k]
                for c in range(3)
            ]
        )

    pairs = []
    if step == 0:
        (applied_ref, edge_ref, alone_ref) = outs
        for k in range(layers):
            for c in range(3):
                applied_ref[c, k] = applied[k][c]
        new = applied
        r = [[right_ref[c, k] for c in range(3)] for k in range(layers)]
        pairs = [(r, r), (r, applied), (applied, applied)]
    else:
        if last:
            (v_ref, z_ref, edge_ref, history_ref) = outs
        else:
            (v_ref, z_ref, w_ref, edge_ref, alone_ref, history_ref) = outs
        fresh = got_ref[0, 0:1, ending : ending + 128]
        for peer in range(1, peers):
            fresh = fresh + got_ref[peer, 0:1, ending : ending + 128]
        history_row = lax.broadcasted_iota(jnp.int32, history_ref.shape, 0)
        sums = jnp.where(history_row == step - 1, fresh, sums_ref[...])
        history_ref[...] = sums
        beta, unscale, columns, lengths = weights_of(sums, step)
        weights = columns[-1]
        inverse = 1.0 / lengths[-1]
        spread = lambda value: jnp.broadcast_to(value, (rows, width))
        lead = spread(inverse * unscale if step == 1 else inverse)
        factors = [spread(weights[i] * inverse * (unscale if i == 0 else 1.0)) for i in range(step)]
        new = []
        members = []
        v_all = [[] for _ in range(step)]
        for k in range(layers):
            new.append([])
            members.append([])
            for c in range(3):
                old_v = [right_ref[c, k]] + [earlier[i][0][c, k] for i in range(1, step)]
                old_z = [earlier[0][0][c, k]] + [earlier[i][1][c, k] for i in range(1, step)]
                old_w = [earlier[0][1][c, k]] + [earlier[i][2][c, k] for i in range(1, step)]
                v = old_w[-1] * lead
                z = solved_ref[c, k] * lead
                w = applied[k][c] * lead
                for i in range(step):
                    v = v - factors[i] * old_v[i]
                    z = z - factors[i] * old_z[i]
                    w = w - factors[i] * old_w[i]
                v_ref[c, k] = v
                z_ref[c, k] = z
                if not last:
                    w_ref[c, k] = w
                new[k].append(w)
                members[k].append(v)
        first = spread(unscale)
        basis = [[[right_ref[c, k] * first for c in range(3)] for k in range(layers)]]
        for i in range(1, step):
            basis.append([[earlier[i][0][c, k] for c in range(3)] for k in range(layers)])
        basis.append(members)
        pairs = [(member, new) for member in basis] + [(new, new)]

    edge_ref[...] = jnp.zeros(edge_ref.shape, F32)
    lane = lax.broadcasted_iota(jnp.int32, (1, 128), 1)
    line = jnp.zeros((1, 128), F32)
    for number, (left, right) in enumerate(pairs):
        total = jnp.zeros((rows, width), F32)
        for k in range(layers):
            for c in range(3):
                total = total + left[k][c] * right[k][c]
        total = jnp.sum(jnp.sum(total, axis=0, keepdims=True), axis=1, keepdims=True)
        line = jnp.where(lane == number, total, line)
    if last:
        for peer in range(edge_ref.shape[0]):
            edge_ref[peer] = line
    else:
        edge_ref[6 * rows : 6 * rows + 1, 0:128] = line
        lowest, alone = local_sweeps(new, pivot_ref, lower_ref, upper_ref, layers)
        for c in range(3):
            edge_ref[c * rows : (c + 1) * rows] = lowest[c]
            edge_ref[(3 + c) * rows : (4 + c) * rows] = alone[0][c]
            for k in range(layers):
                alone_ref[c, k] = alone[k][c]


def finish_kernel(dots_ref, sums_ref, z0_ref, z1_ref, z2_ref, z3_ref, update_ref, hessenberg_ref):
    z_refs = (z0_ref, z1_ref, z2_ref, z3_ref)
    rows, width = z0_ref.shape[2:]
    fresh = dots_ref[0]
    for peer in range(1, dots_ref.shape[0]):
        fresh = fresh + dots_ref[peer]
    history_row = lax.broadcasted_iota(jnp.int32, sums_ref.shape, 0)
    sums = jnp.where(history_row == ITERS - 1, fresh, sums_ref[...])
    beta, unscale, columns, lengths = weights_of(sums, ITERS)
    shape = hessenberg_ref.shape
    row_at = lax.broadcasted_iota(jnp.int32, shape, 0)
    column_at = lax.broadcasted_iota(jnp.int32, shape, 1)
    table = jnp.zeros(shape, F32)
    for j in range(ITERS):
        for i, weight in enumerate(columns[j] + [lengths[j]]):
            table = jnp.where((row_at == i) & (column_at == j), weight, table)
    hessenberg_ref[...] = table
    goal = [beta]
    triangle = []
    rotations = []
    for j in range(ITERS):
        entries = list(columns[j])
        for i, (cosine, sine) in enumerate(rotations):
            upper, lower = entries[i], entries[i + 1]
            entries[i] = cosine * upper + sine * lower
            entries[i + 1] = cosine * lower - sine * upper
        radius = jnp.sqrt(entries[j] * entries[j] + lengths[j] * lengths[j])
        cosine, sine = entries[j] / radius, lengths[j] / radius
        rotations.append((cosine, sine))
        entries[j] = radius
        triangle.append(entries)
        leading = goal[j]
        goal[j] = cosine * leading
        goal.append(-sine * leading)
    answer = [None] * ITERS
    for i in range(ITERS - 1, -1, -1):
        partial = goal[i]
        for j in range(i + 1, ITERS):
            partial = partial - triangle[j][i] * answer[j]
        answer[i] = partial / triangle[i][i]
    factors = [
        jnp.broadcast_to(answer[j] * unscale if j == 0 else answer[j], (rows, width))
        for j in range(ITERS)
    ]
    for c in range(3):
        for k in range(z0_ref.shape[1]):
            value = factors[0] * z_refs[0][c, k]
            for j in range(1, ITERS):
                value = value + factors[j] * z_refs[j][c, k]
            update_ref[c, k] = value


def turn(array, by):
    count = lax.axis_size("layer")
    return lax.ppermute(array, "layer", [(i, (i + by) % count) for i in range(count)])


def shape_of(*dims, kind=F32):
    return jax.ShapeDtypeStruct(dims, kind)


def local(
    right_side,
    diag_blocks,
    couplings,
    pivot_inverse,
    lower_blocks,
    upper_blocks,
    active_cells,
    link_from,
    link_owner,
    link_target,
    link_blocks,
):
    _, layers, rows, width = right_side.shape
    peers = lax.axis_size("areal")
    sections = lax.axis_size("layer")
    links = link_from.shape[1]
    capacity = 2 * links // peers
    slots = capacity * peers // width
    per_peer = slots // peers
    link_rows = links // width
    field = shape_of(3, layers, rows, width)
    edge_rows = 7 * rows
    sent_width = (3 * per_peer + 3 * layers) * width + 128
    first_width = (4 * per_peer + 3 * layers) * width
    edge_shape = shape_of(edge_rows, width)
    hbm = pl.BlockSpec(memory_space=pltpu.HBM)
    operands = [
        right_side,
        pivot_inverse,
        lower_blocks,
        upper_blocks,
        active_cells,
        link_from,
        link_owner.reshape(1, links),
        link_target,
        link_blocks.reshape(3, 3, links),
    ]
    (
        edge, following, alone, from_above, from_below, matrices,
        slot_block, slot_source, slot_target,
    ) = call(
        functools.partial(setup_kernel, peers),
        [
            edge_shape,
            shape_of(16 * rows, width),
            field,
            shape_of(3, 3, layers, rows, width),
            shape_of(3, 3, layers, rows, width),
            shape_of(27 * rows, width),
            shape_of(3, 3, slots, width),
            shape_of(slots, width, kind=jnp.int32),
            shape_of(slots, width),
        ],
        [pltpu.VMEM(operand.shape, operand.dtype) for operand in operands]
        + [
            pltpu.VMEM((peers * link_rows, width), BF16),
            pltpu.VMEM((13 * slots, width), F32),
            pltpu.VMEM((3, link_rows, width), jnp.int32),
            pltpu.SemaphoreType.DMA((len(operands),)),
        ],
        name="setup",
        inputs=[hbm] * len(operands),
    )(*operands)
    turned = [turn(following, 1)] + [turn(edge, by) for by in range(2, sections)]
    all_matrices = lax.all_gather(matrices, "layer", axis=0, tiled=False)

    target = None
    sums = jnp.zeros((8, 128), F32)
    earlier = []
    zs = []
    for step in range(ITERS):
        last = step == ITERS - 1
        scratch = [
            pltpu.VMEM((sections, 3, rows, width), F32),
            pltpu.VMEM((sections, 3, rows, width), F32),
            pltpu.VMEM((2, 16, width), F32),
            pltpu.VMEM((3, layers * rows, width), F32),
        ]
        if step == 0:
            edges = edge
            scratch.append(pltpu.VMEM((sections, 6 * rows, width), F32))
        else:
            edges = lax.all_gather(edge, "layer", axis=0, tiled=False)
        solved, layer_sides, sent = call(
            functools.partial(couple_kernel, step == 0, sections),
            [
                field,
                shape_of(2, 3, rows, width),
                shape_of(peers, 1, first_width if step == 0 else sent_width),
            ],
            scratch,
            name="couple",
        )(
            *turned, edges, all_matrices, alone, from_above, from_below, active_cells,
            slot_block, slot_source, slot_target,
        )
        got = lax.all_to_all(sent, "areal", split_axis=0, concat_axis=0, tiled=True)
        if step == 0:
            target = got
        operands = [got, target, solved, layer_sides, diag_blocks, couplings, active_cells]
        if not last:
            operands += [pivot_inverse, lower_blocks, upper_blocks]
        operands.append(right_side)
        if step > 0:
            operands.append(sums)
            for group in earlier:
                operands += list(group)
        history = shape_of(8, 128)
        if step == 0:
            outs = [field, edge_shape, field]
        elif last:
            outs = [field, field, shape_of(peers * sections, 1, 128), history]
        else:
            outs = [field, field, field, edge_shape, field, history]
        results = call(
            functools.partial(operate_kernel, step),
            outs,
            [
                pltpu.VMEM((3 * PARTS * layers * rows, width), F32),
            ],
            name="operate",
        )(*operands)
        if step == 0:
            applied, edge, alone = results
            earlier.append((solved, applied))
            zs.append(solved)
        elif last:
            _, z, dots, sums = results
            zs.append(z)
        else:
            v, z, w, edge, alone, sums = results
            earlier.append((v, z, w))
            zs.append(z)
    dots = lax.all_to_all(dots, ("areal", "layer"), split_axis=0, concat_axis=0, tiled=True)
    update, hessenberg = call(
        finish_kernel, [field, shape_of(ITERS + 1, ITERS)], name="finish"
    )(dots, sums, *zs)
    return update, hessenberg


def solution(mesh):
    placed = (
        P(None, "layer", "areal", None),
        P(None, None, "layer", "areal", None),
        P(None, None, None, "layer", "areal", None),
        P(None, None, "layer", "areal", None),
        P(None, None, "layer", "areal", None),
        P(None, None, "layer", "areal", None),
        P("layer", "areal", None),
        P("layer", "areal"),
        P("layer", "areal", None),
        P("layer", "areal"),
        P(None, None, "layer", "areal"),
    )
    return jax.shard_map(
        local,
        mesh=mesh,
        in_specs=placed,
        out_specs=(P(None, "layer", "areal", None), P()),
        check_vma=False,
    )
```

```python
import functools

import jax
import jax.numpy as jnp
from jax import lax
from jax.experimental import pallas as pl
from jax.experimental.pallas import tpu as pltpu
from jax.sharding import PartitionSpec as P

ITERS = 4
PARTS = 3
TINY = 1e-06

F32 = jnp.float32
BF16 = jnp.bfloat16
VMEM = pl.BlockSpec(memory_space=pltpu.VMEM)


def call(kernel, outs, scratch=(), name=None, inputs=None, limit=20, flops=1 << 22, moved=1 << 20):
    many = isinstance(outs, (list, tuple))
    where = {} if inputs is None else {"in_specs": inputs}
    return pl.pallas_call(
        kernel,
        out_shape=outs,
        **where,
        out_specs=[VMEM] * len(outs) if many else VMEM,
        scratch_shapes=list(scratch),
        compiler_params=pltpu.CompilerParams(vmem_limit_bytes=limit << 20),
        cost_estimate=pl.CostEstimate(flops=flops, bytes_accessed=moved, transcendentals=0),
        name=name,
    )


def wide(value):
    return value.astype(F32)


def times(blocks, vector):
    result = []
    for row in blocks:
        total = row[0] * vector[0]
        for entry, element in zip(row[1:], vector[1:]):
            total = total + entry * element
        result.append(total)
    return result


def block_at(ref, layer):
    return [[wide(ref[c, d, layer]) for d in range(3)] for c in range(3)]


def minus(left, right):
    return [a - b for a, b in zip(left, right)]


def plus(left, right):
    return [a + b for a, b in zip(left, right)]


def local_sweeps(planes, pivot, lower, upper, layers):
    forward = []
    previous = None
    for k in range(layers):
        current = times(block_at(pivot, k), planes[k])
        if previous is not None:
            current = minus(current, times(block_at(lower, k), previous))
        forward.append(current)
        previous = current
    backward = [None] * layers
    previous = None
    for k in range(layers - 1, -1, -1):
        current = forward[k]
        if previous is not None:
            current = minus(current, times(block_at(upper, k), previous))
        backward[k] = current
        previous = current
    return forward[layers - 1], backward


def section_part(
    right_ref, pivot_ref, lower_ref, upper_ref, active_ref,
    edge_ref, next_ref, alone_ref, from_above_ref, from_below_ref, matrix_ref,
):
    layers, rows = right_ref.shape[1], right_ref.shape[2]
    planes = [[right_ref[c, k] for c in range(3)] for k in range(layers)]
    lowest, solved = local_sweeps(planes, pivot_ref, lower_ref, upper_ref, layers)
    for c in range(3):
        for ref in (edge_ref, next_ref):
            ref[c * rows : (c + 1) * rows] = lowest[c]
            ref[(3 + c) * rows : (4 + c) * rows] = solved[0][c]
        for k in range(layers):
            alone_ref[c, k] = solved[k][c]
    for d in range(3):
        carried = []
        previous = None
        for k in range(layers):
            blocks = block_at(lower_ref, k)
            if previous is None:
                previous = [-blocks[c][d] for c in range(3)]
            else:
                previous = [-value for value in times(blocks, previous)]
            carried.append(previous)
        for c in range(3):
            matrix_ref[(c * 3 + d) * rows : (c * 3 + d + 1) * rows] = carried[-1][c]
        response = carried[-1]
        for k in range(layers - 1, -1, -1):
            if k < layers - 1:
                response = minus(carried[k], times(block_at(upper_ref, k), response))
            for c in range(3):
                from_above_ref[c, d, k] = response[c]
        for c in range(3):
            matrix_ref[(9 + c * 3 + d) * rows : (10 + c * 3 + d) * rows] = response[c]
        response = None
        for k in range(layers - 1, -1, -1):
            blocks = block_at(upper_ref, k)
            if response is None:
                for c in range(3):
                    next_ref[(6 + c * 3 + d) * rows : (7 + c * 3 + d) * rows] = blocks[c][d]
                response = [-blocks[c][d] for c in range(3)]
            else:
                response = [-value for value in times(blocks, response)]
            for c in range(3):
                from_below_ref[c, d, k] = response[c]
        for c in range(3):
            matrix_ref[(18 + c * 3 + d) * rows : (19 + c * 3 + d) * rows] = response[c]
    edge_ref[6 * rows : 7 * rows] = wide(active_ref[0])
    next_ref[15 * rows : 16 * rows] = wide(active_ref[layers - 1])


def routing_part(
    peers, folded, block_ref, slot_block_ref, slot_source_ref, slot_target_ref, stacked, products
):
    rows, width = folded.shape[1:]
    slots = slot_source_ref.shape[0]
    per_peer = slots // peers
    owner = folded[1]
    for o in range(peers):
        stacked[o * rows : (o + 1) * rows] = jnp.where(owner == o, 1.0, 0.0).astype(BF16)
    chosen = stacked[...]
    ones_before = jnp.where(
        lax.broadcasted_iota(jnp.int32, (width, width), 0)
        < lax.broadcasted_iota(jnp.int32, (width, width), 1),
        1.0,
        0.0,
    ).astype(BF16)
    within = jnp.dot(chosen, ones_before, preferred_element_type=F32)
    totals = jnp.dot(chosen, jnp.ones((width, width), BF16), preferred_element_type=F32)
    row_before = jnp.where(
        lax.broadcasted_iota(jnp.int32, (rows, rows), 1)
        < lax.broadcasted_iota(jnp.int32, (rows, rows), 0),
        1.0,
        0.0,
    ).astype(BF16)
    rank = jnp.zeros((rows, width), F32)
    for o in range(peers):
        part = slice(o * rows, (o + 1) * rows)
        before = jnp.dot(row_before, totals[part].astype(BF16), preferred_element_type=F32)
        rank = rank + jnp.where(owner == o, within[part] + before, 0.0)
    rank = rank.astype(jnp.int32)
    slot_row = owner * per_peer + rank // width
    slot_column = rank % width
    source = folded[0]
    target = folded[2]
    payloads = [
        wide(source // width),
        wide(source % width),
        wide(target // width),
        wide(target % width),
    ]
    row_number = lax.broadcasted_iota(jnp.int32, (slots, width), 0)
    column_number = lax.broadcasted_iota(jnp.int32, (width, width), 0)
    total = jnp.zeros(products.shape, F32)
    for r in range(rows):
        in_row = row_number == slot_row[r : r + 1]
        left = jnp.concatenate(
            [
                jnp.where(in_row, payload, 0.0).astype(BF16)
                for payload in [payload[r : r + 1] for payload in payloads]
                + [
                    wide(block_ref[c, d : d + 1, r * width : (r + 1) * width])
                    for c in range(3)
                    for d in range(3)
                ]
            ],
            axis=0,
        )
        right = jnp.where(column_number == slot_column[r : r + 1], 1.0, 0.0).astype(BF16)
        total = total + lax.dot_general(
            left, right, (((1,), (1,)), ((), ())), preferred_element_type=F32
        )
    products[...] = total
    slot_source_ref[...] = (products[0:slots] * width + products[slots : 2 * slots]).astype(jnp.int32)
    slot_target_ref[...] = products[2 * slots : 3 * slots] * width + products[3 * slots : 4 * slots]
    for c in range(3):
        for d in range(3):
            at = 4 + c * 3 + d
            slot_block_ref[c, d] = products[at * slots : (at + 1) * slots]


def setup_kernel(
    peers,
    right_hbm, pivot_hbm, lower_hbm, upper_hbm, active_hbm,
    from_hbm, owner_hbm, target_hbm, block_hbm,
    edge_ref, next_ref, alone_ref, from_above_ref, from_below_ref, matrix_ref,
    slot_block_ref, slot_source_ref, slot_target_ref,
    right_ref, pivot_ref, lower_ref, upper_ref, active_ref,
    from_ref, owner_ref, target_ref, block_ref,
    stacked, products, folded, semaphores,
):
    copies = [
        pltpu.make_async_copy(source, landing, semaphores.at[number])
        for number, (source, landing) in enumerate(
            [
                (lower_hbm, lower_ref),
                (upper_hbm, upper_ref),
                (active_hbm, active_ref),
                (pivot_hbm, pivot_ref),
                (right_hbm, right_ref),
                (owner_hbm, owner_ref),
                (from_hbm, from_ref),
                (target_hbm, target_ref),
                (block_hbm, block_ref),
            ]
        )
    ]
    for copy in copies:
        copy.start()
    for copy in copies:
        copy.wait()
    section_part(
        right_ref, pivot_ref, lower_ref, upper_ref, active_ref,
        edge_ref, next_ref, alone_ref, from_above_ref, from_below_ref, matrix_ref,
    )
    rows, width = folded.shape[1:]
    for r in range(rows):
        for number, ref in enumerate((from_ref, owner_ref, target_ref)):
            folded[number, r : r + 1] = ref[0:1, r * width : (r + 1) * width]
    routing_part(
        peers, folded, block_ref, slot_block_ref, slot_source_ref, slot_target_ref, stacked, products
    )


def couple_kernel(
    first, sections, *refs,
):
    turned, refs = refs[: sections - 1], refs[sections - 1 :]
    if first:
        own_ref, refs = refs[0], refs[1:]
        edge_ref = refs[-1]
        refs = refs[:-1]
    else:
        edge_ref, refs = refs[0], refs[1:]
    (
        matrix_ref, alone_ref, above_ref, below_ref, active_ref,
        slot_block_ref, slot_source_ref, slot_target_ref,
        solved_ref, layer_ref, sent_ref, arriving, tops, borders, table,
    ) = refs
    layers, rows = alone_ref.shape[1], alone_ref.shape[2]
    width = alone_ref.shape[3]
    peers = sent_ref.shape[0]
    slots = slot_source_ref.shape[0]
    per_peer = slots // peers
    s = lax.axis_index("layer")
    a = lax.axis_index("areal")
    if first:
        edge_ref[s] = own_ref[0 : 6 * rows]
        for turn in range(1, sections):
            edge_ref[lax.rem(s - turn + sections, sections)] = turned[turn - 1][0 : 6 * rows]

    def matrix(section, which):
        return [
            [
                matrix_ref[section, (which * 9 + c * 3 + d) * rows : (which * 9 + c * 3 + d + 1) * rows]
                for d in range(3)
            ]
            for c in range(3)
        ]

    def edge(section, which):
        return [
            edge_ref[section, (which * 3 + c) * rows : (which * 3 + c + 1) * rows] for c in range(3)
        ]

    zero = jnp.zeros((rows, width), F32)
    coming = [[zero] * 3]
    for section in range(1, sections):
        value = edge(section - 1, 0)
        if section > 1:
            value = plus(value, times(matrix(section - 1, 0), coming[section - 1]))
        coming.append(value)
    rising = [None] * sections + [[zero] * 3]
    for section in range(sections - 1, 0, -1):
        value = plus(edge(section, 1), times(matrix(section, 1), coming[section]))
        if section < sections - 1:
            value = plus(value, times(matrix(section, 2), rising[section + 1]))
        rising[section] = value
    rising[0] = [zero] * 3
    for section in range(sections):
        for c in range(3):
            arriving[section, c] = coming[section][c]
            tops[section, c] = rising[section + 1][c]
    above = [arriving[s, c] for c in range(3)]
    below = [tops[s, c] for c in range(3)]
    active = [wide(active_ref[k]) for k in range(layers)]
    for k in range(layers):
        for c in range(3):
            value = alone_ref[c, k]
            for d in range(3):
                value = value + above_ref[c, d, k] * above[d] + below_ref[c, d, k] * below[d]
            solved_ref[c, k] = value
            held = value * active[k]
            table[c, k * rows : (k + 1) * rows] = held
            borders[0, c * layers + k : c * layers + k + 1] = held[0:1]
            borders[1, c * layers + k : c * layers + k + 1] = held[rows - 1 : rows]
    previous, following = turned[0], turned[-1]
    bottom = [
        [previous[(6 + c * 3 + d) * rows : (7 + c * 3 + d) * rows] for d in range(3)]
        for c in range(3)
    ]
    own_top = [solved_ref[c, 0] for c in range(3)]
    upstairs = minus(above, times(bottom, own_top))
    upper_active = jnp.where(s > 0, previous[15 * rows : 16 * rows], 0.0)
    lower_active = jnp.where(s < sections - 1, following[6 * rows : 7 * rows], 0.0)
    for c in range(3):
        layer_ref[0, c] = upstairs[c] * upper_active
        layer_ref[1, c] = below[c] * lower_active
    half = 128
    groups = [(g, h) for g in range(slots // 8) for h in range(width // half)]
    for g in range(slots // 8):
        for h in range(width // half):
            source = slot_source_ref[g * 8 : (g + 1) * 8, h * half : (h + 1) * half]
            line = source // half
            lane = source % half
            found = [jnp.zeros((8, half), F32)] * 3
            for r in range(layers * rows):
                for q in range(width // half):
                    here = line == r * (width // half) + q
                    for c in range(3):
                        row = jnp.broadcast_to(
                            table[c, r : r + 1, q * half : (q + 1) * half], (8, half)
                        )
                        picked = jnp.take_along_axis(row, lane, axis=1)
                        found[c] = jnp.where(here, picked, found[c])
            for c in range(3):
                value = slot_block_ref[c, 0, g * 8 : (g + 1) * 8, h * half : (h + 1) * half] * found[0]
                for d in range(1, 3):
                    value = value + (
                        slot_block_ref[c, d, g * 8 : (g + 1) * 8, h * half : (h + 1) * half] * found[d]
                    )
                for i in range(8):
                    slot = g * 8 + i
                    peer, at = slot // per_peer, slot % per_peer
                    start = (c * per_peer + at) * width + h * half
                    sent_ref[peer, 0:1, start : start + half] = value[i : i + 1]
    base = 3 * per_peer * width
    many = 3 * layers
    if not first:
        sums = edge_ref[0, 6 * rows : 6 * rows + 1, 0:half]
        for section in range(1, sections):
            sums = sums + edge_ref[section, 6 * rows : 6 * rows + 1, 0:half]
    for peer in range(peers):
        side = jnp.where(peer > a, 1, 0)
        for i in range(many):
            start = base + i * width
            sent_ref[peer, 0:1, start : start + width] = borders[side, i : i + 1]
        start = base + many * width
        if not first:
            sent_ref[peer, 0:1, start : start + half] = sums
        else:
            for i in range(per_peer):
                at = peer * per_peer + i
                sent_ref[peer, 0:1, start + i * width : start + (i + 1) * width] = slot_target_ref[
                    at : at + 1
                ]


def weights_of(sums, upto):
    def value(step, at):
        row = jnp.broadcast_to(sums[step : step + 1], (8, 128))
        return jnp.take_along_axis(row, jnp.full((8, 128), at, jnp.int32), axis=1)

    squared = value(0, 0)
    beta = jnp.sqrt(squared + TINY)
    unscale = 1.0 / beta
    gram = [[squared * unscale * unscale]]
    columns = []
    lengths = []
    for step in range(upto):
        if step == 0:
            weights = [value(0, 1) * unscale * unscale]
            own = value(0, 2) * unscale * unscale
        else:
            weights = [value(step, i) for i in range(step + 1)]
            own = value(step, step + 1)
        size = step + 1
        shadow = []
        for i in range(size):
            total = weights[0] * gram[i][0]
            for k in range(1, size):
                total = total + weights[k] * gram[i][k]
            shadow.append(total)
        left = own
        for i in range(size):
            left = left - weights[i] * (2.0 * weights[i] - shadow[i])
        left = jnp.maximum(left, 0.0)
        length = jnp.sqrt(left + TINY)
        inverse = 1.0 / length
        column = [(weights[i] - shadow[i]) * inverse for i in range(size)]
        for i in range(size):
            gram[i].append(column[i])
        gram.append(column + [left * inverse * inverse])
        columns.append(weights)
        lengths.append(length)
    return beta, unscale, columns, lengths


def operate_kernel(step, *refs):
    last = step == ITERS - 1
    got_ref, solved_ref, layer_ref, diag_ref, coupling_ref, active_ref = refs[:6]
    at = 6
    if step > 0:
        hot_row_ref, hot_column_ref = refs[6:8]
        at = 8
    if not last:
        pivot_ref, lower_ref, upper_ref = refs[at : at + 3]
        at += 3
    right_ref = refs[at]
    at += 1
    if step > 0:
        sums_ref = refs[at]
        at += 1
        earlier = []
        for i in range(step):
            earlier.append(refs[at : at + (2 if i == 0 else 3)])
            at += len(earlier[-1])
    outs = refs[at:]
    layers, rows, width = solved_ref.shape[1:]
    peers = got_ref.shape[0]
    per_peer = layers * rows // peers
    base = 3 * per_peer * width
    many = 3 * layers
    ending = base + many * width
    cells = layers * rows
    a = lax.axis_index("areal")
    total_ref = outs[-1]
    outs = outs[:-1]
    if step == 0:
        lines_ref = outs[-1]
        hot_row_ref, hot_column_ref = outs[-3:-1]
        outs = outs[:-3]

    capacity = per_peer * width
    if step == 0:
        for peer in range(peers):
            for i in range(per_peer):
                at = peer * per_peer + i
                lines_ref[at : at + 1] = got_ref[
                    peer, 0:1, ending + i * width : ending + (i + 1) * width
                ]
        where = lines_ref[...].astype(jnp.int32)
        upright = jnp.transpose(wide(where % width))
        upper = where // width
        row_number = lax.broadcasted_iota(jnp.int32, (cells, width), 0)
        column_number = wide(lax.broadcasted_iota(jnp.int32, (width, width), 1))
        for peer in range(peers):
            for i in range(per_peer):
                at = peer * per_peer + i
                hot_column_ref[peer, i * width : (i + 1) * width] = jnp.where(
                    column_number == upright[:, at : at + 1], 1.0, 0.0
                ).astype(BF16)
                hot_row_ref[peer, :, i * width : (i + 1) * width] = jnp.where(
                    row_number == upper[at : at + 1], 1.0, 0.0
                ).astype(BF16)
    total_ref[...] = jnp.zeros(total_ref.shape, F32)

    def from_peer(peer, carry):
        hot = hot_row_ref[peer]
        pieces = []
        for c in range(3):
            rest = got_ref[peer, 0:1, c * capacity : (c + 1) * capacity]
            for part in range(PARTS):
                piece = rest.astype(BF16)
                rest = rest - wide(piece)
                pieces.append(hot * jnp.broadcast_to(piece, hot.shape))
        total_ref[...] += jnp.dot(
            jnp.concatenate(pieces, axis=0), hot_column_ref[peer], preferred_element_type=F32
        )
        return carry

    lax.fori_loop(0, peers, from_peer, 0)

    active = [wide(active_ref[k]) for k in range(layers)]
    held = [[solved_ref[c, k] * active[k] for c in range(3)] for k in range(layers)]
    row_at = lax.broadcasted_iota(jnp.int32, (rows, width), 0)
    column_at = lax.broadcasted_iota(jnp.int32, (rows, width), 1)
    before, after = jnp.maximum(a - 1, 0), jnp.minimum(a + 1, peers - 1)
    has_before = jnp.where(a > 0, 1.0, 0.0)
    has_after = jnp.where(a < peers - 1, 1.0, 0.0)
    applied = []
    for k in range(layers):
        beside = []
        beside.append(held[k - 1] if k > 0 else [layer_ref[0, c] for c in range(3)])
        beside.append(held[k + 1] if k < layers - 1 else [layer_ref[1, c] for c in range(3)])
        sides = [[], [], [], []]
        for c in range(3):
            border = base + (c * layers + k) * width
            low = got_ref[before, 0:1, border : border + width] * has_before
            high = got_ref[after, 0:1, border : border + width] * has_after
            value = held[k][c]
            sides[0].append(jnp.where(row_at == 0, low, pltpu.roll(value, 1, 0)))
            sides[1].append(jnp.where(row_at == rows - 1, high, pltpu.roll(value, rows - 1, 0)))
            sides[2].append(jnp.where(column_at == 0, 0.0, pltpu.roll(value, 1, 1)))
            sides[3].append(jnp.where(column_at == width - 1, 0.0, pltpu.roll(value, width - 1, 1)))
        result = times(block_at(diag_ref, k), held[k])
        for d, neighbour in enumerate(beside + sides):
            blocks = [[wide(coupling_ref[d, i, j, k]) for j in range(3)] for i in range(3)]
            result = plus(result, times(blocks, neighbour))
        for c in range(3):
            for part in range(PARTS):
                start = (c * PARTS + part) * cells + k * rows
                result[c] = result[c] + total_ref[start : start + rows]
        applied.append(
            [
                active[k] * result[c] + (1.0 - active[k]) * solved_ref[c, k]
                for c in range(3)
            ]
        )

    pairs = []
    if step == 0:
        (applied_ref, edge_ref, alone_ref) = outs
        for k in range(layers):
            for c in range(3):
                applied_ref[c, k] = applied[k][c]
        new = applied
        r = [[right_ref[c, k] for c in range(3)] for k in range(layers)]
        pairs = [(r, r), (r, applied), (applied, applied)]
    else:
        if last:
            (v_ref, z_ref, edge_ref, history_ref) = outs
        else:
            (v_ref, z_ref, w_ref, edge_ref, alone_ref, history_ref) = outs
        fresh = got_ref[0, 0:1, ending : ending + 128]
        for peer in range(1, peers):
            fresh = fresh + got_ref[peer, 0:1, ending : ending + 128]
        history_row = lax.broadcasted_iota(jnp.int32, history_ref.shape, 0)
        sums = jnp.where(history_row == step - 1, fresh, sums_ref[...])
        history_ref[...] = sums
        beta, unscale, columns, lengths = weights_of(sums, step)
        weights = columns[-1]
        inverse = 1.0 / lengths[-1]
        spread = lambda value: jnp.concatenate([value] * (width // 128), axis=1)
        lead = spread(inverse * unscale if step == 1 else inverse)
        factors = [spread(weights[i] * inverse * (unscale if i == 0 else 1.0)) for i in range(step)]
        new = []
        members = []
        v_all = [[] for _ in range(step)]
        for k in range(layers):
            new.append([])
            members.append([])
            for c in range(3):
                old_v = [right_ref[c, k]] + [earlier[i][0][c, k] for i in range(1, step)]
                old_z = [earlier[0][0][c, k]] + [earlier[i][1][c, k] for i in range(1, step)]
                old_w = [earlier[0][1][c, k]] + [earlier[i][2][c, k] for i in range(1, step)]
                v = old_w[-1] * lead
                z = solved_ref[c, k] * lead
                w = applied[k][c] * lead
                for i in range(step):
                    v = v - factors[i] * old_v[i]
                    z = z - factors[i] * old_z[i]
                    w = w - factors[i] * old_w[i]
                v_ref[c, k] = v
                z_ref[c, k] = z
                if not last:
                    w_ref[c, k] = w
                new[k].append(w)
                members[k].append(v)
        first = spread(unscale)
        basis = [[[right_ref[c, k] * first for c in range(3)] for k in range(layers)]]
        for i in range(1, step):
            basis.append([[earlier[i][0][c, k] for c in range(3)] for k in range(layers)])
        basis.append(members)
        pairs = [(member, new) for member in basis] + [(new, new)]

    edge_ref[...] = jnp.zeros(edge_ref.shape, F32)
    lane = lax.broadcasted_iota(jnp.int32, (1, 128), 1)
    line = jnp.zeros((1, 128), F32)
    for number, (left, right) in enumerate(pairs):
        total = jnp.zeros((rows, width), F32)
        for k in range(layers):
            for c in range(3):
                total = total + left[k][c] * right[k][c]
        total = jnp.sum(jnp.sum(total, axis=0, keepdims=True), axis=1, keepdims=True)
        line = jnp.where(lane == number, total, line)
    if last:
        for peer in range(edge_ref.shape[0]):
            edge_ref[peer] = line
    else:
        edge_ref[6 * rows : 6 * rows + 1, 0:128] = line
        lowest, alone = local_sweeps(new, pivot_ref, lower_ref, upper_ref, layers)
        for c in range(3):
            edge_ref[c * rows : (c + 1) * rows] = lowest[c]
            edge_ref[(3 + c) * rows : (4 + c) * rows] = alone[0][c]
            for k in range(layers):
                alone_ref[c, k] = alone[k][c]


def finish_kernel(dots_ref, sums_ref, z0_ref, z1_ref, z2_ref, z3_ref, update_ref, hessenberg_ref):
    z_refs = (z0_ref, z1_ref, z2_ref, z3_ref)
    rows, width = z0_ref.shape[2:]
    fresh = dots_ref[0]
    for peer in range(1, dots_ref.shape[0]):
        fresh = fresh + dots_ref[peer]
    history_row = lax.broadcasted_iota(jnp.int32, sums_ref.shape, 0)
    sums = jnp.where(history_row == ITERS - 1, fresh, sums_ref[...])
    beta, unscale, columns, lengths = weights_of(sums, ITERS)
    row_at = lax.broadcasted_iota(jnp.int32, (8, 128), 0)
    column_at = lax.broadcasted_iota(jnp.int32, (8, 128), 1)
    table = jnp.zeros((8, 128), F32)
    for j in range(ITERS):
        for i, weight in enumerate(columns[j] + [lengths[j]]):
            table = jnp.where((row_at == i) & (column_at == j), weight, table)
    hessenberg_ref[...] = table[0 : hessenberg_ref.shape[0], 0 : hessenberg_ref.shape[1]]
    goal = [beta]
    triangle = []
    rotations = []
    for j in range(ITERS):
        entries = list(columns[j])
        for i, (cosine, sine) in enumerate(rotations):
            upper, lower = entries[i], entries[i + 1]
            entries[i] = cosine * upper + sine * lower
            entries[i + 1] = cosine * lower - sine * upper
        radius = jnp.sqrt(entries[j] * entries[j] + lengths[j] * lengths[j])
        cosine, sine = entries[j] / radius, lengths[j] / radius
        rotations.append((cosine, sine))
        entries[j] = radius
        triangle.append(entries)
        leading = goal[j]
        goal[j] = cosine * leading
        goal.append(-sine * leading)
    answer = [None] * ITERS
    for i in range(ITERS - 1, -1, -1):
        partial = goal[i]
        for j in range(i + 1, ITERS):
            partial = partial - triangle[j][i] * answer[j]
        answer[i] = partial / triangle[i][i]
    factors = [
        jnp.concatenate([answer[j] * unscale if j == 0 else answer[j]] * (width // 128), axis=1)
        for j in range(ITERS)
    ]
    for c in range(3):
        for k in range(z0_ref.shape[1]):
            value = factors[0] * z_refs[0][c, k]
            for j in range(1, ITERS):
                value = value + factors[j] * z_refs[j][c, k]
            update_ref[c, k] = value


def turn(array, by):
    count = lax.axis_size("layer")
    return lax.ppermute(array, "layer", [(i, (i + by) % count) for i in range(count)])


def shape_of(*dims, kind=F32):
    return jax.ShapeDtypeStruct(dims, kind)


def local(
    right_side,
    diag_blocks,
    couplings,
    pivot_inverse,
    lower_blocks,
    upper_blocks,
    active_cells,
    link_from,
    link_owner,
    link_target,
    link_blocks,
):
    _, layers, rows, width = right_side.shape
    peers = lax.axis_size("areal")
    sections = lax.axis_size("layer")
    links = link_from.shape[1]
    capacity = 2 * links // peers
    slots = capacity * peers // width
    per_peer = slots // peers
    link_rows = links // width
    field = shape_of(3, layers, rows, width)
    edge_rows = 7 * rows
    sent_width = (3 * per_peer + 3 * layers) * width + 128
    first_width = (4 * per_peer + 3 * layers) * width
    edge_shape = shape_of(edge_rows, width)
    hbm = pl.BlockSpec(memory_space=pltpu.HBM)
    operands = [
        right_side,
        pivot_inverse,
        lower_blocks,
        upper_blocks,
        active_cells,
        link_from,
        link_owner.reshape(1, links),
        link_target,
        link_blocks.reshape(3, 3, links),
    ]
    (
        edge, following, alone, from_above, from_below, matrices,
        slot_block, slot_source, slot_target,
    ) = call(
        functools.partial(setup_kernel, peers),
        [
            edge_shape,
            shape_of(16 * rows, width),
            field,
            shape_of(3, 3, layers, rows, width),
            shape_of(3, 3, layers, rows, width),
            shape_of(27 * rows, width),
            shape_of(3, 3, slots, width),
            shape_of(slots, width, kind=jnp.int32),
            shape_of(slots, width),
        ],
        [pltpu.VMEM(operand.shape, operand.dtype) for operand in operands]
        + [
            pltpu.VMEM((peers * link_rows, width), BF16),
            pltpu.VMEM((13 * slots, width), F32),
            pltpu.VMEM((3, link_rows, width), jnp.int32),
            pltpu.SemaphoreType.DMA((len(operands),)),
        ],
        name="setup",
        inputs=[hbm] * len(operands),
        limit=16,
    )(*[pltpu.with_memory_space_constraint(operand, pltpu.HBM) for operand in operands])
    turned = [turn(following, 1)] + [turn(edge, by) for by in range(2, sections)]
    all_matrices = lax.all_gather(matrices, "layer", axis=0, tiled=False)

    sums = jnp.zeros((8, 128), F32)
    earlier = []
    zs = []
    for step in range(ITERS):
        last = step == ITERS - 1
        scratch = [
            pltpu.VMEM((sections, 3, rows, width), F32),
            pltpu.VMEM((sections, 3, rows, width), F32),
            pltpu.VMEM((2, 16, width), F32),
            pltpu.VMEM((3, layers * rows, width), F32),
        ]
        if step == 0:
            edges = edge
            scratch.append(pltpu.VMEM((sections, 6 * rows, width), F32))
        else:
            edges = lax.all_gather(edge, "layer", axis=0, tiled=False)
        solved, layer_sides, sent = call(
            functools.partial(couple_kernel, step == 0, sections),
            [
                field,
                shape_of(2, 3, rows, width),
                shape_of(peers, 1, first_width if step == 0 else sent_width),
            ],
            scratch,
            name="couple",
        )(
            *turned, edges, all_matrices, alone, from_above, from_below, active_cells,
            slot_block, slot_source, slot_target,
        )
        got = lax.all_to_all(sent, "areal", split_axis=0, concat_axis=0, tiled=True)
        operands = [got, solved, layer_sides, diag_blocks, couplings, active_cells]
        if step > 0:
            operands += [hot_row, hot_column]
        if not last:
            operands += [pivot_inverse, lower_blocks, upper_blocks]
        operands.append(right_side)
        if step > 0:
            operands.append(sums)
            for group in earlier:
                operands += list(group)
        history = shape_of(8, 128)
        if step == 0:
            outs = [
                field,
                edge_shape,
                field,
                shape_of(peers, layers * rows, capacity, kind=BF16),
                shape_of(peers, capacity, width, kind=BF16),
            ]
        elif last:
            outs = [field, field, shape_of(peers * sections, 1, 128), history]
        else:
            outs = [field, field, field, edge_shape, field, history]
        results = call(
            functools.partial(operate_kernel, step),
            outs,
            ([pltpu.VMEM((slots, width), F32)] if step == 0 else [])
            + [pltpu.VMEM((3 * PARTS * layers * rows, width), F32)],
            name="operate",
        )(*operands)
        if step == 0:
            applied, edge, alone, hot_row, hot_column = results
            earlier.append((solved, applied))
            zs.append(solved)
        elif last:
            _, z, dots, sums = results
            zs.append(z)
        else:
            v, z, w, edge, alone, sums = results
            earlier.append((v, z, w))
            zs.append(z)
    dots = lax.all_to_all(dots, ("areal", "layer"), split_axis=0, concat_axis=0, tiled=True)
    update, hessenberg = call(
        finish_kernel, [field, shape_of(ITERS + 1, ITERS)], name="finish"
    )(dots, sums, *zs)
    return update, hessenberg


def solution(mesh):
    placed = (
        P(None, "layer", "areal", None),
        P(None, None, "layer", "areal", None),
        P(None, None, None, "layer", "areal", None),
        P(None, None, "layer", "areal", None),
        P(None, None, "layer", "areal", None),
        P(None, None, "layer", "areal", None),
        P("layer", "areal", None),
        P("layer", "areal"),
        P("layer", "areal", None),
        P("layer", "areal"),
        P(None, None, "layer", "areal"),
    )
    return jax.shard_map(
        local,
        mesh=mesh,
        in_specs=placed,
        out_specs=(P(None, "layer", "areal", None), P()),
        check_vma=False,
    )
```

```python
import functools

import jax
import jax.numpy as jnp
from jax import lax
from jax.experimental import pallas as pl
from jax.experimental.pallas import tpu as pltpu
from jax.sharding import PartitionSpec as P

ITERS = 4
PARTS = 3
TINY = 1e-06

F32 = jnp.float32
BF16 = jnp.bfloat16
VMEM = pl.BlockSpec(memory_space=pltpu.VMEM)


def call(kernel, outs, scratch=(), name=None, inputs=None, limit=20, flops=1 << 22, moved=1 << 20):
    many = isinstance(outs, (list, tuple))
    where = {} if inputs is None else {"in_specs": inputs}
    return pl.pallas_call(
        kernel,
        out_shape=outs,
        **where,
        out_specs=[VMEM] * len(outs) if many else VMEM,
        scratch_shapes=list(scratch),
        compiler_params=pltpu.CompilerParams(vmem_limit_bytes=limit << 20),
        cost_estimate=pl.CostEstimate(flops=flops, bytes_accessed=moved, transcendentals=0),
        name=name,
    )


def wide(value):
    return value.astype(F32)


def times(blocks, vector):
    result = []
    for row in blocks:
        total = row[0] * vector[0]
        for entry, element in zip(row[1:], vector[1:]):
            total = total + entry * element
        result.append(total)
    return result


def block_at(ref, layer):
    return [[wide(ref[c, d, layer]) for d in range(3)] for c in range(3)]


def minus(left, right):
    return [a - b for a, b in zip(left, right)]


def plus(left, right):
    return [a + b for a, b in zip(left, right)]


def local_sweeps(planes, pivot, lower, upper, layers):
    forward = []
    previous = None
    for k in range(layers):
        current = times(block_at(pivot, k), planes[k])
        if previous is not None:
            current = minus(current, times(block_at(lower, k), previous))
        forward.append(current)
        previous = current
    backward = [None] * layers
    previous = None
    for k in range(layers - 1, -1, -1):
        current = forward[k]
        if previous is not None:
            current = minus(current, times(block_at(upper, k), previous))
        backward[k] = current
        previous = current
    return forward[layers - 1], backward


def section_part(
    right_ref, pivot_ref, lower_ref, upper_ref, active_ref,
    edge_ref, next_ref, alone_ref, from_above_ref, from_below_ref, matrix_ref,
):
    layers, rows = right_ref.shape[1], right_ref.shape[2]
    planes = [[right_ref[c, k] for c in range(3)] for k in range(layers)]
    lowest, solved = local_sweeps(planes, pivot_ref, lower_ref, upper_ref, layers)
    for c in range(3):
        for ref in (edge_ref, next_ref):
            ref[c * rows : (c + 1) * rows] = lowest[c]
            ref[(3 + c) * rows : (4 + c) * rows] = solved[0][c]
        for k in range(layers):
            alone_ref[c, k] = solved[k][c]
    for d in range(3):
        carried = []
        previous = None
        for k in range(layers):
            blocks = block_at(lower_ref, k)
            if previous is None:
                previous = [-blocks[c][d] for c in range(3)]
            else:
                previous = [-value for value in times(blocks, previous)]
            carried.append(previous)
        for c in range(3):
            matrix_ref[(c * 3 + d) * rows : (c * 3 + d + 1) * rows] = carried[-1][c]
        response = carried[-1]
        for k in range(layers - 1, -1, -1):
            if k < layers - 1:
                response = minus(carried[k], times(block_at(upper_ref, k), response))
            for c in range(3):
                from_above_ref[c, d, k] = response[c]
        for c in range(3):
            matrix_ref[(9 + c * 3 + d) * rows : (10 + c * 3 + d) * rows] = response[c]
        response = None
        for k in range(layers - 1, -1, -1):
            blocks = block_at(upper_ref, k)
            if response is None:
                for c in range(3):
                    next_ref[(6 + c * 3 + d) * rows : (7 + c * 3 + d) * rows] = blocks[c][d]
                response = [-blocks[c][d] for c in range(3)]
            else:
                response = [-value for value in times(blocks, response)]
            for c in range(3):
                from_below_ref[c, d, k] = response[c]
        for c in range(3):
            matrix_ref[(18 + c * 3 + d) * rows : (19 + c * 3 + d) * rows] = response[c]
    edge_ref[6 * rows : 7 * rows] = wide(active_ref[0])
    next_ref[15 * rows : 16 * rows] = wide(active_ref[layers - 1])


def routing_part(
    peers, folded, block_ref, slot_block_ref, slot_source_ref, slot_target_ref, stacked, products
):
    rows, width = folded.shape[1:]
    slots = slot_source_ref.shape[0]
    per_peer = slots // peers
    owner = folded[1]
    for o in range(peers):
        stacked[o * rows : (o + 1) * rows] = jnp.where(owner == o, 1.0, 0.0).astype(BF16)
    chosen = stacked[...]
    ones_before = jnp.where(
        lax.broadcasted_iota(jnp.int32, (width, width), 0)
        < lax.broadcasted_iota(jnp.int32, (width, width), 1),
        1.0,
        0.0,
    ).astype(BF16)
    within = jnp.dot(chosen, ones_before, preferred_element_type=F32)
    totals = jnp.dot(chosen, jnp.ones((width, width), BF16), preferred_element_type=F32)
    row_before = jnp.where(
        lax.broadcasted_iota(jnp.int32, (rows, rows), 1)
        < lax.broadcasted_iota(jnp.int32, (rows, rows), 0),
        1.0,
        0.0,
    ).astype(BF16)
    rank = jnp.zeros((rows, width), F32)
    for o in range(peers):
        part = slice(o * rows, (o + 1) * rows)
        before = jnp.dot(row_before, totals[part].astype(BF16), preferred_element_type=F32)
        rank = rank + jnp.where(owner == o, within[part] + before, 0.0)
    rank = rank.astype(jnp.int32)
    slot_row = owner * per_peer + rank // width
    slot_column = rank % width
    source = folded[0]
    target = folded[2]
    payloads = [
        wide(source // width),
        wide(source % width),
        wide(target // width),
        wide(target % width),
    ]
    row_number = lax.broadcasted_iota(jnp.int32, (slots, width), 0)
    column_number = lax.broadcasted_iota(jnp.int32, (width, width), 0)
    total = jnp.zeros(products.shape, F32)
    for r in range(rows):
        in_row = row_number == slot_row[r : r + 1]
        left = jnp.concatenate(
            [
                jnp.where(in_row, payload, 0.0).astype(BF16)
                for payload in [payload[r : r + 1] for payload in payloads]
                + [
                    wide(block_ref[c, d : d + 1, r * width : (r + 1) * width])
                    for c in range(3)
                    for d in range(3)
                ]
            ],
            axis=0,
        )
        right = jnp.where(column_number == slot_column[r : r + 1], 1.0, 0.0).astype(BF16)
        total = total + lax.dot_general(
            left, right, (((1,), (1,)), ((), ())), preferred_element_type=F32
        )
    products[...] = total
    slot_source_ref[...] = (products[0:slots] * width + products[slots : 2 * slots]).astype(jnp.int32)
    slot_target_ref[...] = products[2 * slots : 3 * slots] * width + products[3 * slots : 4 * slots]
    for c in range(3):
        for d in range(3):
            at = 4 + c * 3 + d
            slot_block_ref[c, d] = products[at * slots : (at + 1) * slots]


def setup_kernel(
    peers,
    right_hbm, pivot_hbm, lower_hbm, upper_hbm, active_hbm,
    from_hbm, owner_hbm, target_hbm, block_hbm,
    edge_ref, next_ref, alone_ref, from_above_ref, from_below_ref, matrix_ref,
    slot_block_ref, slot_source_ref, slot_target_ref, mask_ref,
    right_ref, pivot_ref, lower_ref, upper_ref, active_ref,
    from_ref, owner_ref, target_ref, block_ref,
    stacked, products, folded, semaphores,
):
    copies = [
        pltpu.make_async_copy(source, landing, semaphores.at[number])
        for number, (source, landing) in enumerate(
            [
                (lower_hbm, lower_ref),
                (upper_hbm, upper_ref),
                (active_hbm, active_ref),
                (pivot_hbm, pivot_ref),
                (right_hbm, right_ref),
                (owner_hbm, owner_ref),
                (from_hbm, from_ref),
                (target_hbm, target_ref),
                (block_hbm, block_ref),
            ]
        )
    ]
    for copy in copies:
        copy.start()
    for copy in copies:
        copy.wait()
    section_part(
        right_ref, pivot_ref, lower_ref, upper_ref, active_ref,
        edge_ref, next_ref, alone_ref, from_above_ref, from_below_ref, matrix_ref,
    )
    mask_ref[...] = wide(active_ref[...])
    rows, width = folded.shape[1:]
    for r in range(rows):
        for number, ref in enumerate((from_ref, owner_ref, target_ref)):
            folded[number, r : r + 1] = ref[0:1, r * width : (r + 1) * width]
    routing_part(
        peers, folded, block_ref, slot_block_ref, slot_source_ref, slot_target_ref, stacked, products
    )


def couple_kernel(
    first, sections, *refs,
):
    turned, refs = refs[: sections - 1], refs[sections - 1 :]
    if first:
        own_ref, refs = refs[0], refs[1:]
        edge_ref = refs[-1]
        refs = refs[:-1]
    else:
        edge_ref, refs = refs[0], refs[1:]
    (
        matrix_ref, alone_ref, above_ref, below_ref, active_ref,
        slot_block_ref, slot_source_ref, slot_target_ref,
        solved_ref, layer_ref, sent_ref, arriving, tops, borders, table,
    ) = refs
    layers, rows = alone_ref.shape[1], alone_ref.shape[2]
    width = alone_ref.shape[3]
    peers = sent_ref.shape[0]
    slots = slot_source_ref.shape[0]
    per_peer = slots // peers
    s = lax.axis_index("layer")
    a = lax.axis_index("areal")
    if first:
        edge_ref[s] = own_ref[0 : 6 * rows]
        for turn in range(1, sections):
            edge_ref[lax.rem(s - turn + sections, sections)] = turned[turn - 1][0 : 6 * rows]

    def matrix(section, which):
        return [
            [
                matrix_ref[section, (which * 9 + c * 3 + d) * rows : (which * 9 + c * 3 + d + 1) * rows]
                for d in range(3)
            ]
            for c in range(3)
        ]

    def edge(section, which):
        return [
            edge_ref[section, (which * 3 + c) * rows : (which * 3 + c + 1) * rows] for c in range(3)
        ]

    zero = jnp.zeros((rows, width), F32)
    coming = [[zero] * 3]
    for section in range(1, sections):
        value = edge(section - 1, 0)
        if section > 1:
            value = plus(value, times(matrix(section - 1, 0), coming[section - 1]))
        coming.append(value)
    rising = [None] * sections + [[zero] * 3]
    for section in range(sections - 1, 0, -1):
        value = plus(edge(section, 1), times(matrix(section, 1), coming[section]))
        if section < sections - 1:
            value = plus(value, times(matrix(section, 2), rising[section + 1]))
        rising[section] = value
    rising[0] = [zero] * 3
    for section in range(sections):
        for c in range(3):
            arriving[section, c] = coming[section][c]
            tops[section, c] = rising[section + 1][c]
    above = [arriving[s, c] for c in range(3)]
    below = [tops[s, c] for c in range(3)]
    active = [wide(active_ref[k]) for k in range(layers)]
    for k in range(layers):
        for c in range(3):
            value = alone_ref[c, k]
            for d in range(3):
                value = value + above_ref[c, d, k] * above[d] + below_ref[c, d, k] * below[d]
            solved_ref[c, k] = value
            held = value * active[k]
            table[c, k * rows : (k + 1) * rows] = held
            borders[0, c * layers + k : c * layers + k + 1] = held[0:1]
            borders[1, c * layers + k : c * layers + k + 1] = held[rows - 1 : rows]
    previous, following = turned[0], turned[-1]
    bottom = [
        [previous[(6 + c * 3 + d) * rows : (7 + c * 3 + d) * rows] for d in range(3)]
        for c in range(3)
    ]
    own_top = [solved_ref[c, 0] for c in range(3)]
    upstairs = minus(above, times(bottom, own_top))
    upper_active = jnp.where(s > 0, previous[15 * rows : 16 * rows], 0.0)
    lower_active = jnp.where(s < sections - 1, following[6 * rows : 7 * rows], 0.0)
    for c in range(3):
        layer_ref[0, c] = upstairs[c] * upper_active
        layer_ref[1, c] = below[c] * lower_active
    half = 128
    groups = [(g, h) for g in range(slots // 8) for h in range(width // half)]
    for g in range(slots // 8):
        for h in range(width // half):
            source = slot_source_ref[g * 8 : (g + 1) * 8, h * half : (h + 1) * half]
            line = source // half
            lane = source % half
            found = [jnp.zeros((8, half), F32)] * 3
            for r in range(layers * rows):
                for q in range(width // half):
                    here = line == r * (width // half) + q
                    for c in range(3):
                        row = jnp.broadcast_to(
                            table[c, r : r + 1, q * half : (q + 1) * half], (8, half)
                        )
                        picked = jnp.take_along_axis(row, lane, axis=1)
                        found[c] = jnp.where(here, picked, found[c])
            for c in range(3):
                value = slot_block_ref[c, 0, g * 8 : (g + 1) * 8, h * half : (h + 1) * half] * found[0]
                for d in range(1, 3):
                    value = value + (
                        slot_block_ref[c, d, g * 8 : (g + 1) * 8, h * half : (h + 1) * half] * found[d]
                    )
                for i in range(8):
                    slot = g * 8 + i
                    peer, at = slot // per_peer, slot % per_peer
                    start = (c * per_peer + at) * width + h * half
                    sent_ref[peer, 0:1, start : start + half] = value[i : i + 1]
    base = 3 * per_peer * width
    many = 3 * layers
    if not first:
        sums = edge_ref[0, 6 * rows : 6 * rows + 1, 0:half]
        for section in range(1, sections):
            sums = sums + edge_ref[section, 6 * rows : 6 * rows + 1, 0:half]
    for peer in range(peers):
        side = jnp.where(peer > a, 1, 0)
        for i in range(many):
            start = base + i * width
            sent_ref[peer, 0:1, start : start + width] = borders[side, i : i + 1]
        start = base + many * width
        if not first:
            sent_ref[peer, 0:1, start : start + half] = sums
        else:
            for i in range(per_peer):
                at = peer * per_peer + i
                sent_ref[peer, 0:1, start + i * width : start + (i + 1) * width] = slot_target_ref[
                    at : at + 1
                ]


def weights_of(sums, upto):
    def value(step, at):
        row = jnp.broadcast_to(sums[step : step + 1], (8, 128))
        return jnp.take_along_axis(row, jnp.full((8, 128), at, jnp.int32), axis=1)

    squared = value(0, 0)
    beta = jnp.sqrt(squared + TINY)
    unscale = 1.0 / beta
    gram = [[squared * unscale * unscale]]
    columns = []
    lengths = []
    for step in range(upto):
        if step == 0:
            weights = [value(0, 1) * unscale * unscale]
            own = value(0, 2) * unscale * unscale
        else:
            weights = [value(step, i) for i in range(step + 1)]
            own = value(step, step + 1)
        size = step + 1
        shadow = []
        for i in range(size):
            total = weights[0] * gram[i][0]
            for k in range(1, size):
                total = total + weights[k] * gram[i][k]
            shadow.append(total)
        left = own
        for i in range(size):
            left = left - weights[i] * (2.0 * weights[i] - shadow[i])
        left = jnp.maximum(left, 0.0)
        length = jnp.sqrt(left + TINY)
        inverse = 1.0 / length
        column = [(weights[i] - shadow[i]) * inverse for i in range(size)]
        for i in range(size):
            gram[i].append(column[i])
        gram.append(column + [left * inverse * inverse])
        columns.append(weights)
        lengths.append(length)
    return beta, unscale, columns, lengths


def operate_kernel(step, *refs):
    last = step == ITERS - 1
    got_ref, solved_ref, layer_ref, diag_ref, coupling_ref, active_ref = refs[:6]
    at = 6
    if step > 0:
        hot_row_ref, hot_column_ref = refs[6:8]
        at = 8
    if not last:
        pivot_ref, lower_ref, upper_ref = refs[at : at + 3]
        at += 3
    right_ref = refs[at]
    at += 1
    if step > 0:
        sums_ref = refs[at]
        at += 1
        earlier = []
        for i in range(step):
            earlier.append(refs[at : at + (2 if i == 0 else 3)])
            at += len(earlier[-1])
    outs = refs[at:]
    layers, rows, width = solved_ref.shape[1:]
    peers = got_ref.shape[0]
    per_peer = layers * rows // peers
    base = 3 * per_peer * width
    many = 3 * layers
    ending = base + many * width
    cells = layers * rows
    a = lax.axis_index("areal")
    total_ref = outs[-1]
    outs = outs[:-1]
    if step == 0:
        lines_ref = outs[-1]
        hot_row_ref, hot_column_ref = outs[-3:-1]
        outs = outs[:-3]

    capacity = per_peer * width
    if step == 0:
        for peer in range(peers):
            for i in range(per_peer):
                at = peer * per_peer + i
                lines_ref[at : at + 1] = got_ref[
                    peer, 0:1, ending + i * width : ending + (i + 1) * width
                ]
        where = lines_ref[...].astype(jnp.int32)
        upright = jnp.transpose(wide(where % width))
        upper = where // width
        row_number = lax.broadcasted_iota(jnp.int32, (cells, width), 0)
        column_number = wide(lax.broadcasted_iota(jnp.int32, (width, width), 1))
        for peer in range(peers):
            for i in range(per_peer):
                at = peer * per_peer + i
                hot_column_ref[peer, i * width : (i + 1) * width] = jnp.where(
                    column_number == upright[:, at : at + 1], 1.0, 0.0
                ).astype(BF16)
                hot_row_ref[peer, :, i * width : (i + 1) * width] = jnp.where(
                    row_number == upper[at : at + 1], 1.0, 0.0
                ).astype(BF16)
    added = None
    for peer in range(peers):
        hot = hot_row_ref[peer]
        pieces = []
        for c in range(3):
            rest = got_ref[peer, 0:1, c * capacity : (c + 1) * capacity]
            for part in range(PARTS):
                piece = rest.astype(BF16)
                rest = rest - wide(piece)
                pieces.append(hot * jnp.broadcast_to(piece, hot.shape))
        product = jnp.dot(
            jnp.concatenate(pieces, axis=0), hot_column_ref[peer], preferred_element_type=F32
        )
        added = product if added is None else added + product
    total_ref[...] = added

    active = [wide(active_ref[k]) for k in range(layers)]
    held = [[solved_ref[c, k] * active[k] for c in range(3)] for k in range(layers)]
    row_at = lax.broadcasted_iota(jnp.int32, (rows, width), 0)
    column_at = lax.broadcasted_iota(jnp.int32, (rows, width), 1)
    before, after = jnp.maximum(a - 1, 0), jnp.minimum(a + 1, peers - 1)
    has_before = jnp.where(a > 0, 1.0, 0.0)
    has_after = jnp.where(a < peers - 1, 1.0, 0.0)
    applied = []
    for k in range(layers):
        beside = []
        beside.append(held[k - 1] if k > 0 else [layer_ref[0, c] for c in range(3)])
        beside.append(held[k + 1] if k < layers - 1 else [layer_ref[1, c] for c in range(3)])
        sides = [[], [], [], []]
        for c in range(3):
            border = base + (c * layers + k) * width
            low = got_ref[before, 0:1, border : border + width] * has_before
            high = got_ref[after, 0:1, border : border + width] * has_after
            value = held[k][c]
            sides[0].append(jnp.where(row_at == 0, low, pltpu.roll(value, 1, 0)))
            sides[1].append(jnp.where(row_at == rows - 1, high, pltpu.roll(value, rows - 1, 0)))
            sides[2].append(jnp.where(column_at == 0, 0.0, pltpu.roll(value, 1, 1)))
            sides[3].append(jnp.where(column_at == width - 1, 0.0, pltpu.roll(value, width - 1, 1)))
        result = times(block_at(diag_ref, k), held[k])
        for d, neighbour in enumerate(beside + sides):
            blocks = [[wide(coupling_ref[d, i, j, k]) for j in range(3)] for i in range(3)]
            result = plus(result, times(blocks, neighbour))
        for c in range(3):
            for part in range(PARTS):
                start = (c * PARTS + part) * cells + k * rows
                result[c] = result[c] + total_ref[start : start + rows]
        applied.append(
            [
                active[k] * result[c] + (1.0 - active[k]) * solved_ref[c, k]
                for c in range(3)
            ]
        )

    pairs = []
    if step == 0:
        (applied_ref, edge_ref, alone_ref) = outs
        for k in range(layers):
            for c in range(3):
                applied_ref[c, k] = applied[k][c]
        new = applied
        r = [[right_ref[c, k] for c in range(3)] for k in range(layers)]
        pairs = [(r, r), (r, applied), (applied, applied)]
    else:
        if last:
            (z_ref, edge_ref, history_ref) = outs
        else:
            (v_ref, z_ref, w_ref, edge_ref, alone_ref, history_ref) = outs
        fresh = got_ref[0, 0:1, ending : ending + 128]
        for peer in range(1, peers):
            fresh = fresh + got_ref[peer, 0:1, ending : ending + 128]
        history_row = lax.broadcasted_iota(jnp.int32, history_ref.shape, 0)
        sums = jnp.where(history_row == step - 1, fresh, sums_ref[...])
        history_ref[...] = sums
        beta, unscale, columns, lengths = weights_of(sums, step)
        weights = columns[-1]
        inverse = 1.0 / lengths[-1]
        spread = lambda value: jnp.concatenate([value] * (width // 128), axis=1)
        lead = spread(inverse * unscale if step == 1 else inverse)
        factors = [spread(weights[i] * inverse * (unscale if i == 0 else 1.0)) for i in range(step)]
        new = []
        members = []
        v_all = [[] for _ in range(step)]
        for k in range(layers):
            new.append([])
            members.append([])
            for c in range(3):
                old_v = [right_ref[c, k]] + [earlier[i][0][c, k] for i in range(1, step)]
                old_z = [earlier[0][0][c, k]] + [earlier[i][1][c, k] for i in range(1, step)]
                old_w = [earlier[0][1][c, k]] + [earlier[i][2][c, k] for i in range(1, step)]
                v = old_w[-1] * lead
                z = solved_ref[c, k] * lead
                w = applied[k][c] * lead
                for i in range(step):
                    v = v - factors[i] * old_v[i]
                    z = z - factors[i] * old_z[i]
                    w = w - factors[i] * old_w[i]
                z_ref[c, k] = z
                if not last:
                    v_ref[c, k] = v
                    w_ref[c, k] = w
                new[k].append(w)
                members[k].append(v)
        first = spread(unscale)
        basis = [[[right_ref[c, k] * first for c in range(3)] for k in range(layers)]]
        for i in range(1, step):
            basis.append([[earlier[i][0][c, k] for c in range(3)] for k in range(layers)])
        basis.append(members)
        pairs = [(member, new) for member in basis] + [(new, new)]

    edge_ref[...] = jnp.zeros(edge_ref.shape, F32)
    lane = lax.broadcasted_iota(jnp.int32, (1, 128), 1)
    line = jnp.zeros((1, 128), F32)
    for number, (left, right) in enumerate(pairs):
        total = jnp.zeros((rows, width), F32)
        for k in range(layers):
            for c in range(3):
                total = total + left[k][c] * right[k][c]
        total = jnp.sum(jnp.sum(total, axis=0, keepdims=True), axis=1, keepdims=True)
        line = jnp.where(lane == number, total, line)
    if last:
        for peer in range(edge_ref.shape[0]):
            edge_ref[peer] = line
    else:
        edge_ref[6 * rows : 6 * rows + 1, 0:128] = line
        lowest, alone = local_sweeps(new, pivot_ref, lower_ref, upper_ref, layers)
        for c in range(3):
            edge_ref[c * rows : (c + 1) * rows] = lowest[c]
            edge_ref[(3 + c) * rows : (4 + c) * rows] = alone[0][c]
            for k in range(layers):
                alone_ref[c, k] = alone[k][c]


def finish_kernel(dots_ref, sums_ref, z0_ref, z1_ref, z2_ref, z3_ref, update_ref, hessenberg_ref):
    z_refs = (z0_ref, z1_ref, z2_ref, z3_ref)
    rows, width = z0_ref.shape[2:]
    fresh = dots_ref[0]
    for peer in range(1, dots_ref.shape[0]):
        fresh = fresh + dots_ref[peer]
    history_row = lax.broadcasted_iota(jnp.int32, sums_ref.shape, 0)
    sums = jnp.where(history_row == ITERS - 1, fresh, sums_ref[...])
    beta, unscale, columns, lengths = weights_of(sums, ITERS)
    row_at = lax.broadcasted_iota(jnp.int32, (8, 128), 0)
    column_at = lax.broadcasted_iota(jnp.int32, (8, 128), 1)
    table = jnp.zeros((8, 128), F32)
    for j in range(ITERS):
        for i, weight in enumerate(columns[j] + [lengths[j]]):
            table = jnp.where((row_at == j) & (column_at == i), weight, table)
    hessenberg_ref[...] = table[0 : hessenberg_ref.shape[0], 0 : hessenberg_ref.shape[1]]
    goal = [beta]
    triangle = []
    rotations = []
    for j in range(ITERS):
        entries = list(columns[j])
        for i, (cosine, sine) in enumerate(rotations):
            upper, lower = entries[i], entries[i + 1]
            entries[i] = cosine * upper + sine * lower
            entries[i + 1] = cosine * lower - sine * upper
        radius = jnp.sqrt(entries[j] * entries[j] + lengths[j] * lengths[j])
        cosine, sine = entries[j] / radius, lengths[j] / radius
        rotations.append((cosine, sine))
        entries[j] = radius
        triangle.append(entries)
        leading = goal[j]
        goal[j] = cosine * leading
        goal.append(-sine * leading)
    answer = [None] * ITERS
    for i in range(ITERS - 1, -1, -1):
        partial = goal[i]
        for j in range(i + 1, ITERS):
            partial = partial - triangle[j][i] * answer[j]
        answer[i] = partial / triangle[i][i]
    factors = [
        jnp.concatenate([answer[j] * unscale if j == 0 else answer[j]] * (width // 128), axis=1)
        for j in range(ITERS)
    ]
    for c in range(3):
        for k in range(z0_ref.shape[1]):
            value = factors[0] * z_refs[0][c, k]
            for j in range(1, ITERS):
                value = value + factors[j] * z_refs[j][c, k]
            update_ref[c, k] = value


def turn(array, by):
    count = lax.axis_size("layer")
    return lax.ppermute(array, "layer", [(i, (i + by) % count) for i in range(count)])


def shape_of(*dims, kind=F32):
    return jax.ShapeDtypeStruct(dims, kind)


def local(
    right_side,
    diag_blocks,
    couplings,
    pivot_inverse,
    lower_blocks,
    upper_blocks,
    active_cells,
    link_from,
    link_owner,
    link_target,
    link_blocks,
):
    _, layers, rows, width = right_side.shape
    peers = lax.axis_size("areal")
    sections = lax.axis_size("layer")
    links = link_from.shape[1]
    capacity = 2 * links // peers
    slots = capacity * peers // width
    per_peer = slots // peers
    link_rows = links // width
    field = shape_of(3, layers, rows, width)
    edge_rows = 7 * rows
    sent_width = (3 * per_peer + 3 * layers) * width + 128
    first_width = (4 * per_peer + 3 * layers) * width
    edge_shape = shape_of(edge_rows, width)
    hbm = pl.BlockSpec(memory_space=pltpu.HBM)
    operands = [
        right_side,
        pivot_inverse,
        lower_blocks,
        upper_blocks,
        active_cells,
        link_from,
        link_owner.reshape(1, links),
        link_target,
        link_blocks.reshape(3, 3, links),
    ]
    (
        edge, following, alone, from_above, from_below, matrices,
        slot_block, slot_source, slot_target, active,
    ) = call(
        functools.partial(setup_kernel, peers),
        [
            edge_shape,
            shape_of(16 * rows, width),
            field,
            shape_of(3, 3, layers, rows, width),
            shape_of(3, 3, layers, rows, width),
            shape_of(27 * rows, width),
            shape_of(3, 3, slots, width),
            shape_of(slots, width, kind=jnp.int32),
            shape_of(slots, width),
            shape_of(layers, rows, width),
        ],
        [pltpu.VMEM(operand.shape, operand.dtype) for operand in operands]
        + [
            pltpu.VMEM((peers * link_rows, width), BF16),
            pltpu.VMEM((13 * slots, width), F32),
            pltpu.VMEM((3, link_rows, width), jnp.int32),
            pltpu.SemaphoreType.DMA((len(operands),)),
        ],
        name="setup",
        inputs=[hbm] * len(operands),
        limit=16,
    )(*[pltpu.with_memory_space_constraint(operand, pltpu.HBM) for operand in operands])
    turned = [turn(following, 1)] + [turn(edge, by) for by in range(2, sections)]
    all_matrices = lax.all_gather(matrices, "layer", axis=0, tiled=False)

    sums = jnp.zeros((8, 128), F32)
    earlier = []
    zs = []
    for step in range(ITERS):
        last = step == ITERS - 1
        scratch = [
            pltpu.VMEM((sections, 3, rows, width), F32),
            pltpu.VMEM((sections, 3, rows, width), F32),
            pltpu.VMEM((2, 16, width), F32),
            pltpu.VMEM((3, layers * rows, width), F32),
        ]
        if step == 0:
            edges = edge
            scratch.append(pltpu.VMEM((sections, 6 * rows, width), F32))
        else:
            edges = lax.all_gather(edge, "layer", axis=0, tiled=False)
        solved, layer_sides, sent = call(
            functools.partial(couple_kernel, step == 0, sections),
            [
                field,
                shape_of(2, 3, rows, width),
                shape_of(peers, 1, first_width if step == 0 else sent_width),
            ],
            scratch,
            name="couple",
        )(
            *turned, edges, all_matrices, alone, from_above, from_below, active,
            slot_block, slot_source, slot_target,
        )
        got = lax.all_to_all(sent, "areal", split_axis=0, concat_axis=0, tiled=True)
        operands = [got, solved, layer_sides, diag_blocks, couplings, active]
        if step > 0:
            operands += [hot_row, hot_column]
        if not last:
            operands += [pivot_inverse, lower_blocks, upper_blocks]
        operands.append(right_side)
        if step > 0:
            operands.append(sums)
            for group in earlier:
                operands += list(group)
        history = shape_of(8, 128)
        if step == 0:
            outs = [
                field,
                edge_shape,
                field,
                shape_of(peers, layers * rows, capacity, kind=BF16),
                shape_of(peers, capacity, width, kind=BF16),
            ]
        elif last:
            outs = [field, shape_of(peers * sections, 1, 128), history]
        else:
            outs = [field, field, field, edge_shape, field, history]
        results = call(
            functools.partial(operate_kernel, step),
            outs,
            ([pltpu.VMEM((slots, width), F32)] if step == 0 else [])
            + [pltpu.VMEM((3 * PARTS * layers * rows, width), F32)],
            name="operate",
        )(*operands)
        if step == 0:
            applied, edge, alone, hot_row, hot_column = results
            earlier.append((solved, applied))
            zs.append(solved)
        elif last:
            z, dots, sums = results
            zs.append(z)
        else:
            v, z, w, edge, alone, sums = results
            earlier.append((v, z, w))
            zs.append(z)
    dots = lax.all_to_all(dots, ("areal", "layer"), split_axis=0, concat_axis=0, tiled=True)
    update, hessenberg = call(
        finish_kernel, [field, shape_of(ITERS, ITERS + 1)], name="finish"
    )(dots, sums, *zs)
    return update, hessenberg.T


def solution(mesh):
    placed = (
        P(None, "layer", "areal", None),
        P(None, None, "layer", "areal", None),
        P(None, None, None, "layer", "areal", None),
        P(None, None, "layer", "areal", None),
        P(None, None, "layer", "areal", None),
        P(None, None, "layer", "areal", None),
        P("layer", "areal", None),
        P("layer", "areal"),
        P("layer", "areal", None),
        P("layer", "areal"),
        P(None, None, "layer", "areal"),
    )
    return jax.shard_map(
        local,
        mesh=mesh,
        in_specs=placed,
        out_specs=(P(None, "layer", "areal", None), P()),
        check_vma=False,
    )
```

```python
import functools

import jax
import jax.numpy as jnp
from jax import lax
from jax.experimental import pallas as pl
from jax.experimental.pallas import tpu as pltpu
from jax.sharding import PartitionSpec as P

ITERS = 4
PARTS = 2
TINY = 1e-06
LANES = 128

F32 = jnp.float32
BF16 = jnp.bfloat16
VMEM = pl.BlockSpec(memory_space=pltpu.VMEM)


def call(kernel, outs, scratch=(), name=None, inputs=None, limit=20, flops=1 << 22, moved=1 << 20):
    many = isinstance(outs, (list, tuple))
    where = {} if inputs is None else {"in_specs": inputs}
    return pl.pallas_call(
        kernel,
        out_shape=outs,
        **where,
        out_specs=[VMEM] * len(outs) if many else VMEM,
        scratch_shapes=list(scratch),
        compiler_params=pltpu.CompilerParams(vmem_limit_bytes=limit << 20),
        cost_estimate=pl.CostEstimate(flops=flops, bytes_accessed=moved, transcendentals=0),
        name=name,
    )


def wide(value):
    return value.astype(F32)


def times(blocks, vector):
    result = []
    for row in blocks:
        total = row[0] * vector[0]
        for entry, element in zip(row[1:], vector[1:]):
            total = total + entry * element
        result.append(total)
    return result


def block_at(ref, layer):
    return [[wide(ref[c, d, layer]) for d in range(3)] for c in range(3)]


def minus(left, right):
    return [a - b for a, b in zip(left, right)]


def plus(left, right):
    return [a + b for a, b in zip(left, right)]


def local_sweeps(planes, pivot, lower, upper, layers):
    forward = []
    previous = None
    for k in range(layers):
        current = times(block_at(pivot, k), planes[k])
        if previous is not None:
            current = minus(current, times(block_at(lower, k), previous))
        forward.append(current)
        previous = current
    backward = [None] * layers
    previous = None
    for k in range(layers - 1, -1, -1):
        current = forward[k]
        if previous is not None:
            current = minus(current, times(block_at(upper, k), previous))
        backward[k] = current
        previous = current
    return forward[layers - 1], backward


def section_part(
    right_ref, pivot_ref, lower_ref, upper_ref, active_ref,
    edge_ref, next_ref, alone_ref, from_above_ref, from_below_ref, matrix_ref,
):
    layers, rows = right_ref.shape[1], right_ref.shape[2]
    planes = [[right_ref[c, k] for c in range(3)] for k in range(layers)]
    lowest, solved = local_sweeps(planes, pivot_ref, lower_ref, upper_ref, layers)
    for c in range(3):
        for ref in (edge_ref, next_ref):
            ref[c * rows : (c + 1) * rows] = lowest[c]
            ref[(3 + c) * rows : (4 + c) * rows] = solved[0][c]
        for k in range(layers):
            alone_ref[c, k] = solved[k][c]
    for d in range(3):
        carried = []
        previous = None
        for k in range(layers):
            blocks = block_at(lower_ref, k)
            if previous is None:
                previous = [-blocks[c][d] for c in range(3)]
            else:
                previous = [-value for value in times(blocks, previous)]
            carried.append(previous)
        for c in range(3):
            matrix_ref[(c * 3 + d) * rows : (c * 3 + d + 1) * rows] = carried[-1][c]
        response = carried[-1]
        for k in range(layers - 1, -1, -1):
            if k < layers - 1:
                response = minus(carried[k], times(block_at(upper_ref, k), response))
            for c in range(3):
                from_above_ref[c, d, k] = response[c]
        for c in range(3):
            matrix_ref[(9 + c * 3 + d) * rows : (10 + c * 3 + d) * rows] = response[c]
        response = None
        for k in range(layers - 1, -1, -1):
            blocks = block_at(upper_ref, k)
            if response is None:
                for c in range(3):
                    next_ref[(6 + c * 3 + d) * rows : (7 + c * 3 + d) * rows] = blocks[c][d]
                response = [-blocks[c][d] for c in range(3)]
            else:
                response = [-value for value in times(blocks, response)]
            for c in range(3):
                from_below_ref[c, d, k] = response[c]
        for c in range(3):
            matrix_ref[(18 + c * 3 + d) * rows : (19 + c * 3 + d) * rows] = response[c]
    edge_ref[6 * rows : 7 * rows] = wide(active_ref[0])
    next_ref[15 * rows : 16 * rows] = wide(active_ref[layers - 1])


def routing_part(
    peers, cells, folded, block_ref,
    slot_block_ref, slot_source_ref, slot_target_ref, start_ref, stacked, products, packed,
):
    rows, width = folded.shape[1:]
    slots = slot_source_ref.shape[0]
    per_peer = slot_target_ref.shape[0] // peers
    owner = folded[1]
    for o in range(peers):
        stacked[o * rows : (o + 1) * rows] = jnp.where(owner == o, 1.0, 0.0).astype(BF16)
    chosen = stacked[...]
    ones_before = jnp.where(
        lax.broadcasted_iota(jnp.int32, (width, width), 0)
        < lax.broadcasted_iota(jnp.int32, (width, width), 1),
        1.0,
        0.0,
    ).astype(BF16)
    within = jnp.dot(chosen, ones_before, preferred_element_type=F32)
    totals = jnp.dot(chosen, jnp.ones((width, width), BF16), preferred_element_type=F32)
    row_before = jnp.where(
        lax.broadcasted_iota(jnp.int32, (rows, rows), 1)
        < lax.broadcasted_iota(jnp.int32, (rows, rows), 0),
        1.0,
        0.0,
    ).astype(BF16)
    rank = jnp.zeros((rows, width), F32)
    start = jnp.zeros((1, width), jnp.int32)
    starts, counts = [], []
    slot_row = jnp.zeros((rows, width), jnp.int32)
    lane = lax.broadcasted_iota(jnp.int32, start_ref.shape, 1)
    listed = jnp.zeros(start_ref.shape, jnp.int32)
    for o in range(peers):
        part = slice(o * rows, (o + 1) * rows)
        before = jnp.dot(row_before, totals[part].astype(BF16), preferred_element_type=F32)
        rank = rank + jnp.where(owner == o, within[part] + before, 0.0)
        slot_row = slot_row + jnp.where(owner == o, start, 0)
        listed = jnp.where(lane == o, start[:, 0:LANES], listed)
        count = jnp.sum(totals[part], axis=0, keepdims=True).astype(jnp.int32)
        starts.append(start)
        counts.append(count)
        start = start + (count + (LANES - 1)) // LANES
    start_ref[...] = listed
    rank = rank.astype(jnp.int32)
    slot_row = slot_row + rank // LANES
    slot_column = rank % LANES
    source = folded[0]
    target = folded[2]
    payloads = [
        wide(source // width),
        wide(source % width),
        wide(target // width),
        wide(target % width),
    ]
    row_number = lax.broadcasted_iota(jnp.int32, (slots, width), 0)
    column_number = lax.broadcasted_iota(jnp.int32, (LANES, width), 0)
    total = jnp.zeros(products.shape, F32)
    for r in range(rows):
        in_row = row_number == slot_row[r : r + 1]
        left = jnp.concatenate(
            [
                jnp.where(in_row, payload, 0.0).astype(BF16)
                for payload in [payload[r : r + 1] for payload in payloads]
                + [
                    wide(block_ref[c, d : d + 1, r * width : (r + 1) * width])
                    for c in range(3)
                    for d in range(3)
                ]
            ],
            axis=0,
        )
        right = jnp.where(column_number == slot_column[r : r + 1], 1.0, 0.0).astype(BF16)
        total = total + lax.dot_general(
            left, right, (((1,), (1,)), ((), ())), preferred_element_type=F32
        )
    products[...] = total
    slot_source_ref[...] = (products[0:slots] * width + products[slots : 2 * slots]).astype(jnp.int32)
    packed[...] = jnp.zeros(packed.shape, F32)
    packed[0:slots] = products[2 * slots : 3 * slots] * width + products[3 * slots : 4 * slots]
    at_lane = lax.broadcasted_iota(jnp.int32, (1, LANES), 1)
    nowhere = float(cells)
    for o in range(peers):
        first = starts[o][0, 0]
        for i in range(per_peer):
            row = packed[pl.ds(first + i, 1), :]
            slot_target_ref[o * per_peer + i : o * per_peer + i + 1] = jnp.where(
                at_lane + i * LANES < counts[o][:, 0:LANES], row, nowhere
            )
    for c in range(3):
        for d in range(3):
            at = 4 + c * 3 + d
            slot_block_ref[c, d] = products[at * slots : (at + 1) * slots]


def setup_kernel(
    peers,
    right_hbm, pivot_hbm, lower_hbm, upper_hbm, active_hbm,
    from_hbm, owner_hbm, target_hbm, block_hbm,
    edge_ref, next_ref, alone_ref, from_above_ref, from_below_ref, matrix_ref,
    slot_block_ref, slot_source_ref, slot_target_ref, start_ref, mask_ref,
    right_ref, pivot_ref, lower_ref, upper_ref, active_ref,
    from_ref, owner_ref, target_ref, block_ref,
    stacked, products, packed, folded, semaphores,
):
    copies = [
        pltpu.make_async_copy(source, landing, semaphores.at[number])
        for number, (source, landing) in enumerate(
            [
                (lower_hbm, lower_ref),
                (upper_hbm, upper_ref),
                (active_hbm, active_ref),
                (pivot_hbm, pivot_ref),
                (right_hbm, right_ref),
                (owner_hbm, owner_ref),
                (from_hbm, from_ref),
                (target_hbm, target_ref),
                (block_hbm, block_ref),
            ]
        )
    ]
    for copy in copies:
        copy.start()
    for copy in copies:
        copy.wait()
    section_part(
        right_ref, pivot_ref, lower_ref, upper_ref, active_ref,
        edge_ref, next_ref, alone_ref, from_above_ref, from_below_ref, matrix_ref,
    )
    mask_ref[...] = wide(active_ref[...])
    rows, width = folded.shape[1:]
    for r in range(rows):
        for number, ref in enumerate((from_ref, owner_ref, target_ref)):
            folded[number, r : r + 1] = ref[0:1, r * width : (r + 1) * width]
    routing_part(
        peers, active_ref.size, folded, block_ref,
        slot_block_ref, slot_source_ref, slot_target_ref, start_ref, stacked, products, packed,
    )


def couple_kernel(
    first, sections, *refs,
):
    turned, refs = refs[: sections - 1], refs[sections - 1 :]
    if first:
        own_ref, refs = refs[0], refs[1:]
        edge_ref = refs[-1]
        refs = refs[:-1]
    else:
        edge_ref, refs = refs[0], refs[1:]
    (
        matrix_ref, alone_ref, above_ref, below_ref, active_ref,
        slot_block_ref, slot_source_ref, slot_target_ref, start_ref,
        solved_ref, layer_ref, sent_ref, arriving, tops, borders, table, packed,
    ) = refs
    layers, rows = alone_ref.shape[1], alone_ref.shape[2]
    width = alone_ref.shape[3]
    peers = sent_ref.shape[0]
    slots = slot_source_ref.shape[0]
    per_peer = slot_target_ref.shape[0] // peers
    capacity = per_peer * LANES
    s = lax.axis_index("layer")
    a = lax.axis_index("areal")
    if first:
        edge_ref[s] = own_ref[0 : 6 * rows]
        for turn in range(1, sections):
            edge_ref[lax.rem(s - turn + sections, sections)] = turned[turn - 1][0 : 6 * rows]

    def matrix(section, which):
        return [
            [
                matrix_ref[section, (which * 9 + c * 3 + d) * rows : (which * 9 + c * 3 + d + 1) * rows]
                for d in range(3)
            ]
            for c in range(3)
        ]

    def edge(section, which):
        return [
            edge_ref[section, (which * 3 + c) * rows : (which * 3 + c + 1) * rows] for c in range(3)
        ]

    zero = jnp.zeros((rows, width), F32)
    coming = [[zero] * 3]
    for section in range(1, sections):
        value = edge(section - 1, 0)
        if section > 1:
            value = plus(value, times(matrix(section - 1, 0), coming[section - 1]))
        coming.append(value)
    rising = [None] * sections + [[zero] * 3]
    for section in range(sections - 1, 0, -1):
        value = plus(edge(section, 1), times(matrix(section, 1), coming[section]))
        if section < sections - 1:
            value = plus(value, times(matrix(section, 2), rising[section + 1]))
        rising[section] = value
    rising[0] = [zero] * 3
    for section in range(sections):
        for c in range(3):
            arriving[section, c] = coming[section][c]
            tops[section, c] = rising[section + 1][c]
    above = [arriving[s, c] for c in range(3)]
    below = [tops[s, c] for c in range(3)]
    active = [wide(active_ref[k]) for k in range(layers)]
    for k in range(layers):
        for c in range(3):
            value = alone_ref[c, k]
            for d in range(3):
                value = value + above_ref[c, d, k] * above[d] + below_ref[c, d, k] * below[d]
            solved_ref[c, k] = value
            held = value * active[k]
            table[c, k * rows : (k + 1) * rows] = held
            borders[0, c * layers + k : c * layers + k + 1] = held[0:1]
            borders[1, c * layers + k : c * layers + k + 1] = held[rows - 1 : rows]
    previous, following = turned[0], turned[-1]
    bottom = [
        [previous[(6 + c * 3 + d) * rows : (7 + c * 3 + d) * rows] for d in range(3)]
        for c in range(3)
    ]
    own_top = [solved_ref[c, 0] for c in range(3)]
    upstairs = minus(above, times(bottom, own_top))
    upper_active = jnp.where(s > 0, previous[15 * rows : 16 * rows], 0.0)
    lower_active = jnp.where(s < sections - 1, following[6 * rows : 7 * rows], 0.0)
    for c in range(3):
        layer_ref[0, c] = upstairs[c] * upper_active
        layer_ref[1, c] = below[c] * lower_active
    starts = start_ref[...]
    packed[...] = jnp.zeros(packed.shape, F32)
    for g in range(slots // 8):
        group = slice(g * 8, (g + 1) * 8)
        source = slot_source_ref[group]
        line = source // LANES
        lane = source % LANES
        found = [jnp.zeros((8, LANES), F32)] * 3
        for r in range(layers * rows):
            for q in range(width // LANES):
                here = line == r * (width // LANES) + q
                for c in range(3):
                    row = jnp.broadcast_to(
                        table[c, r : r + 1, q * LANES : (q + 1) * LANES], (8, LANES)
                    )
                    picked = jnp.take_along_axis(row, lane, axis=1)
                    found[c] = jnp.where(here, picked, found[c])
        for c in range(3):
            value = slot_block_ref[c, 0, group] * found[0]
            for d in range(1, 3):
                value = value + slot_block_ref[c, d, group] * found[d]
            packed[c, group] = value
    for peer in range(peers):
        start = starts[0, peer]
        for i in range(per_peer):
            for c in range(3):
                at = c * capacity + i * LANES
                sent_ref[peer, 0:1, at : at + LANES] = packed[c, pl.ds(start + i, 1), :]
    base = 3 * capacity
    many = 3 * layers
    if not first:
        sums = edge_ref[0, 6 * rows : 6 * rows + 1, 0:LANES]
        for section in range(1, sections):
            sums = sums + edge_ref[section, 6 * rows : 6 * rows + 1, 0:LANES]
    for peer in range(peers):
        side = jnp.where(peer > a, 1, 0)
        for i in range(many):
            start = base + i * width
            sent_ref[peer, 0:1, start : start + width] = borders[side, i : i + 1]
        start = base + many * width
        if not first:
            sent_ref[peer, 0:1, start : start + LANES] = sums
        else:
            for i in range(per_peer):
                at = peer * per_peer + i
                sent_ref[peer, 0:1, start + i * LANES : start + (i + 1) * LANES] = slot_target_ref[
                    at : at + 1
                ]


def weights_of(sums, upto):
    def value(step, at):
        row = jnp.broadcast_to(sums[step : step + 1], (8, 128))
        return jnp.take_along_axis(row, jnp.full((8, 128), at, jnp.int32), axis=1)

    squared = value(0, 0)
    beta = jnp.sqrt(squared + TINY)
    unscale = 1.0 / beta
    gram = [[squared * unscale * unscale]]
    columns = []
    lengths = []
    for step in range(upto):
        if step == 0:
            weights = [value(0, 1) * unscale * unscale]
            own = value(0, 2) * unscale * unscale
        else:
            weights = [value(step, i) for i in range(step + 1)]
            own = value(step, step + 1)
        size = step + 1
        shadow = []
        for i in range(size):
            total = weights[0] * gram[i][0]
            for k in range(1, size):
                total = total + weights[k] * gram[i][k]
            shadow.append(total)
        left = own
        for i in range(size):
            left = left - weights[i] * (2.0 * weights[i] - shadow[i])
        left = jnp.maximum(left, 0.0)
        length = jnp.sqrt(left + TINY)
        inverse = 1.0 / length
        column = [(weights[i] - shadow[i]) * inverse for i in range(size)]
        for i in range(size):
            gram[i].append(column[i])
        gram.append(column + [left * inverse * inverse])
        columns.append(weights)
        lengths.append(length)
    return beta, unscale, columns, lengths


def operate_kernel(step, *refs):
    last = step == ITERS - 1
    got_ref, solved_ref, layer_ref, diag_ref, coupling_ref, active_ref = refs[:6]
    at = 6
    if step > 0:
        hot_row_ref, hot_column_ref = refs[6:8]
        at = 8
    if not last:
        pivot_ref, lower_ref, upper_ref = refs[at : at + 3]
        at += 3
    right_ref = refs[at]
    at += 1
    if step > 0:
        sums_ref = refs[at]
        at += 1
        earlier = []
        for i in range(step):
            earlier.append(refs[at : at + (2 if i == 0 else 3)])
            at += len(earlier[-1])
    outs = refs[at:]
    layers, rows, width = solved_ref.shape[1:]
    peers = got_ref.shape[0]
    per_peer = layers * rows // peers
    base = 3 * per_peer * width
    many = 3 * layers
    ending = base + many * width
    cells = layers * rows
    a = lax.axis_index("areal")
    total_ref = outs[-1]
    outs = outs[:-1]
    if step == 0:
        lines_ref = outs[-1]
        hot_row_ref, hot_column_ref = outs[-3:-1]
        outs = outs[:-3]

    capacity = per_peer * width
    if step == 0:
        for peer in range(peers):
            for i in range(per_peer):
                at = peer * per_peer + i
                lines_ref[at : at + 1] = got_ref[
                    peer, 0:1, ending + i * width : ending + (i + 1) * width
                ]
        where = lines_ref[...].astype(jnp.int32)
        upright = jnp.transpose(wide(where % width))
        upper = where // width
        row_number = lax.broadcasted_iota(jnp.int32, (cells, width), 0)
        column_number = wide(lax.broadcasted_iota(jnp.int32, (width, width), 1))
        for peer in range(peers):
            for i in range(per_peer):
                at = peer * per_peer + i
                hot_column_ref[peer, i * width : (i + 1) * width] = jnp.where(
                    column_number == upright[:, at : at + 1], 1.0, 0.0
                ).astype(BF16)
                hot_row_ref[peer, :, i * width : (i + 1) * width] = jnp.where(
                    row_number == upper[at : at + 1], 1.0, 0.0
                ).astype(BF16)
    added = None
    for peer in range(peers):
        hot = hot_row_ref[peer]
        pieces = []
        for c in range(3):
            rest = got_ref[peer, 0:1, c * capacity : (c + 1) * capacity]
            for part in range(PARTS):
                piece = rest.astype(BF16)
                rest = rest - wide(piece)
                pieces.append(hot * jnp.broadcast_to(piece, hot.shape))
        product = jnp.dot(
            jnp.concatenate(pieces, axis=0), hot_column_ref[peer], preferred_element_type=F32
        )
        added = product if added is None else added + product
    total_ref[...] = added

    active = [wide(active_ref[k]) for k in range(layers)]
    held = [[solved_ref[c, k] * active[k] for c in range(3)] for k in range(layers)]
    row_at = lax.broadcasted_iota(jnp.int32, (rows, width), 0)
    column_at = lax.broadcasted_iota(jnp.int32, (rows, width), 1)
    before, after = jnp.maximum(a - 1, 0), jnp.minimum(a + 1, peers - 1)
    has_before = jnp.where(a > 0, 1.0, 0.0)
    has_after = jnp.where(a < peers - 1, 1.0, 0.0)
    applied = []
    for k in range(layers):
        beside = []
        beside.append(held[k - 1] if k > 0 else [layer_ref[0, c] for c in range(3)])
        beside.append(held[k + 1] if k < layers - 1 else [layer_ref[1, c] for c in range(3)])
        sides = [[], [], [], []]
        for c in range(3):
            border = base + (c * layers + k) * width
            low = got_ref[before, 0:1, border : border + width] * has_before
            high = got_ref[after, 0:1, border : border + width] * has_after
            value = held[k][c]
            sides[0].append(jnp.where(row_at == 0, low, pltpu.roll(value, 1, 0)))
            sides[1].append(jnp.where(row_at == rows - 1, high, pltpu.roll(value, rows - 1, 0)))
            sides[2].append(jnp.where(column_at == 0, 0.0, pltpu.roll(value, 1, 1)))
            sides[3].append(jnp.where(column_at == width - 1, 0.0, pltpu.roll(value, width - 1, 1)))
        result = times(block_at(diag_ref, k), held[k])
        for d, neighbour in enumerate(beside + sides):
            blocks = [[wide(coupling_ref[d, i, j, k]) for j in range(3)] for i in range(3)]
            result = plus(result, times(blocks, neighbour))
        for c in range(3):
            for part in range(PARTS):
                start = (c * PARTS + part) * cells + k * rows
                result[c] = result[c] + total_ref[start : start + rows]
        applied.append(
            [
                active[k] * result[c] + (1.0 - active[k]) * solved_ref[c, k]
                for c in range(3)
            ]
        )

    pairs = []
    if step == 0:
        (applied_ref, edge_ref, alone_ref) = outs
        for k in range(layers):
            for c in range(3):
                applied_ref[c, k] = applied[k][c]
        new = applied
        r = [[right_ref[c, k] for c in range(3)] for k in range(layers)]
        pairs = [(r, r), (r, applied), (applied, applied)]
    else:
        if last:
            (z_ref, edge_ref, history_ref) = outs
        else:
            (v_ref, z_ref, w_ref, edge_ref, alone_ref, history_ref) = outs
        fresh = got_ref[0, 0:1, ending : ending + 128]
        for peer in range(1, peers):
            fresh = fresh + got_ref[peer, 0:1, ending : ending + 128]
        history_row = lax.broadcasted_iota(jnp.int32, history_ref.shape, 0)
        sums = jnp.where(history_row == step - 1, fresh, sums_ref[...])
        history_ref[...] = sums
        beta, unscale, columns, lengths = weights_of(sums, step)
        weights = columns[-1]
        inverse = 1.0 / lengths[-1]
        spread = lambda value: jnp.concatenate([value] * (width // 128), axis=1)
        lead = spread(inverse * unscale if step == 1 else inverse)
        factors = [spread(weights[i] * inverse * (unscale if i == 0 else 1.0)) for i in range(step)]
        new = []
        members = []
        v_all = [[] for _ in range(step)]
        for k in range(layers):
            new.append([])
            members.append([])
            for c in range(3):
                old_v = [right_ref[c, k]] + [earlier[i][0][c, k] for i in range(1, step)]
                old_z = [earlier[0][0][c, k]] + [earlier[i][1][c, k] for i in range(1, step)]
                old_w = [earlier[0][1][c, k]] + [earlier[i][2][c, k] for i in range(1, step)]
                v = old_w[-1] * lead
                z = solved_ref[c, k] * lead
                w = applied[k][c] * lead
                for i in range(step):
                    v = v - factors[i] * old_v[i]
                    z = z - factors[i] * old_z[i]
                    w = w - factors[i] * old_w[i]
                z_ref[c, k] = z
                if not last:
                    v_ref[c, k] = v
                    w_ref[c, k] = w
                new[k].append(w)
                members[k].append(v)
        first = spread(unscale)
        basis = [[[right_ref[c, k] * first for c in range(3)] for k in range(layers)]]
        for i in range(1, step):
            basis.append([[earlier[i][0][c, k] for c in range(3)] for k in range(layers)])
        basis.append(members)
        pairs = [(member, new) for member in basis] + [(new, new)]

    edge_ref[...] = jnp.zeros(edge_ref.shape, F32)
    lane = lax.broadcasted_iota(jnp.int32, (1, 128), 1)
    line = jnp.zeros((1, 128), F32)
    for number, (left, right) in enumerate(pairs):
        total = jnp.zeros((rows, width), F32)
        for k in range(layers):
            for c in range(3):
                total = total + left[k][c] * right[k][c]
        total = jnp.sum(jnp.sum(total, axis=0, keepdims=True), axis=1, keepdims=True)
        line = jnp.where(lane == number, total, line)
    if last:
        for peer in range(edge_ref.shape[0]):
            edge_ref[peer] = line
    else:
        edge_ref[6 * rows : 6 * rows + 1, 0:128] = line
        lowest, alone = local_sweeps(new, pivot_ref, lower_ref, upper_ref, layers)
        for c in range(3):
            edge_ref[c * rows : (c + 1) * rows] = lowest[c]
            edge_ref[(3 + c) * rows : (4 + c) * rows] = alone[0][c]
            for k in range(layers):
                alone_ref[c, k] = alone[k][c]


def finish_kernel(dots_ref, sums_ref, z0_ref, z1_ref, z2_ref, z3_ref, update_ref, hessenberg_ref):
    z_refs = (z0_ref, z1_ref, z2_ref, z3_ref)
    rows, width = z0_ref.shape[2:]
    fresh = dots_ref[0]
    for peer in range(1, dots_ref.shape[0]):
        fresh = fresh + dots_ref[peer]
    history_row = lax.broadcasted_iota(jnp.int32, sums_ref.shape, 0)
    sums = jnp.where(history_row == ITERS - 1, fresh, sums_ref[...])
    beta, unscale, columns, lengths = weights_of(sums, ITERS)
    row_at = lax.broadcasted_iota(jnp.int32, (8, 128), 0)
    column_at = lax.broadcasted_iota(jnp.int32, (8, 128), 1)
    table = jnp.zeros((8, 128), F32)
    for j in range(ITERS):
        for i, weight in enumerate(columns[j] + [lengths[j]]):
            table = jnp.where((row_at == j) & (column_at == i), weight, table)
    hessenberg_ref[...] = table[0 : hessenberg_ref.shape[0], 0 : hessenberg_ref.shape[1]]
    goal = [beta]
    triangle = []
    rotations = []
    for j in range(ITERS):
        entries = list(columns[j])
        for i, (cosine, sine) in enumerate(rotations):
            upper, lower = entries[i], entries[i + 1]
            entries[i] = cosine * upper + sine * lower
            entries[i + 1] = cosine * lower - sine * upper
        radius = jnp.sqrt(entries[j] * entries[j] + lengths[j] * lengths[j])
        cosine, sine = entries[j] / radius, lengths[j] / radius
        rotations.append((cosine, sine))
        entries[j] = radius
        triangle.append(entries)
        leading = goal[j]
        goal[j] = cosine * leading
        goal.append(-sine * leading)
    answer = [None] * ITERS
    for i in range(ITERS - 1, -1, -1):
        partial = goal[i]
        for j in range(i + 1, ITERS):
            partial = partial - triangle[j][i] * answer[j]
        answer[i] = partial / triangle[i][i]
    factors = [
        jnp.concatenate([answer[j] * unscale if j == 0 else answer[j]] * (width // 128), axis=1)
        for j in range(ITERS)
    ]
    for c in range(3):
        for k in range(z0_ref.shape[1]):
            value = factors[0] * z_refs[0][c, k]
            for j in range(1, ITERS):
                value = value + factors[j] * z_refs[j][c, k]
            update_ref[c, k] = value


def turn(array, by):
    count = lax.axis_size("layer")
    return lax.ppermute(array, "layer", [(i, (i + by) % count) for i in range(count)])


def shape_of(*dims, kind=F32):
    return jax.ShapeDtypeStruct(dims, kind)


def local(
    right_side,
    diag_blocks,
    couplings,
    pivot_inverse,
    lower_blocks,
    upper_blocks,
    active_cells,
    link_from,
    link_owner,
    link_target,
    link_blocks,
):
    _, layers, rows, width = right_side.shape
    peers = lax.axis_size("areal")
    sections = lax.axis_size("layer")
    links = link_from.shape[1]
    capacity = 2 * links // peers
    slots = capacity * peers // width
    per_peer = slots // peers
    link_rows = links // width
    compact = -(-(links // LANES + peers) // 8) * 8
    packed_rows = compact + -(-capacity // LANES // 8) * 8
    field = shape_of(3, layers, rows, width)
    edge_rows = 7 * rows
    sent_width = (3 * per_peer + 3 * layers) * width + 128
    first_width = (4 * per_peer + 3 * layers) * width
    edge_shape = shape_of(edge_rows, width)
    hbm = pl.BlockSpec(memory_space=pltpu.HBM)
    operands = [
        right_side,
        pivot_inverse,
        lower_blocks,
        upper_blocks,
        active_cells,
        link_from,
        link_owner.reshape(1, links),
        link_target,
        link_blocks.reshape(3, 3, links),
    ]
    (
        edge, following, alone, from_above, from_below, matrices,
        slot_block, slot_source, slot_target, starts, active,
    ) = call(
        functools.partial(setup_kernel, peers),
        [
            edge_shape,
            shape_of(16 * rows, width),
            field,
            shape_of(3, 3, layers, rows, width),
            shape_of(3, 3, layers, rows, width),
            shape_of(27 * rows, width),
            shape_of(3, 3, compact, LANES),
            shape_of(compact, LANES, kind=jnp.int32),
            shape_of(capacity * peers // LANES, LANES),
            shape_of(1, LANES, kind=jnp.int32),
            shape_of(layers, rows, width),
        ],
        [pltpu.VMEM(operand.shape, operand.dtype) for operand in operands]
        + [
            pltpu.VMEM((peers * link_rows, width), BF16),
            pltpu.VMEM((13 * compact, LANES), F32),
            pltpu.VMEM((packed_rows, LANES), F32),
            pltpu.VMEM((3, link_rows, width), jnp.int32),
            pltpu.SemaphoreType.DMA((len(operands),)),
        ],
        name="setup",
        inputs=[hbm] * len(operands),
        limit=16,
    )(*[pltpu.with_memory_space_constraint(operand, pltpu.HBM) for operand in operands])
    turned = [turn(following, 1)] + [turn(edge, by) for by in range(2, sections)]
    all_matrices = lax.all_gather(matrices, "layer", axis=0, tiled=False)

    sums = jnp.zeros((8, 128), F32)
    earlier = []
    zs = []
    for step in range(ITERS):
        last = step == ITERS - 1
        scratch = [
            pltpu.VMEM((sections, 3, rows, width), F32),
            pltpu.VMEM((sections, 3, rows, width), F32),
            pltpu.VMEM((2, 16, width), F32),
            pltpu.VMEM((3, layers * rows, width), F32),
            pltpu.VMEM((3, packed_rows, LANES), F32),
        ]
        if step == 0:
            edges = edge
            scratch.append(pltpu.VMEM((sections, 6 * rows, width), F32))
        else:
            edges = lax.all_gather(edge, "layer", axis=0, tiled=False)
        solved, layer_sides, sent = call(
            functools.partial(couple_kernel, step == 0, sections),
            [
                field,
                shape_of(2, 3, rows, width),
                shape_of(peers, 1, first_width if step == 0 else sent_width),
            ],
            scratch,
            name="couple",
        )(
            *turned, edges, all_matrices, alone, from_above, from_below, active,
            slot_block, slot_source, slot_target, starts,
        )
        got = lax.all_to_all(sent, "areal", split_axis=0, concat_axis=0, tiled=True)
        operands = [got, solved, layer_sides, diag_blocks, couplings, active]
        if step > 0:
            operands += [hot_row, hot_column]
        if not last:
            operands += [pivot_inverse, lower_blocks, upper_blocks]
        operands.append(right_side)
        if step > 0:
            operands.append(sums)
            for group in earlier:
                operands += list(group)
        history = shape_of(8, 128)
        if step == 0:
            outs = [
                field,
                edge_shape,
                field,
                shape_of(peers, layers * rows, capacity, kind=BF16),
                shape_of(peers, capacity, width, kind=BF16),
            ]
        elif last:
            outs = [field, shape_of(peers * sections, 1, 128), history]
        else:
            outs = [field, field, field, edge_shape, field, history]
        results = call(
            functools.partial(operate_kernel, step),
            outs,
            ([pltpu.VMEM((slots, width), F32)] if step == 0 else [])
            + [pltpu.VMEM((3 * PARTS * layers * rows, width), F32)],
            name="operate",
        )(*operands)
        if step == 0:
            applied, edge, alone, hot_row, hot_column = results
            earlier.append((solved, applied))
            zs.append(solved)
        elif last:
            z, dots, sums = results
            zs.append(z)
        else:
            v, z, w, edge, alone, sums = results
            earlier.append((v, z, w))
            zs.append(z)
    dots = lax.all_to_all(dots, ("areal", "layer"), split_axis=0, concat_axis=0, tiled=True)
    update, hessenberg = call(
        finish_kernel, [field, shape_of(ITERS, ITERS + 1)], name="finish"
    )(dots, sums, *zs)
    return update, hessenberg.T


def solution(mesh):
    placed = (
        P(None, "layer", "areal", None),
        P(None, None, "layer", "areal", None),
        P(None, None, None, "layer", "areal", None),
        P(None, None, "layer", "areal", None),
        P(None, None, "layer", "areal", None),
        P(None, None, "layer", "areal", None),
        P("layer", "areal", None),
        P("layer", "areal"),
        P("layer", "areal", None),
        P("layer", "areal"),
        P(None, None, "layer", "areal"),
    )
    return jax.shard_map(
        local,
        mesh=mesh,
        in_specs=placed,
        out_specs=(P(None, "layer", "areal", None), P()),
        check_vma=False,
    )
```

```python
import functools

import jax
import jax.numpy as jnp
from jax import lax
from jax.experimental import pallas as pl
from jax.experimental.pallas import tpu as pltpu
from jax.sharding import PartitionSpec as P

ITERS = 4
PARTS = 2
TINY = 1e-06
LANES = 128

F32 = jnp.float32
BF16 = jnp.bfloat16
VMEM = pl.BlockSpec(memory_space=pltpu.VMEM)


def call(kernel, outs, scratch=(), name=None, inputs=None, limit=20, flops=1 << 22, moved=1 << 20):
    many = isinstance(outs, (list, tuple))
    where = {} if inputs is None else {"in_specs": inputs}
    return pl.pallas_call(
        kernel,
        out_shape=outs,
        **where,
        out_specs=[VMEM] * len(outs) if many else VMEM,
        scratch_shapes=list(scratch),
        compiler_params=pltpu.CompilerParams(vmem_limit_bytes=limit << 20),
        cost_estimate=pl.CostEstimate(flops=flops, bytes_accessed=moved, transcendentals=0),
        name=name,
    )


def wide(value):
    return value.astype(F32)


def times(blocks, vector):
    result = []
    for row in blocks:
        total = row[0] * vector[0]
        for entry, element in zip(row[1:], vector[1:]):
            total = total + entry * element
        result.append(total)
    return result


def block_at(ref, layer):
    return [[wide(ref[c, d, layer]) for d in range(3)] for c in range(3)]


def minus(left, right):
    return [a - b for a, b in zip(left, right)]


def plus(left, right):
    return [a + b for a, b in zip(left, right)]


def local_sweeps(planes, pivot, lower, upper, layers):
    forward = []
    previous = None
    for k in range(layers):
        current = times(block_at(pivot, k), planes[k])
        if previous is not None:
            current = minus(current, times(block_at(lower, k), previous))
        forward.append(current)
        previous = current
    backward = [None] * layers
    previous = None
    for k in range(layers - 1, -1, -1):
        current = forward[k]
        if previous is not None:
            current = minus(current, times(block_at(upper, k), previous))
        backward[k] = current
        previous = current
    return forward[layers - 1], backward


def section_part(
    right_ref, pivot_ref, lower_ref, upper_ref, active_ref,
    edge_ref, next_ref, alone_ref, from_above_ref, from_below_ref, matrix_ref,
):
    layers, rows = right_ref.shape[1], right_ref.shape[2]
    planes = [[right_ref[c, k] for c in range(3)] for k in range(layers)]
    lowest, solved = local_sweeps(planes, pivot_ref, lower_ref, upper_ref, layers)
    for c in range(3):
        for ref in (edge_ref, next_ref):
            ref[c * rows : (c + 1) * rows] = lowest[c]
            ref[(3 + c) * rows : (4 + c) * rows] = solved[0][c]
        for k in range(layers):
            alone_ref[c, k] = solved[k][c]
    for d in range(3):
        carried = []
        previous = None
        for k in range(layers):
            blocks = block_at(lower_ref, k)
            if previous is None:
                previous = [-blocks[c][d] for c in range(3)]
            else:
                previous = [-value for value in times(blocks, previous)]
            carried.append(previous)
        for c in range(3):
            matrix_ref[(c * 3 + d) * rows : (c * 3 + d + 1) * rows] = carried[-1][c]
        response = carried[-1]
        for k in range(layers - 1, -1, -1):
            if k < layers - 1:
                response = minus(carried[k], times(block_at(upper_ref, k), response))
            for c in range(3):
                from_above_ref[c, d, k] = response[c]
        for c in range(3):
            matrix_ref[(9 + c * 3 + d) * rows : (10 + c * 3 + d) * rows] = response[c]
        response = None
        for k in range(layers - 1, -1, -1):
            blocks = block_at(upper_ref, k)
            if response is None:
                for c in range(3):
                    next_ref[(6 + c * 3 + d) * rows : (7 + c * 3 + d) * rows] = blocks[c][d]
                response = [-blocks[c][d] for c in range(3)]
            else:
                response = [-value for value in times(blocks, response)]
            for c in range(3):
                from_below_ref[c, d, k] = response[c]
        for c in range(3):
            matrix_ref[(18 + c * 3 + d) * rows : (19 + c * 3 + d) * rows] = response[c]
    edge_ref[6 * rows : 7 * rows] = wide(active_ref[0])
    next_ref[15 * rows : 16 * rows] = wide(active_ref[layers - 1])


def routing_part(
    peers, cells, folded, block_ref,
    slot_block_ref, slot_source_ref, slot_target_ref, start_ref, stacked, products, packed,
):
    rows, width = folded.shape[1:]
    slots = slot_source_ref.shape[0]
    per_peer = slot_target_ref.shape[0] // peers
    owner = folded[1]
    for o in range(peers):
        stacked[o * rows : (o + 1) * rows] = jnp.where(owner == o, 1.0, 0.0).astype(BF16)
    chosen = stacked[...]
    ones_before = jnp.where(
        lax.broadcasted_iota(jnp.int32, (width, width), 0)
        < lax.broadcasted_iota(jnp.int32, (width, width), 1),
        1.0,
        0.0,
    ).astype(BF16)
    within = jnp.dot(chosen, ones_before, preferred_element_type=F32)
    totals = jnp.dot(chosen, jnp.ones((width, width), BF16), preferred_element_type=F32)
    row_before = jnp.where(
        lax.broadcasted_iota(jnp.int32, (rows, rows), 1)
        < lax.broadcasted_iota(jnp.int32, (rows, rows), 0),
        1.0,
        0.0,
    ).astype(BF16)
    rank = jnp.zeros((rows, width), F32)
    start = jnp.zeros((1, width), jnp.int32)
    starts, counts = [], []
    slot_row = jnp.zeros((rows, width), jnp.int32)
    lane = lax.broadcasted_iota(jnp.int32, start_ref.shape, 1)
    listed = jnp.zeros(start_ref.shape, jnp.int32)
    for o in range(peers):
        part = slice(o * rows, (o + 1) * rows)
        before = jnp.dot(row_before, totals[part].astype(BF16), preferred_element_type=F32)
        rank = rank + jnp.where(owner == o, within[part] + before, 0.0)
        slot_row = slot_row + jnp.where(owner == o, start, 0)
        listed = jnp.where(lane == o, start[:, 0:LANES], listed)
        count = jnp.sum(totals[part], axis=0, keepdims=True).astype(jnp.int32)
        starts.append(start)
        counts.append(count)
        start = start + (count + (LANES - 1)) // LANES
    start_ref[...] = listed
    rank = rank.astype(jnp.int32)
    slot_row = slot_row + rank // LANES
    slot_column = rank % LANES
    source = folded[0]
    target = folded[2]
    payloads = [
        wide(source // width),
        wide(source % width),
        wide(target // width),
        wide(target % width),
    ]
    row_number = lax.broadcasted_iota(jnp.int32, (slots, width), 0)
    column_number = lax.broadcasted_iota(jnp.int32, (LANES, width), 0)
    total = jnp.zeros(products.shape, F32)
    for r in range(rows):
        in_row = row_number == slot_row[r : r + 1]
        left = jnp.concatenate(
            [
                jnp.where(in_row, payload, 0.0).astype(BF16)
                for payload in [payload[r : r + 1] for payload in payloads]
                + [
                    wide(block_ref[c, d : d + 1, r * width : (r + 1) * width])
                    for c in range(3)
                    for d in range(3)
                ]
            ],
            axis=0,
        )
        right = jnp.where(column_number == slot_column[r : r + 1], 1.0, 0.0).astype(BF16)
        total = total + lax.dot_general(
            left, right, (((1,), (1,)), ((), ())), preferred_element_type=F32
        )
    products[...] = total
    slot_source_ref[...] = (products[0:slots] * width + products[slots : 2 * slots]).astype(jnp.int32)
    packed[...] = jnp.zeros(packed.shape, F32)
    packed[0:slots] = products[2 * slots : 3 * slots] * width + products[3 * slots : 4 * slots]
    at_lane = lax.broadcasted_iota(jnp.int32, (1, LANES), 1)
    nowhere = float(cells)
    for o in range(peers):
        first = starts[o][0, 0]
        for i in range(per_peer):
            row = packed[pl.ds(first + i, 1), :]
            slot_target_ref[o * per_peer + i : o * per_peer + i + 1] = jnp.where(
                at_lane + i * LANES < counts[o][:, 0:LANES], row, nowhere
            )
    for c in range(3):
        for d in range(3):
            at = 4 + c * 3 + d
            slot_block_ref[c, d] = products[at * slots : (at + 1) * slots]


def setup_kernel(
    peers,
    right_hbm, pivot_hbm, lower_hbm, upper_hbm, active_hbm,
    from_hbm, owner_hbm, target_hbm, block_hbm,
    edge_ref, next_ref, alone_ref, from_above_ref, from_below_ref, matrix_ref,
    slot_block_ref, slot_source_ref, slot_target_ref, start_ref, mask_ref,
    right_ref, pivot_ref, lower_ref, upper_ref, active_ref,
    from_ref, owner_ref, target_ref, block_ref,
    stacked, products, packed, folded, semaphores,
):
    copies = [
        pltpu.make_async_copy(source, landing, semaphores.at[number])
        for number, (source, landing) in enumerate(
            [
                (lower_hbm, lower_ref),
                (upper_hbm, upper_ref),
                (active_hbm, active_ref),
                (pivot_hbm, pivot_ref),
                (right_hbm, right_ref),
                (owner_hbm, owner_ref),
                (from_hbm, from_ref),
                (target_hbm, target_ref),
                (block_hbm, block_ref),
            ]
        )
    ]
    for copy in copies:
        copy.start()
    for copy in copies:
        copy.wait()
    section_part(
        right_ref, pivot_ref, lower_ref, upper_ref, active_ref,
        edge_ref, next_ref, alone_ref, from_above_ref, from_below_ref, matrix_ref,
    )
    mask_ref[...] = wide(active_ref[...])
    rows, width = folded.shape[1:]
    for r in range(rows):
        for number, ref in enumerate((from_ref, owner_ref, target_ref)):
            folded[number, r : r + 1] = ref[0:1, r * width : (r + 1) * width]
    routing_part(
        peers, active_ref.size, folded, block_ref,
        slot_block_ref, slot_source_ref, slot_target_ref, start_ref, stacked, products, packed,
    )


def couple_kernel(
    first, sections, *refs,
):
    turned, refs = refs[: sections - 1], refs[sections - 1 :]
    own_ref, refs = refs[0], refs[1:]
    moved = turned
    if not first:
        moved, refs = refs[: sections - 1], refs[sections - 1 :]
    edge_ref = refs[-1]
    refs = refs[:-1]
    (
        matrix_ref, alone_ref, above_ref, below_ref, active_ref,
        slot_block_ref, slot_source_ref, slot_target_ref, start_ref,
        solved_ref, layer_ref, sent_ref, arriving, tops, borders, table, packed,
    ) = refs
    layers, rows = alone_ref.shape[1], alone_ref.shape[2]
    width = alone_ref.shape[3]
    peers = sent_ref.shape[0]
    slots = slot_source_ref.shape[0]
    per_peer = slot_target_ref.shape[0] // peers
    capacity = per_peer * LANES
    s = lax.axis_index("layer")
    a = lax.axis_index("areal")
    edge_ref[s] = own_ref[0 : 7 * rows]
    for turn in range(1, sections):
        edge_ref[lax.rem(s - turn + sections, sections)] = moved[turn - 1][0 : 7 * rows]

    def matrix(section, which):
        return [
            [
                matrix_ref[section, (which * 9 + c * 3 + d) * rows : (which * 9 + c * 3 + d + 1) * rows]
                for d in range(3)
            ]
            for c in range(3)
        ]

    def edge(section, which):
        return [
            edge_ref[section, (which * 3 + c) * rows : (which * 3 + c + 1) * rows] for c in range(3)
        ]

    zero = jnp.zeros((rows, width), F32)
    coming = [[zero] * 3]
    for section in range(1, sections):
        value = edge(section - 1, 0)
        if section > 1:
            value = plus(value, times(matrix(section - 1, 0), coming[section - 1]))
        coming.append(value)
    rising = [None] * sections + [[zero] * 3]
    for section in range(sections - 1, 0, -1):
        value = plus(edge(section, 1), times(matrix(section, 1), coming[section]))
        if section < sections - 1:
            value = plus(value, times(matrix(section, 2), rising[section + 1]))
        rising[section] = value
    rising[0] = [zero] * 3
    for section in range(sections):
        for c in range(3):
            arriving[section, c] = coming[section][c]
            tops[section, c] = rising[section + 1][c]
    above = [arriving[s, c] for c in range(3)]
    below = [tops[s, c] for c in range(3)]
    active = [wide(active_ref[k]) for k in range(layers)]
    for k in range(layers):
        for c in range(3):
            value = alone_ref[c, k]
            for d in range(3):
                value = value + above_ref[c, d, k] * above[d] + below_ref[c, d, k] * below[d]
            solved_ref[c, k] = value
            held = value * active[k]
            table[c, k * rows : (k + 1) * rows] = held
            borders[0, c * layers + k : c * layers + k + 1] = held[0:1]
            borders[1, c * layers + k : c * layers + k + 1] = held[rows - 1 : rows]
    previous, following = turned[0], turned[-1]
    bottom = [
        [previous[(6 + c * 3 + d) * rows : (7 + c * 3 + d) * rows] for d in range(3)]
        for c in range(3)
    ]
    own_top = [solved_ref[c, 0] for c in range(3)]
    upstairs = minus(above, times(bottom, own_top))
    upper_active = jnp.where(s > 0, previous[15 * rows : 16 * rows], 0.0)
    lower_active = jnp.where(s < sections - 1, following[6 * rows : 7 * rows], 0.0)
    for c in range(3):
        layer_ref[0, c] = upstairs[c] * upper_active
        layer_ref[1, c] = below[c] * lower_active
    starts = start_ref[...]
    packed[...] = jnp.zeros(packed.shape, F32)
    for g in range(slots // 8):
        group = slice(g * 8, (g + 1) * 8)
        source = slot_source_ref[group]
        line = source // LANES
        lane = source % LANES
        found = [jnp.zeros((8, LANES), F32)] * 3
        for r in range(layers * rows):
            for q in range(width // LANES):
                here = line == r * (width // LANES) + q
                for c in range(3):
                    row = jnp.broadcast_to(
                        table[c, r : r + 1, q * LANES : (q + 1) * LANES], (8, LANES)
                    )
                    picked = jnp.take_along_axis(row, lane, axis=1)
                    found[c] = jnp.where(here, picked, found[c])
        for c in range(3):
            value = slot_block_ref[c, 0, group] * found[0]
            for d in range(1, 3):
                value = value + slot_block_ref[c, d, group] * found[d]
            packed[c, group] = value
    for peer in range(peers):
        start = starts[0, peer]
        for i in range(per_peer):
            for c in range(3):
                at = c * capacity + i * LANES
                sent_ref[peer, 0:1, at : at + LANES] = packed[c, pl.ds(start + i, 1), :]
    base = 3 * capacity
    many = 3 * layers
    if not first:
        sums = edge_ref[0, 6 * rows : 6 * rows + 1, 0:LANES]
        for section in range(1, sections):
            sums = sums + edge_ref[section, 6 * rows : 6 * rows + 1, 0:LANES]
    for peer in range(peers):
        side = jnp.where(peer > a, 1, 0)
        for i in range(many):
            start = base + i * width
            sent_ref[peer, 0:1, start : start + width] = borders[side, i : i + 1]
        start = base + many * width
        if not first:
            sent_ref[peer, 0:1, start : start + LANES] = sums
        else:
            for i in range(per_peer):
                at = peer * per_peer + i
                sent_ref[peer, 0:1, start + i * LANES : start + (i + 1) * LANES] = slot_target_ref[
                    at : at + 1
                ]


def weights_of(sums, upto):
    def value(step, at):
        row = jnp.broadcast_to(sums[step : step + 1], (8, 128))
        return jnp.take_along_axis(row, jnp.full((8, 128), at, jnp.int32), axis=1)

    squared = value(0, 0)
    beta = jnp.sqrt(squared + TINY)
    unscale = 1.0 / beta
    gram = [[squared * unscale * unscale]]
    columns = []
    lengths = []
    for step in range(upto):
        if step == 0:
            weights = [value(0, 1) * unscale * unscale]
            own = value(0, 2) * unscale * unscale
        else:
            weights = [value(step, i) for i in range(step + 1)]
            own = value(step, step + 1)
        size = step + 1
        shadow = []
        for i in range(size):
            total = weights[0] * gram[i][0]
            for k in range(1, size):
                total = total + weights[k] * gram[i][k]
            shadow.append(total)
        left = own
        for i in range(size):
            left = left - weights[i] * (2.0 * weights[i] - shadow[i])
        left = jnp.maximum(left, 0.0)
        length = jnp.sqrt(left + TINY)
        inverse = 1.0 / length
        column = [(weights[i] - shadow[i]) * inverse for i in range(size)]
        for i in range(size):
            gram[i].append(column[i])
        gram.append(column + [left * inverse * inverse])
        columns.append(weights)
        lengths.append(length)
    return beta, unscale, columns, lengths


def operate_kernel(step, *refs):
    last = step == ITERS - 1
    got_ref, solved_ref, layer_ref, diag_ref, coupling_ref, active_ref = refs[:6]
    at = 6
    if step > 0:
        hot_row_ref, hot_column_ref = refs[6:8]
        at = 8
    if not last:
        pivot_ref, lower_ref, upper_ref = refs[at : at + 3]
        at += 3
    right_ref = refs[at]
    at += 1
    if step > 0:
        sums_ref = refs[at]
        at += 1
        earlier = []
        for i in range(step):
            earlier.append(refs[at : at + (2 if i == 0 else 3)])
            at += len(earlier[-1])
    outs = refs[at:]
    layers, rows, width = solved_ref.shape[1:]
    peers = got_ref.shape[0]
    per_peer = layers * rows // peers
    base = 3 * per_peer * width
    many = 3 * layers
    ending = base + many * width
    cells = layers * rows
    a = lax.axis_index("areal")
    total_ref = outs[-1]
    outs = outs[:-1]
    if step == 0:
        lines_ref = outs[-1]
        hot_row_ref, hot_column_ref = outs[-3:-1]
        outs = outs[:-3]

    capacity = per_peer * width
    if step == 0:
        for peer in range(peers):
            for i in range(per_peer):
                at = peer * per_peer + i
                lines_ref[at : at + 1] = got_ref[
                    peer, 0:1, ending + i * width : ending + (i + 1) * width
                ]
        where = lines_ref[...].astype(jnp.int32)
        upright = jnp.transpose(wide(where % width))
        upper = where // width
        row_number = lax.broadcasted_iota(jnp.int32, (cells, width), 0)
        column_number = wide(lax.broadcasted_iota(jnp.int32, (width, width), 1))
        for peer in range(peers):
            for i in range(per_peer):
                at = peer * per_peer + i
                hot_column_ref[peer, i * width : (i + 1) * width] = jnp.where(
                    column_number == upright[:, at : at + 1], 1.0, 0.0
                ).astype(BF16)
                hot_row_ref[peer, :, i * width : (i + 1) * width] = jnp.where(
                    row_number == upper[at : at + 1], 1.0, 0.0
                ).astype(BF16)
    added = None
    for peer in range(peers):
        hot = hot_row_ref[peer]
        pieces = []
        for c in range(3):
            rest = got_ref[peer, 0:1, c * capacity : (c + 1) * capacity]
            for part in range(PARTS):
                piece = rest.astype(BF16)
                rest = rest - wide(piece)
                pieces.append(hot * jnp.broadcast_to(piece, hot.shape))
        product = jnp.dot(
            jnp.concatenate(pieces, axis=0), hot_column_ref[peer], preferred_element_type=F32
        )
        added = product if added is None else added + product
    total_ref[...] = added

    active = [wide(active_ref[k]) for k in range(layers)]
    held = [[solved_ref[c, k] * active[k] for c in range(3)] for k in range(layers)]
    row_at = lax.broadcasted_iota(jnp.int32, (rows, width), 0)
    column_at = lax.broadcasted_iota(jnp.int32, (rows, width), 1)
    before, after = jnp.maximum(a - 1, 0), jnp.minimum(a + 1, peers - 1)
    has_before = jnp.where(a > 0, 1.0, 0.0)
    has_after = jnp.where(a < peers - 1, 1.0, 0.0)
    applied = []
    for k in range(layers):
        beside = []
        beside.append(held[k - 1] if k > 0 else [layer_ref[0, c] for c in range(3)])
        beside.append(held[k + 1] if k < layers - 1 else [layer_ref[1, c] for c in range(3)])
        sides = [[], [], [], []]
        for c in range(3):
            border = base + (c * layers + k) * width
            low = got_ref[before, 0:1, border : border + width] * has_before
            high = got_ref[after, 0:1, border : border + width] * has_after
            value = held[k][c]
            sides[0].append(jnp.where(row_at == 0, low, pltpu.roll(value, 1, 0)))
            sides[1].append(jnp.where(row_at == rows - 1, high, pltpu.roll(value, rows - 1, 0)))
            sides[2].append(jnp.where(column_at == 0, 0.0, pltpu.roll(value, 1, 1)))
            sides[3].append(jnp.where(column_at == width - 1, 0.0, pltpu.roll(value, width - 1, 1)))
        result = times(block_at(diag_ref, k), held[k])
        for d, neighbour in enumerate(beside + sides):
            blocks = [[wide(coupling_ref[d, i, j, k]) for j in range(3)] for i in range(3)]
            result = plus(result, times(blocks, neighbour))
        for c in range(3):
            for part in range(PARTS):
                start = (c * PARTS + part) * cells + k * rows
                result[c] = result[c] + total_ref[start : start + rows]
        applied.append(
            [
                active[k] * result[c] + (1.0 - active[k]) * solved_ref[c, k]
                for c in range(3)
            ]
        )

    pairs = []
    if step == 0:
        (applied_ref, edge_ref, alone_ref) = outs
        for k in range(layers):
            for c in range(3):
                applied_ref[c, k] = applied[k][c]
        new = applied
        r = [[right_ref[c, k] for c in range(3)] for k in range(layers)]
        pairs = [(r, r), (r, applied), (applied, applied)]
    else:
        if last:
            (z_ref, edge_ref, history_ref) = outs
        else:
            (v_ref, z_ref, w_ref, edge_ref, alone_ref, history_ref) = outs
        fresh = got_ref[0, 0:1, ending : ending + 128]
        for peer in range(1, peers):
            fresh = fresh + got_ref[peer, 0:1, ending : ending + 128]
        history_row = lax.broadcasted_iota(jnp.int32, history_ref.shape, 0)
        sums = jnp.where(history_row == step - 1, fresh, sums_ref[...])
        history_ref[...] = sums
        beta, unscale, columns, lengths = weights_of(sums, step)
        weights = columns[-1]
        inverse = 1.0 / lengths[-1]
        spread = lambda value: jnp.concatenate([value] * (width // 128), axis=1)
        lead = spread(inverse * unscale if step == 1 else inverse)
        factors = [spread(weights[i] * inverse * (unscale if i == 0 else 1.0)) for i in range(step)]
        new = []
        members = []
        v_all = [[] for _ in range(step)]
        for k in range(layers):
            new.append([])
            members.append([])
            for c in range(3):
                old_v = [right_ref[c, k]] + [earlier[i][0][c, k] for i in range(1, step)]
                old_z = [earlier[0][0][c, k]] + [earlier[i][1][c, k] for i in range(1, step)]
                old_w = [earlier[0][1][c, k]] + [earlier[i][2][c, k] for i in range(1, step)]
                v = old_w[-1] * lead
                z = solved_ref[c, k] * lead
                w = applied[k][c] * lead
                for i in range(step):
                    v = v - factors[i] * old_v[i]
                    z = z - factors[i] * old_z[i]
                    w = w - factors[i] * old_w[i]
                z_ref[c, k] = z
                if not last:
                    v_ref[c, k] = v
                    w_ref[c, k] = w
                new[k].append(w)
                members[k].append(v)
        first = spread(unscale)
        basis = [[[right_ref[c, k] * first for c in range(3)] for k in range(layers)]]
        for i in range(1, step):
            basis.append([[earlier[i][0][c, k] for c in range(3)] for k in range(layers)])
        basis.append(members)
        pairs = [(member, new) for member in basis] + [(new, new)]

    edge_ref[...] = jnp.zeros(edge_ref.shape, F32)
    lane = lax.broadcasted_iota(jnp.int32, (1, 128), 1)
    line = jnp.zeros((1, 128), F32)
    for number, (left, right) in enumerate(pairs):
        total = jnp.zeros((rows, width), F32)
        for k in range(layers):
            for c in range(3):
                total = total + left[k][c] * right[k][c]
        total = jnp.sum(jnp.sum(total, axis=0, keepdims=True), axis=1, keepdims=True)
        line = jnp.where(lane == number, total, line)
    if last:
        for peer in range(edge_ref.shape[0]):
            edge_ref[peer] = line
    else:
        edge_ref[6 * rows : 6 * rows + 1, 0:128] = line
        lowest, alone = local_sweeps(new, pivot_ref, lower_ref, upper_ref, layers)
        for c in range(3):
            edge_ref[c * rows : (c + 1) * rows] = lowest[c]
            edge_ref[(3 + c) * rows : (4 + c) * rows] = alone[0][c]
            for k in range(layers):
                alone_ref[c, k] = alone[k][c]


def finish_kernel(dots_ref, sums_ref, z0_ref, z1_ref, z2_ref, z3_ref, update_ref, hessenberg_ref):
    z_refs = (z0_ref, z1_ref, z2_ref, z3_ref)
    rows, width = z0_ref.shape[2:]
    fresh = dots_ref[0]
    for peer in range(1, dots_ref.shape[0]):
        fresh = fresh + dots_ref[peer]
    history_row = lax.broadcasted_iota(jnp.int32, sums_ref.shape, 0)
    sums = jnp.where(history_row == ITERS - 1, fresh, sums_ref[...])
    beta, unscale, columns, lengths = weights_of(sums, ITERS)
    row_at = lax.broadcasted_iota(jnp.int32, (8, 128), 0)
    column_at = lax.broadcasted_iota(jnp.int32, (8, 128), 1)
    table = jnp.zeros((8, 128), F32)
    for j in range(ITERS):
        for i, weight in enumerate(columns[j] + [lengths[j]]):
            table = jnp.where((row_at == j) & (column_at == i), weight, table)
    hessenberg_ref[...] = table[0 : hessenberg_ref.shape[0], 0 : hessenberg_ref.shape[1]]
    goal = [beta]
    triangle = []
    rotations = []
    for j in range(ITERS):
        entries = list(columns[j])
        for i, (cosine, sine) in enumerate(rotations):
            upper, lower = entries[i], entries[i + 1]
            entries[i] = cosine * upper + sine * lower
            entries[i + 1] = cosine * lower - sine * upper
        radius = jnp.sqrt(entries[j] * entries[j] + lengths[j] * lengths[j])
        cosine, sine = entries[j] / radius, lengths[j] / radius
        rotations.append((cosine, sine))
        entries[j] = radius
        triangle.append(entries)
        leading = goal[j]
        goal[j] = cosine * leading
        goal.append(-sine * leading)
    answer = [None] * ITERS
    for i in range(ITERS - 1, -1, -1):
        partial = goal[i]
        for j in range(i + 1, ITERS):
            partial = partial - triangle[j][i] * answer[j]
        answer[i] = partial / triangle[i][i]
    factors = [
        jnp.concatenate([answer[j] * unscale if j == 0 else answer[j]] * (width // 128), axis=1)
        for j in range(ITERS)
    ]
    for c in range(3):
        for k in range(z0_ref.shape[1]):
            value = factors[0] * z_refs[0][c, k]
            for j in range(1, ITERS):
                value = value + factors[j] * z_refs[j][c, k]
            update_ref[c, k] = value


def turn(array, by):
    count = lax.axis_size("layer")
    return lax.ppermute(array, "layer", [(i, (i + by) % count) for i in range(count)])


def shape_of(*dims, kind=F32):
    return jax.ShapeDtypeStruct(dims, kind)


def local(
    right_side,
    diag_blocks,
    couplings,
    pivot_inverse,
    lower_blocks,
    upper_blocks,
    active_cells,
    link_from,
    link_owner,
    link_target,
    link_blocks,
):
    _, layers, rows, width = right_side.shape
    peers = lax.axis_size("areal")
    sections = lax.axis_size("layer")
    links = link_from.shape[1]
    capacity = 2 * links // peers
    slots = capacity * peers // width
    per_peer = slots // peers
    link_rows = links // width
    compact = -(-(links // LANES + peers) // 8) * 8
    packed_rows = compact + -(-capacity // LANES // 8) * 8
    field = shape_of(3, layers, rows, width)
    edge_rows = 7 * rows
    sent_width = (3 * per_peer + 3 * layers) * width + 128
    first_width = (4 * per_peer + 3 * layers) * width
    edge_shape = shape_of(edge_rows, width)
    hbm = pl.BlockSpec(memory_space=pltpu.HBM)
    operands = [
        right_side,
        pivot_inverse,
        lower_blocks,
        upper_blocks,
        active_cells,
        link_from,
        link_owner.reshape(1, links),
        link_target,
        link_blocks.reshape(3, 3, links),
    ]
    (
        edge, following, alone, from_above, from_below, matrices,
        slot_block, slot_source, slot_target, starts, active,
    ) = call(
        functools.partial(setup_kernel, peers),
        [
            edge_shape,
            shape_of(16 * rows, width),
            field,
            shape_of(3, 3, layers, rows, width),
            shape_of(3, 3, layers, rows, width),
            shape_of(27 * rows, width),
            shape_of(3, 3, compact, LANES),
            shape_of(compact, LANES, kind=jnp.int32),
            shape_of(capacity * peers // LANES, LANES),
            shape_of(1, LANES, kind=jnp.int32),
            shape_of(layers, rows, width),
        ],
        [pltpu.VMEM(operand.shape, operand.dtype) for operand in operands]
        + [
            pltpu.VMEM((peers * link_rows, width), BF16),
            pltpu.VMEM((13 * compact, LANES), F32),
            pltpu.VMEM((packed_rows, LANES), F32),
            pltpu.VMEM((3, link_rows, width), jnp.int32),
            pltpu.SemaphoreType.DMA((len(operands),)),
        ],
        name="setup",
        inputs=[hbm] * len(operands),
        limit=16,
    )(*[pltpu.with_memory_space_constraint(operand, pltpu.HBM) for operand in operands])
    turned = [turn(following, 1)] + [turn(edge, by) for by in range(2, sections)]
    all_matrices = lax.all_gather(matrices, "layer", axis=0, tiled=False)

    sums = jnp.zeros((8, 128), F32)
    earlier = []
    zs = []
    for step in range(ITERS):
        last = step == ITERS - 1
        scratch = [
            pltpu.VMEM((sections, 3, rows, width), F32),
            pltpu.VMEM((sections, 3, rows, width), F32),
            pltpu.VMEM((2, 16, width), F32),
            pltpu.VMEM((3, layers * rows, width), F32),
            pltpu.VMEM((3, packed_rows, LANES), F32),
        ]
        edges = [edge]
        scratch.append(pltpu.VMEM((sections, 7 * rows, width), F32))
        if step > 0:
            edges += [turn(edge, by) for by in range(1, sections)]
        solved, layer_sides, sent = call(
            functools.partial(couple_kernel, step == 0, sections),
            [
                field,
                shape_of(2, 3, rows, width),
                shape_of(peers, 1, first_width if step == 0 else sent_width),
            ],
            scratch,
            name="couple",
        )(
            *turned, *edges, all_matrices, alone, from_above, from_below, active,
            slot_block, slot_source, slot_target, starts,
        )
        got = lax.all_to_all(sent, "areal", split_axis=0, concat_axis=0, tiled=True)
        operands = [got, solved, layer_sides, diag_blocks, couplings, active]
        if step > 0:
            operands += [hot_row, hot_column]
        if not last:
            operands += [pivot_inverse, lower_blocks, upper_blocks]
        operands.append(right_side)
        if step > 0:
            operands.append(sums)
            for group in earlier:
                operands += list(group)
        history = shape_of(8, 128)
        if step == 0:
            outs = [
                field,
                edge_shape,
                field,
                shape_of(peers, layers * rows, capacity, kind=BF16),
                shape_of(peers, capacity, width, kind=BF16),
            ]
        elif last:
            outs = [field, shape_of(peers * sections, 1, 128), history]
        else:
            outs = [field, field, field, edge_shape, field, history]
        results = call(
            functools.partial(operate_kernel, step),
            outs,
            ([pltpu.VMEM((slots, width), F32)] if step == 0 else [])
            + [pltpu.VMEM((3 * PARTS * layers * rows, width), F32)],
            name="operate",
        )(*operands)
        if step == 0:
            applied, edge, alone, hot_row, hot_column = results
            earlier.append((solved, applied))
            zs.append(solved)
        elif last:
            z, dots, sums = results
            zs.append(z)
        else:
            v, z, w, edge, alone, sums = results
            earlier.append((v, z, w))
            zs.append(z)
    dots = lax.all_to_all(dots, ("areal", "layer"), split_axis=0, concat_axis=0, tiled=True)
    update, hessenberg = call(
        finish_kernel, [field, shape_of(ITERS, ITERS + 1)], name="finish"
    )(dots, sums, *zs)
    return update, hessenberg.T


def solution(mesh):
    placed = (
        P(None, "layer", "areal", None),
        P(None, None, "layer", "areal", None),
        P(None, None, None, "layer", "areal", None),
        P(None, None, "layer", "areal", None),
        P(None, None, "layer", "areal", None),
        P(None, None, "layer", "areal", None),
        P("layer", "areal", None),
        P("layer", "areal"),
        P("layer", "areal", None),
        P("layer", "areal"),
        P(None, None, "layer", "areal"),
    )
    return jax.shard_map(
        local,
        mesh=mesh,
        in_specs=placed,
        out_specs=(P(None, "layer", "areal", None), P()),
        check_vma=False,
    )
```
